32 devices in a mesh: rep: 8 (over y, x, core), shard: 4 (over z).
Axes of the slice: x: 2, y: 2, z: 4, core: 2. Of those that a mesh axis runs over, the one named last changes fastest.
Arguments:
- tokens: bfloat16 [8192, 2048], P(('rep', 'shard')), may hold values from -6 to 6
- cotangent: bfloat16 [8192, 2048], P(('rep', 'shard')), may hold values from -6 to 6
- lengths: int32 [64], replicated, may hold values from 1 to 256, as said below
- seq_owner: int32 [64], replicated, may hold values from 0 to 31, as said below
- expert_ids: int32 [8192, 6], P(('rep', 'shard')), may hold values from 0 to 63, as said below
- attention_gain: bfloat16 [2048], P('shard'), may hold values from 0.25 to 1.75
- query_weight: bfloat16 [2048, 3072], P('shard'), may hold values from -0.125 to 0.125
- latent_down: bfloat16 [2048, 576], P('shard'), may hold values from -0.125 to 0.125
- latent_gain: bfloat16 [512], P('shard'), may hold values from 0.25 to 1.75
- latent_up: bfloat16 [512, 4096], P('shard'), may hold values from -0.25 to 0.25
- output_weight: bfloat16 [2048, 2048], P('shard'), may hold values from -0.5 to 0.5
- feedforward_gain: bfloat16 [2048], P('shard'), may hold values from 0.25 to 1.75
- router_weight: bfloat16 [2048, 64], P('shard'), may hold values from -0.25 to 0.25
- shared_gate: bfloat16 [2048, 2816], P('shard'), may hold values from -0.125 to 0.125
- shared_up: bfloat16 [2048, 2816], P('shard'), may hold values from -0.125 to 0.125
- shared_down: bfloat16 [2816, 2048], P('shard'), may hold values from -0.109375 to 0.109375
- expert_gate: bfloat16 [2, 2048, 1408], P(None, 'shard'), may hold values from -0.125 to 0.125
- expert_up: bfloat16 [2, 2048, 1408], P(None, 'shard'), may hold values from -0.125 to 0.125
- expert_down: bfloat16 [2, 1408, 2048], P(None, 'shard'), may hold values from -0.15625 to 0.15625
Outputs:
- layer_out: bfloat16 [8192, 2048], P(('rep', 'shard'))
- token_grad: float32 [8192, 2048], P(('rep', 'shard'))
- attention_gain_grad: float32 [2048], P('shard')
- query_weight_grad: float32 [2048, 3072], P('shard')
- latent_down_grad: float32 [2048, 576], P('shard')
- latent_gain_grad: float32 [512], P('shard')
- latent_up_grad: float32 [512, 4096], P('shard')
- output_weight_grad: float32 [2048, 2048], P('shard')
- feedforward_gain_grad: float32 [2048], P('shard')
- router_weight_grad: float32 [2048, 64], P('shard')
- shared_gate_grad: float32 [2048, 2816], P('shard')
- shared_up_grad: float32 [2048, 2816], P('shard')
- shared_down_grad: float32 [2816, 2048], P('shard')
- expert_gate_grad: float32 [2, 2048, 1408], P(None, 'shard')
- expert_up_grad: float32 [2, 2048, 1408], P(None, 'shard')
- expert_down_grad: float32 [2, 1408, 2048], P(None, 'shard')
The draws below stay inside these ranges and needn't reach their ends.
Inputs may be any that keep to these rules, and one draw needn't show every extreme that they name: `lengths`: every sequence has at least one token; the sequences of one device have 256 tokens or fewer in all; some device holds a single sequence of 256 tokens. `seq_owner`: every device holds at least one sequence. `expert_ids`: each row names 6 different experts. Among the 256 rows of one device each expert numbered below 2 is named by at most 32 rows, and in every draw by exactly 32 rows on some device.
All inputs are finite; a program needn't handle non-finite values.
Results may differ from the reference program's by a relative error of at most 0.024.
Values may be sent and summed in bfloat16 or wider, within the bound.
No kernel may reach another device: no remote copies, remote signals or barrier semaphores. Data moves between devices by JAX's collectives and lax.ppermute only.
A program may use at most 448 MiB of HBM per device.

```python
import jax
import jax.numpy as jnp
from jax import lax

D = 2048
HEADS = 16
NOPE = 128
ROPE = 64
VDIM = 128
RANK = 512
NEXP = 64
TOPK = 6
FFE = 1408
SHARED = 2816
WINDOW = 2
TOK_DEV = 256
CAP = 32
TOKENS = 8192
NSEQ = 64


def seq_layout(key):
    devices = NSEQ // 2
    keys = jax.random.split(key, 5)
    fullest = jax.random.randint(keys[0], (), 0, devices)
    others = (fullest + jax.random.randint(keys[1], (NSEQ - devices,), 1, devices)) % devices
    base_owner = jnp.concatenate([jnp.arange(devices, dtype=jnp.int32), others.astype(jnp.int32)])
    owner = base_owner[jax.random.permutation(keys[2], NSEQ)]
    device_order = jnp.arange(devices, dtype=jnp.int32)
    used = jax.random.randint(keys[3], (devices,), TOK_DEV // 2, TOK_DEV + 1)
    used = jnp.where(device_order == fullest, TOK_DEV, used)
    weight = jax.random.randint(keys[4], (NSEQ,), 1, 5)
    member = (owner[:, None] == device_order[None, :]).astype(jnp.int32)
    count = jnp.sum(member, 0)
    weight_total = jnp.sum(member * weight[:, None], 0)
    spare = jnp.maximum(used - count, 0)
    share = 1 + spare[owner] * weight // weight_total[owner]
    placed = jnp.sum(member * share[:, None], 0)
    seq_order = jnp.arange(NSEQ, dtype=jnp.int32)
    earlier = (owner[:, None] == owner[None, :]) & (seq_order[None, :] < seq_order[:, None])
    first_one = jnp.logical_not(jnp.any(earlier, 1))
    lengths = share + jnp.where(first_one, used[owner] - placed[owner], 0)
    return (lengths.astype(jnp.int32), owner.astype(jnp.int32))


def draw_lengths(key, part):
    return seq_layout(jax.random.fold_in(key, 7))[0]


def draw_seq_owner(key, part):
    return seq_layout(jax.random.fold_in(key, 7))[1]


def draw_expert_ids(key, part):
    blocks = TOKENS // TOK_DEV
    keys = jax.random.split(key, 6)
    counts = jax.random.randint(keys[0], (blocks, WINDOW), CAP // 2, CAP + 1)
    full_block = jax.random.randint(keys[1], (), 0, blocks)
    full_expert = jax.random.randint(keys[2], (), 0, WINDOW)
    counts = jnp.where((jnp.arange(blocks)[:, None] == full_block) & (jnp.arange(WINDOW)[None, :] == full_expert), CAP, counts)
    ranks = jax.vmap(lambda each_key: jax.random.permutation(each_key, TOK_DEV))(jax.random.split(keys[3], blocks * WINDOW))
    ranks = ranks.reshape(blocks, WINDOW, TOK_DEV)
    chosen = jnp.transpose(ranks < counts[:, :, None], (0, 2, 1)).reshape(TOKENS, WINDOW)
    order = jax.vmap(lambda each_key: jax.random.permutation(each_key, NEXP))(jax.random.split(keys[4], TOKENS))
    chosen_full = jnp.concatenate([chosen, jnp.zeros((TOKENS, NEXP - WINDOW), dtype=bool)], 1)
    window_flag = jnp.arange(NEXP)[None, :] < WINDOW
    score = order + jnp.where(window_flag, jnp.where(chosen_full, 4 * NEXP, -4 * NEXP), 0)
    picked = lax.top_k(score, TOPK)[1]
    shuffle = jax.vmap(lambda each_key: jax.random.permutation(each_key, TOPK))(jax.random.split(keys[5], TOKENS))
    return jnp.take_along_axis(picked, shuffle, 1).astype(jnp.int32)


def block_scale(stream_key, extent, cuts, smallest, largest):
    def one(dim, shards_of):
        heights = jax.random.uniform(jax.random.fold_in(jax.random.fold_in(stream_key, 6), dim), (shards_of,), jnp.float32, smallest / len(cuts), largest / len(cuts))
        return jnp.repeat(jnp.exp(heights), extent[dim] // shards_of).reshape((-1,) + (1,) * (len(extent) - dim - 1))

    level = one(*cuts[0])
    for cut in cuts[1:]:
        level = level * one(*cut)
    return level


def normal_values(key, dims, scale, reach, shards=(), kind=jnp.bfloat16):
    level = block_scale(key, dims, shards, -0.22, 0.18) if shards else 1.0
    entries = jax.random.normal(key, dims, jnp.float32) * scale * level
    return jnp.minimum(jnp.maximum(entries, -reach), reach).astype(kind)


def setup_inputs(seed: int = 0) -> dict:
    splits = jax.random.split(jax.random.key(seed), 20)
    tokens = normal_values(splits[0], (TOKENS, D), 1.0, 6.0, ((0, 32),))
    cotangent = normal_values(splits[1], (TOKENS, D), 1.0, 6.0, ((0, 32),))
    lengths = draw_lengths(jax.random.fold_in(splits[19], 71), 0)
    seq_owner = draw_seq_owner(jax.random.fold_in(splits[19], 71), 0)
    expert_ids = draw_expert_ids(jax.random.fold_in(splits[19], 71), 0)
    attention_gain = jnp.clip(1.0 + 0.15 * jax.random.normal(splits[5], (D,), jnp.float32), 0.25, 1.75).astype(jnp.bfloat16)
    query_weight = normal_values(splits[6], (D, HEADS * (NOPE + ROPE)), D ** -0.5, 0.125, ((0, 4),))
    latent_down = normal_values(splits[7], (D, RANK + ROPE), D ** -0.5, 0.125, ((0, 4),))
    latent_gain = jnp.clip(1.0 + 0.15 * jax.random.normal(splits[8], (RANK,), jnp.float32), 0.25, 1.75).astype(jnp.bfloat16)
    latent_up = normal_values(splits[9], (RANK, HEADS * (NOPE + VDIM)), RANK ** -0.5, 0.25, ((0, 4),))
    output_weight = normal_values(splits[10], (HEADS * VDIM, D), 128 ** -0.5, 0.5, ((0, 4),))
    feedforward_gain = jnp.clip(1.0 + 0.15 * jax.random.normal(splits[11], (D,), jnp.float32), 0.25, 1.75).astype(jnp.bfloat16)
    router_weight = normal_values(splits[12], (D, NEXP), (D // 4) ** -0.5, 0.25, ((0, 4),))
    shared_gate = normal_values(splits[13], (D, SHARED), D ** -0.5, 0.125, ((0, 4),))
    shared_up = normal_values(splits[14], (D, SHARED), D ** -0.5, 0.125, ((0, 4),))
    shared_down = normal_values(splits[15], (SHARED, D), SHARED ** -0.5, 0.109375, ((0, 4),))
    expert_gate = normal_values(splits[16], (WINDOW, D, FFE), D ** -0.5, 0.125, ((1, 4),))
    expert_up = normal_values(splits[17], (WINDOW, D, FFE), D ** -0.5, 0.125, ((1, 4),))
    expert_down = normal_values(splits[18], (WINDOW, FFE, D), FFE ** -0.5, 0.15625, ((1, 4),))
    return {"tokens": tokens, "cotangent": cotangent, "lengths": lengths, "seq_owner": seq_owner, "expert_ids": expert_ids, "attention_gain": attention_gain, "query_weight": query_weight, "latent_down": latent_down, "latent_gain": latent_gain, "latent_up": latent_up, "output_weight": output_weight, "feedforward_gain": feedforward_gain, "router_weight": router_weight, "shared_gate": shared_gate, "shared_up": shared_up, "shared_down": shared_down, "expert_gate": expert_gate, "expert_up": expert_up, "expert_down": expert_down}


EPSILON = 1e-06
ROPE_BASE = 50000.0
ROUTE_SCALE = 2.446
NEG_FILL = -1e+30
EXACT = lax.Precision.HIGHEST

@jax.custom_vjp
def low(v):
    return lax.optimization_barrier(v.astype(jnp.bfloat16)).astype(jnp.float32)

@jax.custom_vjp
def latent_backward_rows(v):
    return v

def low_keep(v):
    return (low(v), None)

def low_pass(kept, grad):
    return (grad,)

def back_keep(v):
    return (v, None)

def back_low(kept, grad):
    return (low(grad),)
low.defvjp(low_keep, low_pass)
latent_backward_rows.defvjp(back_keep, back_low)

def matrix_multiply(left, right):
    return jnp.dot(left, right, precision=EXACT, preferred_element_type=jnp.float32)

def rms_norm(values, gain):
    return values * lax.rsqrt(lax.optimization_barrier(jnp.mean(values * values, -1, keepdims=True)) + EPSILON) * gain

def rotate(values, cosine, sine_table):
    half_width = values.shape[-1] // 2
    first_half = values[..., :half_width]
    second_half = values[..., half_width:]
    return jnp.concatenate([first_half * cosine - second_half * sine_table, second_half * cosine + first_half * sine_table], -1)

def token_layout(lengths, seq_owner, device, row_count):
    seq_count = lengths.shape[0]
    mine = seq_owner == device
    own_length = jnp.where(mine, lengths, 0).astype(jnp.int32)
    starts = (jnp.cumsum(own_length) - own_length).astype(jnp.int32)
    row_order = jnp.arange(row_count, dtype=jnp.int32)
    inside = mine[None, :] & (row_order[:, None] >= starts[None, :]) & (row_order[:, None] < (starts + own_length)[None, :])
    valid_rows = jnp.any(inside, 1)
    numbers = jnp.arange(seq_count, dtype=jnp.int32)
    segment = jnp.where(valid_rows, lax.optimization_barrier(jnp.sum(jnp.where(inside, numbers[None, :], 0), 1)), seq_count).astype(jnp.int32)
    position = (row_order - lax.optimization_barrier(jnp.sum(jnp.where(inside, starts[None, :], 0), 1))).astype(jnp.int32)
    return (segment, position, valid_rows)

def attend_block(pieces):
    query_nope, query_rope, key_nope, key_rope, values, segment = pieces
    row_order = jnp.arange(segment.shape[0], dtype=jnp.int32)
    allowed = (segment[:, None] == segment[None, :]) & (row_order[None, :] <= row_order[:, None])
    raw_scores = jnp.einsum('thd,shd->hts', query_nope, key_nope, precision=EXACT)
    raw_scores = raw_scores + jnp.einsum('thd,sd->hts', query_rope, key_rope, precision=EXACT)
    scores = latent_backward_rows(jnp.where(allowed[None], raw_scores * (NOPE + ROPE) ** (-0.5), NEG_FILL))
    probs = low(jax.nn.softmax(scores, -1))
    return jnp.einsum('hts,shd->thd', probs, values, precision=EXACT)

def reference(tokens, cotangent, lengths, seq_owner, expert_ids, attention_gain, query_weight, latent_down, latent_gain, latent_up, output_weight, feedforward_gain, router_weight, shared_gate, shared_up, shared_down, expert_gate, expert_up, expert_down):
    devices = TOKENS // TOK_DEV
    segment, position, valid_rows = jax.vmap(lambda device: token_layout(lengths, seq_owner, device, TOK_DEV))(jnp.arange(devices, dtype=jnp.int32))
    valid_col = valid_rows.reshape(TOKENS, 1).astype(jnp.float32)
    frequency = jnp.power(ROPE_BASE, -2.0 * jnp.arange(ROPE // 2, dtype=jnp.float32) / ROPE)
    angle_table = position.reshape(TOKENS).astype(jnp.float32)[:, None] * frequency[None, :]
    cosine = jnp.cos(angle_table)
    sine_table = jnp.sin(angle_table)
    onehot = (expert_ids[:, :, None] == jnp.arange(NEXP, dtype=jnp.int32)[None, None, :]).astype(jnp.float32)
    weights_in = (attention_gain, query_weight, latent_down, latent_gain, latent_up, output_weight, feedforward_gain, router_weight, shared_gate, shared_up, shared_down, expert_gate, expert_up, expert_down)
    parameter_tree = tuple((weight.astype(jnp.float32) for weight in weights_in))

    def forward(hidden_in, parameter_tree):
        attention_gain_vector, query_projection, down_projection_fn, latent_gain_vector, up_projection_fn, output_projection, mixer_gain_vector, router_projection, shared_gate_projection, shared_up_projection, shared_down_projection, expert_gate_projection, expert_up_projection, expert_down_projection = parameter_tree
        normed = low(rms_norm(hidden_in, attention_gain_vector))
        query_heads = latent_backward_rows(matrix_multiply(normed, query_projection)).reshape(TOKENS, HEADS, NOPE + ROPE)
        query_nope = low(query_heads[:, :, :NOPE])
        query_rope = low(rotate(query_heads[:, :, NOPE:], cosine[:, None, :], sine_table[:, None, :]))
        latent = latent_backward_rows(matrix_multiply(normed, down_projection_fn))
        key_rope = low(rotate(latent[:, RANK:], cosine, sine_table))
        latent_normed = low(rms_norm(latent[:, :RANK], latent_gain_vector))
        keyval = low(latent_backward_rows(matrix_multiply(latent_normed, up_projection_fn))).reshape(TOKENS, HEADS, NOPE + VDIM)
        pieces = (query_nope.reshape(devices, TOK_DEV, HEADS, NOPE), query_rope.reshape(devices, TOK_DEV, HEADS, ROPE), keyval[:, :, :NOPE].reshape(devices, TOK_DEV, HEADS, NOPE), key_rope.reshape(devices, TOK_DEV, ROPE), keyval[:, :, NOPE:].reshape(devices, TOK_DEV, HEADS, VDIM), segment)
        attended = lax.map(jax.checkpoint(attend_block), pieces).reshape(TOKENS, HEADS * VDIM)
        attended = low(latent_backward_rows(attended))
        mid_stream = hidden_in + latent_backward_rows(matrix_multiply(attended, output_projection))
        mixed_rms_norm = low(rms_norm(mid_stream, mixer_gain_vector))
        sigmoid_all = jax.nn.sigmoid(latent_backward_rows(matrix_multiply(mixed_rms_norm, router_projection)))
        picked = lax.optimization_barrier(jnp.sum(sigmoid_all[:, None, :] * onehot, -1))
        route_weight = ROUTE_SCALE * picked / lax.optimization_barrier(jnp.sum(picked, -1, keepdims=True))
        shared_pre = latent_backward_rows(matrix_multiply(mixed_rms_norm, shared_gate_projection))
        shared_upv = latent_backward_rows(matrix_multiply(mixed_rms_norm, shared_up_projection))
        shared_hidden = low(jax.nn.silu(shared_pre) * shared_upv)
        combined = mid_stream + matrix_multiply(shared_hidden, shared_down_projection)
        for expert_slot_index in range(WINDOW):
            hit_table = (expert_ids == expert_slot_index).astype(jnp.float32)
            expert_weight = lax.optimization_barrier(jnp.sum(route_weight * hit_table, -1)) * valid_col[:, 0]
            expert_pre = latent_backward_rows(matrix_multiply(mixed_rms_norm, expert_gate_projection[expert_slot_index]))
            expert_up_value = latent_backward_rows(matrix_multiply(mixed_rms_norm, expert_up_projection[expert_slot_index]))
            expert_hidden = low(jax.nn.silu(expert_pre) * expert_up_value)
            expert_out = latent_backward_rows(matrix_multiply(expert_hidden, expert_down_projection[expert_slot_index]))
            combined = combined + expert_weight[:, None] * expert_out
        return valid_col * combined
    final, backward = jax.vjp(forward, tokens.astype(jnp.float32), parameter_tree)
    token_grad, grads = backward(cotangent.astype(jnp.float32))
    return (final.astype(jnp.bfloat16), token_grad, grads[0], grads[1], grads[2], grads[3], grads[4], grads[5], grads[6], grads[7], grads[8], grads[9], grads[10], grads[11], grads[12], grads[13])
```

```python
import functools

import jax
import jax.numpy as jnp
from jax import lax
from jax.experimental import pallas as pl
from jax.experimental.pallas import tpu as pltpu
from jax.sharding import PartitionSpec as P

HEADS = 16
NOPE = 128
ROPE = 64
VDIM = 128
RANK = 512
NEXP = 64
WINDOW = 2

EPSILON = 1e-06
ROPE_BASE = 50000.0
ROUTE_SCALE = 2.446
NEG_FILL = -1e30
SCORE_SCALE = (NOPE + ROPE) ** (-0.5)

F32 = jnp.float32
LOW = jnp.bfloat16


def dot(left, right):
    return jnp.dot(left, right, preferred_element_type=F32)


def dot_rows(left, right):
    return lax.dot_general(left, right, (((0,), (0,)), ((), ())), preferred_element_type=F32)


def dot_last(left, right):
    return lax.dot_general(left, right, (((1,), (1,)), ((), ())), preferred_element_type=F32)


def rms_scale(values):
    return lax.rsqrt(jnp.mean(values * values, -1, keepdims=True) + EPSILON)


def rms_back(values, scale, gain, upstream):
    gained = upstream * gain
    inner = jnp.mean(values * gained, -1, keepdims=True)
    return scale * gained - values * scale * scale * scale * inner


def round_up(value, unit):
    return -(-value // unit) * unit


class Group:
    def __init__(self, reps, shards):
        self.reps = reps
        self.shards = shards
        bits = reps.bit_length() - 1
        assert bits >= 1 and 1 << bits == reps
        self.levels = [(1 << b, 1 << (bits - b)) for b in range(1, bits)]
        self.half = reps // 2

    def devices(self, rep):
        lists = []
        for side in (0, 1):
            masks = [0]
            for level in self.levels:
                masks = masks + [m ^ level[side] for m in masks]
            lists.append(masks)
        first = lists[0] + [m ^ 1 for m in lists[1]]
        second = lists[1] + [m ^ 1 for m in lists[0]]
        masks = jnp.where(
            rep % 2 == 0, jnp.array(first, jnp.int32), jnp.array(second, jnp.int32)
        )
        return rep.astype(jnp.int32) ^ masks

    def cross(self, value, level):
        pairs = [(i, i ^ level[i & 1]) for i in range(self.reps)]
        return lax.ppermute(value, "rep", pairs)

    def gather(self, block):
        blocks = [block]
        for level in self.levels:
            blocks = blocks + [self.cross(b, level) for b in blocks]
        return blocks + [self.cross(b, (1, 1)) for b in blocks]

    def reduce(self, second, first, axis=0):
        terms = [first, self.cross(second, (1, 1))]

        def cut(start, size):
            total = None
            for term in terms:
                term = lax.slice_in_dim(term, start, start + size, axis=axis).astype(F32)
                total = term if total is None else total + term
            return total

        size = first.shape[axis]
        for level in reversed(self.levels):
            size //= 2
            terms.append(self.cross(cut(size, size).astype(LOW), level))
        return cut(0, size)

    def along(self, block):
        count = self.shards
        up = [block]
        down = [block]
        for _ in range(count - 1):
            up.append(lax.ppermute(up[-1], "shard", [(i, i + 1) for i in range(count - 1)]))
            down.append(lax.ppermute(down[-1], "shard", [(i + 1, i) for i in range(count - 1)]))
        return up, down

    def reduce_shard(self, blocks, position):
        count = self.shards

        def own(index):
            return lax.dynamic_index_in_dim(
                blocks, jnp.clip(index, 0, count - 1), 0, keepdims=False
            ).astype(F32)

        came = [None, None]
        for step in range(1, count):
            for side, sign in ((0, 1), (1, -1)):
                value = own(position + sign * (count - step))
                if came[side] is not None:
                    value = value + came[side].astype(F32)
                if sign == 1:
                    pairs = [(i, i + 1) for i in range(step)]
                else:
                    pairs = [(i, i - 1) for i in range(count - step, count)]
                came[side] = lax.ppermute(value.astype(LOW), "shard", pairs)
        total = own(position)
        for side in came:
            if side is not None:
                total = total + side.astype(F32)
        return total


def head_probs(h, allowed, q_nope, q_rope, keyval, k_rope):
    width = q_rope.shape[1]
    base = h * (NOPE + VDIM)
    scores = dot_last(q_nope[:, h * NOPE : (h + 1) * NOPE], keyval[:, base : base + NOPE])
    scores = scores + dot_last(q_rope, k_rope[:, h * width : (h + 1) * width])
    scores = jnp.where(allowed, scores * SCORE_SCALE, NEG_FILL)
    unnormed = jnp.exp(scores - jnp.max(scores, -1, keepdims=True))
    return unnormed / jnp.sum(unnormed, -1, keepdims=True)


def same_segment(sc_ref, sr_ref):
    rows = sc_ref.shape[0]
    t = lax.broadcasted_iota(jnp.int32, (rows, rows), 0)
    u = lax.broadcasted_iota(jnp.int32, (rows, rows), 1)
    return (sc_ref[...] == sr_ref[0]) & (u <= t)


def turned(values):
    half = values.shape[1] // 2
    return jnp.concatenate([values[:, half:], values[:, :half]], 1)


def whole(a):
    return pl.BlockSpec(a.shape, lambda b, dev_ref: (0,) * a.ndim, pipeline_mode=pl.Buffered(1))


def attend_forward(
    devices, blocks, gain, latent_gain, query_w, small_w, up_w, spread, cosine, sine, seg_col, seg_row
):
    count = len(blocks)
    rows, model = blocks[0].shape
    heads = up_w.shape[1] // (NOPE + VDIM)
    half = 32 * heads
    width = 2 * half

    def kernel(dev_ref, *refs):
        parts = refs[:count]
        gain_ref, lgain_ref, qw_ref, sw_ref, uw_ref, spread_ref, cos_ref, sin_ref, sc_ref, sr_ref = (
            refs[count : count + 10]
        )
        normed_ref, qn_ref, qr_ref, kv_ref, kr_ref, low_ref, own_ref, out_ref, held = refs[
            count + 10 :
        ]
        step = pl.program_id(0)
        for k in range(count):

            @pl.when(step == k)
            def _():
                held[...] = parts[k][...]

        x = held[...].astype(F32)
        normed = (x * rms_scale(x) * gain_ref[...]).astype(LOW)
        normed_ref[...] = normed
        query = dot(normed, qw_ref[...])
        q_nope = query[:, : heads * NOPE].astype(LOW)
        q_rope = query[:, heads * NOPE :]
        cos = cos_ref[...]
        sin = sin_ref[...]
        q_rope = (q_rope * cos + turned(q_rope) * sin).astype(LOW)
        latent = dot(normed, sw_ref[...])

        @pl.when(step == 0)
        def _():
            own_ref[...] = latent

        compressed = latent[:, :RANK]
        low = (compressed * rms_scale(compressed) * lgain_ref[...]).astype(LOW)
        key = latent[:, RANK : RANK + ROPE]
        key = key * cos[:, :ROPE] + turned(key) * sin[:, half - 32 : half + 32]
        k_rope = dot(key.astype(LOW), spread_ref[...]).astype(LOW)
        keyval = dot(low, uw_ref[...]).astype(LOW)
        qn_ref[...] = q_nope
        qr_ref[...] = q_rope
        kv_ref[...] = keyval
        kr_ref[...] = k_rope
        low_ref[...] = low
        allowed = same_segment(sc_ref, sr_ref)
        for h in range(heads):
            probs = head_probs(h, allowed, q_nope, q_rope, keyval, k_rope)
            base = h * (NOPE + VDIM) + NOPE
            out_ref[:, h * VDIM : (h + 1) * VDIM] = dot(
                probs.astype(LOW), keyval[:, base : base + VDIM]
            ).astype(LOW)

    def tok(cols):
        return pl.BlockSpec((rows, cols), lambda b, dev_ref: (b, 0))

    total = count * rows
    widths = [model, heads * NOPE, width, heads * (NOPE + VDIM), heads * width, RANK]
    return pl.pallas_call(
        kernel,
        grid_spec=pltpu.PrefetchScalarGridSpec(
            num_scalar_prefetch=1,
            grid=(count,),
            in_specs=[whole(a) for a in blocks]
            + [whole(a) for a in (gain, latent_gain, query_w, small_w, up_w, spread)]
            + [tok(width), tok(width), tok(1)]
            + [pl.BlockSpec((1, 1, rows), lambda b, dev_ref: (b, 0, 0))],
            out_specs=[tok(w) for w in widths]
            + [pl.BlockSpec((rows, small_w.shape[1]), lambda b, dev_ref: (0, 0))]
            + [pl.BlockSpec((rows, heads * VDIM), lambda b, dev_ref: (dev_ref[b], 0))],
            scratch_shapes=[pltpu.VMEM((rows, model), LOW)],
        ),
        out_shape=[jax.ShapeDtypeStruct((total, w), LOW) for w in widths]
        + [jax.ShapeDtypeStruct((rows, small_w.shape[1]), F32)]
        + [jax.ShapeDtypeStruct((total, heads * VDIM), LOW)],
        cost_estimate=pl.CostEstimate(
            flops=2 * total * model * (query_w.shape[1] + small_w.shape[1] + 512),
            bytes_accessed=total * model * 6,
            transcendentals=total * rows * heads,
        ),
    )(devices, *blocks, gain, latent_gain, query_w, small_w, up_w, spread, cosine, sine, seg_col, seg_row)


def attend_backward(
    devices, kept, given, normed, low, query_w, up_w, cosine, sine, seg_col, seg_row, rows
):
    q_nope, q_rope, keyval, k_rope = kept
    total, model = normed.shape
    count = total // rows
    heads = up_w.shape[1] // (NOPE + VDIM)
    half = 32 * heads
    width = 2 * half
    nope = heads * NOPE
    middle = count // 2

    def kernel(
        dev_ref,
        qn_ref,
        qr_ref,
        kv_ref,
        kr_ref,
        da_ref,
        n_ref,
        low_ref,
        qw_ref,
        uw_ref,
        cos_ref,
        sin_ref,
        sc_ref,
        sr_ref,
        first_ref,
        second_ref,
        lat_first_ref,
        lat_second_ref,
        qg_ref,
        ug_ref,
        q_sum,
        u_sum,
    ):
        step = pl.program_id(0)
        allowed = same_segment(sc_ref, sr_ref)
        qn = qn_ref[...]
        qr = qr_ref[...]
        kv = kv_ref[...]
        kr = kr_ref[...]
        d_rope = None
        d_key = None
        d_nope = []
        d_keyval = []
        for h in range(heads):
            probs = head_probs(h, allowed, qn, qr, kv, kr)
            base = h * (NOPE + VDIM)
            keys = kv[:, base : base + NOPE]
            values = kv[:, base + NOPE : base + NOPE + VDIM]
            d_att = da_ref[:, h * VDIM : (h + 1) * VDIM]
            d_values = dot_rows(probs.astype(LOW), d_att)
            d_probs = dot_last(d_att, values)
            inner = jnp.sum(probs * d_probs, -1, keepdims=True)
            d_scores = (probs * (d_probs - inner)).astype(LOW)
            d_nope.append((dot(d_scores, keys) * SCORE_SCALE).astype(LOW))
            rope = dot(d_scores, kr[:, h * width : (h + 1) * width])
            d_rope = rope if d_rope is None else d_rope + rope
            d_keys = dot_rows(d_scores, qn[:, h * NOPE : (h + 1) * NOPE]) * SCORE_SCALE
            d_keyval += [d_keys.astype(LOW), d_values.astype(LOW)]
            turn = dot_rows(d_scores, qr)
            turn = jnp.concatenate(
                [turn[:, 32 * h : 32 * h + 32], turn[:, half + 32 * h : half + 32 * h + 32]], 1
            )
            d_key = turn if d_key is None else d_key + turn
        d_rope = d_rope * SCORE_SCALE
        d_rope = (d_rope * cos_ref[...] - turned(d_rope) * sin_ref[...]).astype(LOW)
        d_query = jnp.concatenate(d_nope + [d_rope], 1)
        d_keyval = jnp.concatenate(d_keyval, 1)
        d_key = (d_key * SCORE_SCALE).astype(LOW)
        d_normed = dot_last(d_query, qw_ref[...]).astype(LOW)
        d_low = dot_last(d_keyval, uw_ref[...]).astype(LOW)

        @pl.when(step < middle)
        def _():
            first_ref[...] = d_normed
            lat_first_ref[:, :RANK] = d_low
            lat_first_ref[:, RANK:] = d_key

        @pl.when(step >= middle)
        def _():
            second_ref[...] = d_normed
            lat_second_ref[:, :RANK] = d_low
            lat_second_ref[:, RANK:] = d_key

        q_add = dot_rows(n_ref[...], d_query)
        u_add = dot_rows(low_ref[...], d_keyval)

        @pl.when(step == 0)
        def _():
            q_sum[...] = q_add
            u_sum[...] = u_add

        @pl.when(step > 0)
        def _():
            q_sum[...] += q_add
            u_sum[...] += u_add

        @pl.when(step == count - 1)
        def _():
            qg_ref[...] = q_sum[...].astype(LOW)
            ug_ref[...] = u_sum[...].astype(LOW)

    def tok(a):
        return pl.BlockSpec((rows, a.shape[1]), lambda b, dev_ref: (b, 0))

    def low_half(cols):
        return pl.BlockSpec((rows, cols), lambda b, dev_ref: (jnp.minimum(b, middle - 1), 0))

    def high_half(cols):
        return pl.BlockSpec((rows, cols), lambda b, dev_ref: (jnp.maximum(b - middle, 0), 0))

    arrays = [q_nope, q_rope, keyval, k_rope]
    wide = RANK + ROPE
    return pl.pallas_call(
        kernel,
        grid_spec=pltpu.PrefetchScalarGridSpec(
            num_scalar_prefetch=1,
            grid=(count,),
            in_specs=[tok(a) for a in arrays]
            + [pl.BlockSpec((rows, given.shape[1]), lambda b, dev_ref: (dev_ref[b], 0))]
            + [tok(normed), tok(low), whole(query_w), whole(up_w), tok(cosine), tok(sine)]
            + [tok(seg_col), pl.BlockSpec((1, 1, rows), lambda b, dev_ref: (b, 0, 0))],
            out_specs=[low_half(model), high_half(model), low_half(wide), high_half(wide)]
            + [
                pl.BlockSpec(query_w.shape, lambda b, dev_ref: (0, 0)),
                pl.BlockSpec(up_w.shape, lambda b, dev_ref: (0, 0)),
            ],
            scratch_shapes=[pltpu.VMEM(query_w.shape, F32), pltpu.VMEM(up_w.shape, F32)],
        ),
        out_shape=[
            jax.ShapeDtypeStruct((total // 2, model), LOW),
            jax.ShapeDtypeStruct((total // 2, model), LOW),
            jax.ShapeDtypeStruct((total // 2, wide), LOW),
            jax.ShapeDtypeStruct((total // 2, wide), LOW),
            jax.ShapeDtypeStruct(query_w.shape, LOW),
            jax.ShapeDtypeStruct(up_w.shape, LOW),
        ],
        cost_estimate=pl.CostEstimate(
            flops=4 * total * model * query_w.shape[1] + 12 * total * rows * 192 * heads,
            bytes_accessed=total * model * 6,
            transcendentals=total * rows * heads,
        ),
    )(devices, *arrays, given, normed, low, query_w, up_w, cosine, sine, seg_col, seg_row)


def experts(info, blocks, grad, counts, valid, small_w, gate_w, raise_w, lower_w, is_expert):
    count = len(blocks)
    rows, model = blocks[0].shape
    hidden = gate_w.shape[1]
    total = count * rows
    middle = count // 2
    lanes = counts.shape[1]
    router_at = small_w.shape[1] - lanes

    def kernel(info_ref, *refs):
        parts = refs[:count]
        grad_ref, counts_ref, valid_ref, sw_ref, gw_ref, rw_ref, lw_ref, ex_ref = refs[
            count : count + 8
        ]
        (
            mixed_ref,
            hid_ref,
            dg_ref,
            dl_ref,
            dm_first,
            dm_second,
            out_first,
            out_second,
            dw_ref,
            sig_ref,
            held,
        ) = refs[count + 8 :]
        step = pl.program_id(0)
        for k in range(count):

            @pl.when(step == k)
            def _():
                held[...] = parts[k][...]

        mixed = held[...]
        mixed_ref[...] = mixed
        sig = jax.nn.sigmoid(dot(mixed, sw_ref[:, router_at:]))
        sig_count = sig * counts_ref[...].astype(F32)
        lane = lax.broadcasted_iota(jnp.int32, (rows, lanes), 1)
        picked = jnp.sum(jnp.where(lane == lanes - NEXP + info_ref[0], sig_count, 0.0), 1, keepdims=True)
        picked_total = jnp.sum(sig_count, 1, keepdims=True)
        weight = ROUTE_SCALE * picked / picked_total * valid_ref[...]

        @pl.when(step == 0)
        def _():
            sig_ref[...] = sig

        routed = ex_ref[...] > 0.0
        gate = dot(mixed, gw_ref[...])
        lift = dot(mixed, rw_ref[...])
        d_hidden = dot_last(grad_ref[...], lw_ref[...])
        gate_sig = jax.nn.sigmoid(gate)
        gated = gate * gate_sig
        act = gated * lift
        wide = jnp.where(routed, weight, 1.0)
        hid = (act * wide).astype(LOW)
        hid_ref[...] = hid
        dw_ref[...] = jnp.sum(jnp.where(routed, act * d_hidden, 0.0), 1, keepdims=True)
        d_hidden = d_hidden * wide
        d_gate = (d_hidden * lift * gate_sig * (1.0 + gate * (1.0 - gate_sig))).astype(LOW)
        d_lift = (d_hidden * gated).astype(LOW)
        dg_ref[...] = d_gate
        dl_ref[...] = d_lift
        d_mixed = (dot_last(d_gate, gw_ref[...]) + dot_last(d_lift, rw_ref[...])).astype(LOW)
        out = dot(hid, lw_ref[...]).astype(LOW)

        @pl.when(step < middle)
        def _():
            dm_first[...] = d_mixed
            out_first[...] = out

        @pl.when(step >= middle)
        def _():
            dm_second[...] = d_mixed
            out_second[...] = out

    def tok(cols):
        return pl.BlockSpec((rows, cols), lambda b, info_ref: (b, 0))

    low_half = pl.BlockSpec((rows, model), lambda b, info_ref: (jnp.minimum(b, middle - 1), 0))
    high_half = pl.BlockSpec((rows, model), lambda b, info_ref: (jnp.maximum(b - middle, 0), 0))
    part = jax.ShapeDtypeStruct((total // 2, model), LOW)
    return pl.pallas_call(
        kernel,
        grid_spec=pltpu.PrefetchScalarGridSpec(
            num_scalar_prefetch=1,
            grid=(count,),
            in_specs=[whole(a) for a in blocks]
            + [tok(model), tok(lanes), tok(1)]
            + [whole(a) for a in (small_w, gate_w, raise_w, lower_w, is_expert)],
            out_specs=[tok(model), tok(hidden), tok(hidden), tok(hidden)]
            + [low_half, high_half, low_half, high_half, tok(1)]
            + [pl.BlockSpec((rows, lanes), lambda b, info_ref: (0, 0))],
            scratch_shapes=[pltpu.VMEM((rows, model), LOW)],
        ),
        out_shape=[jax.ShapeDtypeStruct((total, model), LOW)]
        + [jax.ShapeDtypeStruct((total, hidden), LOW)] * 3
        + [part] * 4
        + [jax.ShapeDtypeStruct((total, 1), F32), jax.ShapeDtypeStruct((rows, lanes), F32)],
        cost_estimate=pl.CostEstimate(
            flops=12 * total * model * hidden,
            bytes_accessed=total * model * 12,
            transcendentals=total * hidden,
        ),
    )(info, *blocks, grad, counts, valid, small_w, gate_w, raise_w, lower_w, is_expert)


def cost(size, flops=0):
    return pl.CostEstimate(flops=flops, bytes_accessed=size, transcendentals=0)


def shard_merge(group, block, shard, splits):
    up, down = group.along(block)
    return [shard_place(up, down, shard, start, size) for start, size in splits]


def shard_place(up, down, shard, start, size):
    count = len(up)
    width = up[0].shape[1]
    tile = size
    while tile > 128 and tile % 2 == 0 and start % (tile // 2) == 0:
        tile //= 2

    def kernel(at_ref, *refs):
        ups = refs[:count]
        downs = refs[count - 1 : 2 * count - 1]
        out = refs[-1]
        here = at_ref[0]
        out[here] = ups[0][...]
        for step in range(1, count):

            @pl.when(here + step < count)
            def _():
                out[here + step] = downs[step][...]

            @pl.when(here >= step)
            def _():
                out[here - step] = ups[step][...]

    return pl.pallas_call(
        kernel,
        grid_spec=pltpu.PrefetchScalarGridSpec(
            num_scalar_prefetch=1,
            grid=(size // tile,),
            in_specs=[pl.BlockSpec((tile, width), lambda b, at_ref: (b + start // tile, 0))]
            * (2 * count - 1),
            out_specs=pl.BlockSpec((count, tile, width), lambda b, at_ref: (0, b, 0)),
        ),
        out_shape=jax.ShapeDtypeStruct((count, size, width), LOW),
        cost_estimate=cost(4 * count * size * width),
    )(jnp.reshape(shard, (1,)).astype(jnp.int32), *up, *down[1:])


def merge_rows(blocks, act, extra, width):
    rows = blocks[0].shape[0]
    count = len(blocks)

    def kernel(*refs):
        index = pl.program_id(0)
        more = [r[...] for r in refs[count:-1]]
        for k in range(count):

            @pl.when(index == k)
            def _():
                refs[-1][...] = act(refs[k][...], *more)

    def spec(a):
        if a.shape[0] == 1:
            return pl.BlockSpec(a.shape, lambda b: (0, 0))
        return pl.BlockSpec((rows, a.shape[1]), lambda b: (b, 0))

    return pl.pallas_call(
        kernel,
        grid=(count,),
        in_specs=[pl.BlockSpec(a.shape, lambda b: (0, 0)) for a in blocks]
        + [spec(a) for a in extra],
        out_specs=pl.BlockSpec((rows, width), lambda b: (b, 0)),
        out_shape=jax.ShapeDtypeStruct((count * rows, width), LOW),
        cost_estimate=cost(count * rows * width * 4),
    )(*blocks, *extra)


def assemble(blocks, devices, grid, block_shape, block_map, outs, place):
    reps = len(blocks)

    def kernel(dev_ref, *refs):
        held = refs[-1]
        for k in range(reps):
            held[dev_ref[k]] = refs[k][...].astype(F32)
        for j in range(reps):
            place(pl.program_id(0), j, held[j], refs[reps:-1])

    return pl.pallas_call(
        kernel,
        grid_spec=pltpu.PrefetchScalarGridSpec(
            num_scalar_prefetch=1,
            grid=(grid,),
            in_specs=[pl.BlockSpec(block_shape, lambda b, dev_ref: block_map(b)) for _ in blocks],
            out_specs=[
                pl.BlockSpec(shape, functools.partial(lambda m, b, dev_ref: m(b), where))
                for _, shape, where in outs
            ],
            scratch_shapes=[pltpu.VMEM((reps,) + block_shape, F32)],
        ),
        out_shape=[jax.ShapeDtypeStruct(shape, F32) for shape, _, _ in outs],
        cost_estimate=cost(reps * blocks[0].size * 6),
    )(devices, *blocks)


def layouts(lengths, seq_owner, devices, rows):
    count = lengths.shape[0]
    mine = seq_owner[None, :] == devices[:, None]
    own_length = jnp.where(mine, lengths[None, :], 0)
    numbers = jnp.arange(count, dtype=jnp.int32)
    ahead = numbers[:, None] < numbers[None, :]
    starts = jnp.sum(jnp.where(ahead[None], own_length[:, :, None], 0), 1)[:, None, :]
    ends = starts + own_length[:, None, :]
    row = jnp.arange(rows, dtype=jnp.int32)[None, :, None]
    inside = mine[:, None, :] & (row >= starts) & (row < ends)
    valid = jnp.any(inside, 2, keepdims=True)
    segment = jnp.sum(jnp.where(inside, numbers, 0), 2, keepdims=True)
    position = row - jnp.sum(jnp.where(inside, starts, 0), 2, keepdims=True)
    return jnp.where(valid, segment, count), position, valid


def make_local(reps, shards):
    group = Group(reps, shards)
    heads = HEADS // reps
    half = 32 * heads
    width = 2 * half

    def local(
        tokens,
        cotangent,
        lengths,
        seq_owner,
        expert_ids,
        attention_gain,
        query_weight,
        latent_down,
        latent_gain,
        latent_up,
        output_weight,
        feedforward_gain,
        router_weight,
        shared_gate,
        shared_up,
        shared_down,
        expert_gate,
        expert_up,
        expert_down,
    ):
        rows, model = tokens.shape
        rep = lax.axis_index("rep")
        shard = lax.axis_index("shard")
        devices = group.devices(rep)
        slab = model // shards
        strip = slab // reps
        lat = latent_gain.shape[0]
        cut = group.half * rows

        tokens_parts = group.gather(tokens)

        small = jnp.concatenate(
            [
                lax.dynamic_slice_in_dim(latent_down, rep * strip, strip, 0),
                lax.dynamic_slice_in_dim(router_weight, rep * strip, strip, 0),
            ],
            1,
        )
        small = lax.all_gather(small, ("shard", "rep"), axis=0, tiled=True)
        output_all = lax.all_gather(
            lax.dynamic_slice_in_dim(output_weight, rep * strip, strip, 0),
            ("shard", "rep"),
            axis=0,
            tiled=True,
        )

        query_cols = heads * (NOPE + ROPE)
        up_cols = heads * (NOPE + VDIM)
        query_wide = round_up(query_cols, 128)
        query_part = lax.dynamic_slice_in_dim(
            query_weight, rep * query_cols, query_cols, 1
        ).reshape(slab, heads, NOPE + ROPE)
        query_part = jnp.concatenate(
            [
                query_part[:, :, :NOPE].reshape(slab, heads * NOPE),
                query_part[:, :, NOPE : NOPE + 32].reshape(slab, half),
                query_part[:, :, NOPE + 32 :].reshape(slab, half),
                jnp.zeros((slab, query_wide - query_cols), LOW),
            ],
            1,
        )
        up_part = lax.dynamic_slice_in_dim(latent_up, rep * up_cols, up_cols, 1)
        up_part = fold(up_part, slab)
        gain_rows = jnp.concatenate([attention_gain, feedforward_gain, latent_gain])
        gain_lanes = query_wide + 128
        gain_count = round_up(gain_rows.shape[0], 16 * gain_lanes)
        gain_rows = jnp.pad(gain_rows, (0, gain_count - gain_rows.shape[0])).reshape(-1, gain_lanes)
        query_up, gains = shard_merge(
            group,
            jnp.concatenate([jnp.concatenate([query_part, up_part], 1), gain_rows], 0),
            shard,
            [(0, slab), (slab, gain_rows.shape[0])],
        )
        query_all = query_up[:, :, :query_cols].reshape(model, query_cols)
        up_all = jnp.concatenate(
            [
                query_up[:, i * lat : (i + 1) * lat, query_wide:].reshape(RANK, 128)
                for i in range(up_cols // 128)
            ],
            1,
        )
        gains = gains.reshape(shards, -1).astype(F32)
        attention_gain_all = gains[:, :slab].reshape(1, model)
        mixer_gain_all = gains[:, slab : 2 * slab].reshape(1, model)
        latent_gain_all = gains[:, 2 * slab : 2 * slab + lat].reshape(1, RANK)

        part_s = shared_down.shape[0] // reps
        local_e = expert_down.shape[1]
        part_e = WINDOW * local_e // reps
        per = reps // WINDOW
        my_expert = rep // per
        used = part_s + part_e
        hidden = round_up(shards * used, 128)
        unit = hidden // shards
        place = jnp.arange(hidden, dtype=jnp.int32)
        within = place % unit
        is_shared = within < part_s
        is_expert = (within >= part_s) & (within < used)
        from_shared = jnp.where(
            is_shared, (place // unit) * shared_down.shape[0] + rep * part_s + within, -1
        )
        from_expert = jnp.where(
            is_expert, (place // unit) * local_e + (rep % per) * part_e + within - part_s, -1
        )
        pick_s = (
            jnp.arange(shared_gate.shape[1], dtype=jnp.int32)[:, None] == from_shared[None, :]
        ).astype(LOW)
        pick_e = (
            jnp.arange(expert_gate.shape[2], dtype=jnp.int32)[:, None] == from_expert[None, :]
        ).astype(LOW)

        def my_columns(shared, expert):
            expert = lax.dynamic_index_in_dim(expert, my_expert, 0, keepdims=False)
            return (dot(shared, pick_s) + dot(expert, pick_e)).astype(LOW)

        gate_all, raise_all = shard_merge(
            group,
            jnp.concatenate(
                [my_columns(shared_gate, expert_gate), my_columns(shared_up, expert_up)], 0
            ),
            shard,
            [(0, slab), (slab, slab)],
        )
        gate_all = gate_all.reshape(model, hidden)
        raise_all = raise_all.reshape(model, hidden)
        lower_part = jnp.concatenate(
            [
                lax.dynamic_slice_in_dim(shared_down, rep * part_s, part_s, 0),
                lax.dynamic_slice(
                    expert_down, (my_expert, (rep % per) * part_e, 0), (1, part_e, model)
                )[0],
                jnp.zeros((unit - used, model), LOW),
            ],
            0,
        )
        (lower_all,) = shard_merge(group, lower_part, shard, [(0, unit)])
        lower_all = lower_all.reshape(hidden, model)

        segment, position, valid = layouts(lengths, seq_owner, devices * shards + shard, rows)
        total_rows = reps * rows
        seg_col = segment.reshape(total_rows, 1)
        seg_row = segment.reshape(reps, 1, rows)
        valid_all = valid.reshape(total_rows, 1).astype(F32)
        valid_own = valid_all[:rows]
        frequency = jnp.power(ROPE_BASE, -2.0 * jnp.arange(32, dtype=F32) / ROPE)
        angles = position.reshape(total_rows, 1).astype(F32) * jnp.tile(frequency, 2 * heads)[None]
        cosine = jnp.cos(angles)
        side = jnp.where(jnp.arange(width) < half, -1.0, 1.0).astype(F32)
        sine = jnp.sin(angles) * side[None, :]

        hidden_in = tokens.astype(F32)
        counts = jnp.sum(
            (expert_ids[:, :, None] == jnp.arange(NEXP, dtype=jnp.int32)).astype(F32), 1
        )
        given = jnp.concatenate(
            [cotangent, jnp.zeros((rows, 128 - NEXP), LOW), counts.astype(LOW)], 1
        )
        given_parts = group.gather(given)
        grad_all = merge_rows(
            given_parts,
            lambda block, ok: (block[:, :model].astype(F32) * ok).astype(LOW),
            [valid_all],
            model,
        )
        counts_all = merge_rows(given_parts, lambda block: block[:, model:], [], 128)

        lane = jnp.arange(heads * width, dtype=jnp.int32)
        head = lane // width
        spot = lane % width
        source = jnp.where(
            (spot % half) // 32 == head, (spot // half) * 32 + spot % 32, -1
        )
        spread = (jnp.arange(ROPE, dtype=jnp.int32)[:, None] == source[None, :]).astype(LOW)
        cols = heads * VDIM
        normed_all, qn, qr, keyval, kr, latent_low, latent_own, attended = attend_forward(
            devices,
            tokens_parts,
            attention_gain_all,
            latent_gain_all,
            query_all,
            small,
            up_all,
            spread,
            cosine,
            sine,
            seg_col,
            seg_row,
        )
        attended_own = lax.all_to_all(
            attended.reshape(reps, rows, cols), "rep", 0, 0, tiled=True
        )
        attended_own = jnp.transpose(attended_own, (1, 0, 2)).reshape(rows, HEADS * VDIM)
        mid = hidden_in + dot(attended_own, output_all)
        mixed_scale = rms_scale(mid)
        mixed = (mid * mixed_scale * mixer_gain_all).astype(LOW)

        (
            mixed_all,
            hidden_low,
            d_gate,
            d_lift,
            d_mixed_first,
            d_mixed_second,
            ffn_first,
            ffn_second,
            d_weight,
            sig_own,
        ) = experts(
            jnp.reshape(my_expert, (1,)).astype(jnp.int32),
            group.gather(mixed),
            grad_all,
            counts_all,
            valid_all,
            small,
            gate_all,
            raise_all,
            lower_all,
            is_expert.astype(F32)[None, :],
        )
        sig_own = sig_own[:, -NEXP:]
        d_mixed = group.reduce(d_mixed_second, d_mixed_first)
        numbers = jnp.arange(reps, dtype=jnp.int32)
        by_device = jnp.sum(
            jnp.where(
                (devices[None, :] == numbers[:, None])[:, :, None],
                d_weight.reshape(1, reps, rows),
                0.0,
            ),
            1,
        )
        d_weight_own = lax.all_to_all(by_device, "rep", 0, 0, tiled=True)
        d_weight_own = jnp.sum(d_weight_own.reshape(WINDOW, per, rows), 1)
        ffn = group.reduce(ffn_second, ffn_first)
        layer_out = (valid_own * (mid + ffn)).astype(LOW)

        def finish(value):
            value = group.reduce_shard(
                value.reshape(shards, value.shape[0] // shards, value.shape[1]), shard
            )
            return value.astype(LOW)

        gate_grad = dot_rows(mixed_all, d_gate).astype(LOW)
        lift_grad = dot_rows(mixed_all, d_lift).astype(LOW)
        lower_grad = finish(dot_rows(hidden_low, grad_all).astype(LOW))[:used]

        tile = min(slab, 64)

        def place_columns(step, j, block, refs):
            for s in range(shards):
                at = s * part_s * reps + j * part_s
                refs[0][:, at : at + part_s] = block[:, s * unit : s * unit + part_s]
                at = s * part_e * per + (j % per) * part_e
                refs[1][j // per, :, at : at + part_e] = block[:, s * unit + part_s : s * unit + used]

        def hidden_columns(value):
            shared = shared_gate.shape
            expert = expert_gate.shape
            return assemble(
                group.gather(value),
                devices,
                slab // tile,
                (tile, hidden),
                lambda b: (b, 0),
                [
                    (shared, (tile, shared[1]), lambda b: (b, 0)),
                    (expert, (WINDOW, tile, expert[2]), lambda b: (0, b, 0)),
                ],
                place_columns,
            )

        sgate_grad, egate_grad = hidden_columns(finish(gate_grad))
        sup_grad, eup_grad = hidden_columns(finish(lift_grad))

        def place_rows(step, j, block, refs):
            refs[0][j * part_s : (j + 1) * part_s] = block[:part_s]
            at = (j % per) * part_e
            refs[1][j // per, at : at + part_e] = block[part_s:]

        lane_tile = 256
        sdown_grad, edown_grad = assemble(
            group.gather(lower_grad),
            devices,
            model // lane_tile,
            (used, lane_tile),
            lambda b: (0, b),
            [
                (shared_down.shape, (shared_down.shape[0], lane_tile), lambda b: (0, b)),
                (expert_down.shape, (WINDOW, local_e, lane_tile), lambda b: (0, 0, b)),
            ],
            place_rows,
        )

        total_own = jnp.sum(sig_own * counts, 1, keepdims=True)
        hit = counts[:, :WINDOW]
        d_route = jnp.concatenate(
            [valid_own * d_weight_own.T * hit, jnp.zeros((rows, NEXP - WINDOW), F32)], 1
        )
        inner = jnp.sum(d_route * sig_own, 1, keepdims=True)
        d_sig = ROUTE_SCALE * (d_route / total_own - counts * inner / (total_own * total_own))
        d_logits = (d_sig * sig_own * (1.0 - sig_own)).astype(LOW)
        d_mixed = d_mixed + dot_last(d_logits, small[:, RANK + ROPE :])
        grad_own = cotangent.astype(F32) * valid_own
        d_mid = grad_own + rms_back(mid, mixed_scale, mixer_gain_all, d_mixed)
        d_branch = d_mid.astype(LOW)

        d_attended = dot_last(d_branch, output_all).astype(LOW)
        d_attended = jnp.transpose(d_attended.reshape(rows, reps, cols), (1, 0, 2))
        d_attended = lax.all_to_all(d_attended, "rep", 0, 0, tiled=True)
        d_attended = d_attended.reshape(total_rows, cols)
        (
            d_normed_first,
            d_normed_second,
            latent_first,
            latent_second,
            query_grad,
            up_grad,
        ) = attend_backward(
            devices,
            (qn, qr, keyval, kr),
            d_attended,
            normed_all,
            latent_low,
            query_all,
            up_all,
            cosine,
            sine,
            seg_col,
            seg_row,
            rows,
        )
        d_latent_sum = group.reduce(latent_second, latent_first)
        d_normed = group.reduce(d_normed_second, d_normed_first)
        compressed = latent_own[:, :RANK]
        d_compressed = rms_back(
            compressed, rms_scale(compressed), latent_gain_all, d_latent_sum[:, :RANK]
        )
        kg_first = d_latent_sum[:, RANK : RANK + 32]
        kg_second = d_latent_sum[:, RANK + 32 :]
        cos_own = cosine[:rows, :32]
        sin_own = sine[:rows, half : half + 32]
        d_latent = jnp.concatenate(
            [
                d_compressed,
                kg_first * cos_own + kg_second * sin_own,
                kg_second * cos_own - kg_first * sin_own,
            ],
            1,
        ).astype(LOW)
        d_normed = d_normed + dot_last(d_latent, small[:, : RANK + ROPE])
        token_grad = d_mid + rms_back(
            hidden_in, rms_scale(hidden_in), attention_gain_all, d_normed
        )

        out_cols = model // reps

        def output_part(index):
            picked = [
                lax.dynamic_slice_in_dim(d_branch, devices[k] * out_cols, out_cols, 1)
                for k in index
            ]
            return dot_rows(attended_own, jnp.concatenate(picked, 1)).astype(LOW)

        output_grad = group.reduce(
            output_part(range(group.half, reps)), output_part(range(group.half)), axis=1
        )
        wide = round_up(out_cols, 128)
        attention_grad = jnp.concatenate(
            [
                query_grad.reshape(shards, slab, query_cols),
                jnp.zeros((shards, slab, query_wide - query_cols), LOW),
                output_grad.astype(LOW).reshape(shards, slab, out_cols),
                jnp.zeros((shards, slab, wide - out_cols), LOW),
                jax.vmap(lambda v: fold(v, slab))(
                    up_grad.reshape(shards, lat, up_cols)
                ),
            ],
            2,
        )
        attention_grad = group.reduce_shard(attention_grad, shard).astype(LOW)

        def place_attention(step, j, block, refs):
            for h in range(heads):
                base = j * query_cols + h * (NOPE + ROPE)
                refs[0][:, base : base + NOPE] = block[:, h * NOPE : (h + 1) * NOPE]
                at = heads * NOPE + 32 * h
                refs[0][:, base + NOPE : base + NOPE + 32] = block[:, at : at + 32]
                refs[0][:, base + NOPE + 32 : base + NOPE + ROPE] = block[
                    :, at + half : at + half + 32
                ]
            refs[1][:, j * out_cols : (j + 1) * out_cols] = block[
                :, query_wide : query_wide + out_cols
            ]

            @pl.when(step < up_cols // 128)
            def _():
                at = pl.multiple_of(j * up_cols + step * 128, 128)
                refs[2][:, pl.ds(at, 128)] = block[:, query_wide + wide :]

        query_grad, output_grad, up_grad = assemble(
            group.gather(attention_grad),
            devices,
            slab // lat,
            (lat, query_wide + wide + 128),
            lambda b: (b, 0),
            [
                (query_weight.shape, (lat, query_weight.shape[1]), lambda b: (b, 0)),
                (output_weight.shape, (lat, model), lambda b: (b, 0)),
                (latent_up.shape, latent_up.shape, lambda b: (0, 0)),
            ],
            place_attention,
        )

        row_grads = merge_rows(
            group.gather(jnp.concatenate([d_latent, d_logits], 1)),
            lambda block: block,
            [],
            RANK + ROPE + NEXP,
        )

        def my_strip(values):
            return jnp.concatenate(
                [
                    lax.dynamic_slice_in_dim(values, s * slab + rep * strip, strip, 1)
                    for s in range(shards)
                ],
                1,
            )

        strip_grad = jnp.concatenate(
            [
                dot_rows(my_strip(normed_all), row_grads[:, : RANK + ROPE]),
                dot_rows(my_strip(mixed_all), row_grads[:, RANK + ROPE :]),
            ],
            1,
        ).astype(LOW)

        def place_strip(step, j, block, refs):
            refs[0][j * strip : (j + 1) * strip] = block[:, : RANK + ROPE]
            refs[1][j * strip : (j + 1) * strip] = block[:, RANK + ROPE :]

        down_grad, router_grad = assemble(
            group.gather(finish(strip_grad)),
            devices,
            1,
            (strip, RANK + ROPE + NEXP),
            lambda b: (0, 0),
            [
                (latent_down.shape, latent_down.shape, lambda b: (0, 0)),
                (router_weight.shape, router_weight.shape, lambda b: (0, 0)),
            ],
            place_strip,
        )

        def row_sum(weight, grad):
            return jnp.sum(weight.astype(F32) * grad, -1)

        attention_gain_grad = (
            row_sum(query_weight, query_grad) + row_sum(latent_down, down_grad)
        ) / attention_gain.astype(F32)
        latent_gain_grad = row_sum(latent_up, up_grad) / latent_gain.astype(F32)
        mixer_gain_grad = (
            row_sum(router_weight, router_grad)
            + row_sum(shared_gate, sgate_grad)
            + row_sum(shared_up, sup_grad)
            + jnp.sum(row_sum(expert_gate, egate_grad) + row_sum(expert_up, eup_grad), 0)
        ) / feedforward_gain.astype(F32)

        return (
            layer_out,
            token_grad,
            attention_gain_grad,
            query_grad,
            down_grad,
            latent_gain_grad,
            up_grad,
            output_grad,
            mixer_gain_grad,
            router_grad,
            sgate_grad,
            sup_grad,
            sdown_grad,
            egate_grad,
            eup_grad,
            edown_grad,
        )

    return local


def fold(value, rows):
    count = value.shape[1] // 128
    parts = [value[:, i * 128 : (i + 1) * 128] for i in range(count)]
    left = rows - count * value.shape[0]
    if left:
        parts.append(jnp.zeros((left, 128), value.dtype))
    return jnp.concatenate(parts, 0)


def solution(mesh):
    tokens = P(("rep", "shard"), None)
    vector = P("shard")
    matrix = P("shard", None)
    stack = P(None, "shard", None)
    in_specs = (
        (tokens, tokens, P(), P(), tokens, vector, matrix, matrix, vector, matrix, matrix, vector)
        + (matrix,) * 4
        + (stack,) * 3
    )
    out_specs = (
        (tokens, tokens, vector, matrix, matrix, vector, matrix, matrix, vector)
        + (matrix,) * 4
        + (stack,) * 3
    )
    local = make_local(mesh.shape["rep"], mesh.shape["shard"])
    return jax.shard_map(local, mesh=mesh, in_specs=in_specs, out_specs=out_specs, check_vma=False)
```

```python
import functools

import jax
import jax.numpy as jnp
from jax import lax
from jax.experimental import pallas as pl
from jax.experimental.pallas import tpu as pltpu
from jax.sharding import PartitionSpec as P

HEADS = 16
NOPE = 128
ROPE = 64
VDIM = 128
RANK = 512
NEXP = 64
WINDOW = 2

EPSILON = 1e-06
ROPE_BASE = 50000.0
ROUTE_SCALE = 2.446
NEG_FILL = -1e30
SCORE_SCALE = (NOPE + ROPE) ** (-0.5)

F32 = jnp.float32
LOW = jnp.bfloat16


def dot(left, right):
    return jnp.dot(left, right, preferred_element_type=F32)


def dot_rows(left, right):
    return lax.dot_general(left, right, (((0,), (0,)), ((), ())), preferred_element_type=F32)


def dot_last(left, right):
    return lax.dot_general(left, right, (((1,), (1,)), ((), ())), preferred_element_type=F32)


def rms_scale(values):
    return lax.rsqrt(jnp.mean(values * values, -1, keepdims=True) + EPSILON)


def rms_back(values, scale, gain, upstream):
    gained = upstream * gain
    inner = jnp.mean(values * gained, -1, keepdims=True)
    return scale * gained - values * scale * scale * scale * inner


def round_up(value, unit):
    return -(-value // unit) * unit


class Group:
    def __init__(self, reps, shards):
        self.reps = reps
        self.shards = shards
        bits = reps.bit_length() - 1
        assert bits >= 1 and 1 << bits == reps
        self.levels = [(1 << b, 1 << (bits - b)) for b in range(1, bits)]
        self.half = reps // 2

    def devices(self, rep):
        lists = []
        for side in (0, 1):
            masks = [0]
            for level in self.levels:
                masks = masks + [m ^ level[side] for m in masks]
            lists.append(masks)
        first = lists[0] + [m ^ 1 for m in lists[1]]
        second = lists[1] + [m ^ 1 for m in lists[0]]
        masks = jnp.where(
            rep % 2 == 0, jnp.array(first, jnp.int32), jnp.array(second, jnp.int32)
        )
        return rep.astype(jnp.int32) ^ masks

    def cross(self, value, level):
        pairs = [(i, i ^ level[i & 1]) for i in range(self.reps)]
        return lax.ppermute(value, "rep", pairs)


class Gathering:
    def __init__(self, group, block):
        self.group = group
        self.blocks = {0: block}
        self.stage = 0
        self.pending = {}

    def start(self):
        group = self.group
        self.stage += 1
        if self.stage <= len(group.levels):
            for k in range(group.half):
                if bin(k).count("1") == self.stage:
                    top = k.bit_length() - 1
                    self.pending[k] = group.cross(self.blocks[k ^ (1 << top)], group.levels[top])
        elif self.stage == len(group.levels) + 1:
            for k in range(group.half):
                self.pending[group.half + k] = group.cross(self.blocks[k], (1, 1))

    def settle(self, values):
        self.blocks.update(zip(self.pending, values))
        self.pending = {}

    def list(self):
        while True:
            self.settle(list(self.pending.values()))
            if len(self.blocks) == self.group.reps:
                return [self.blocks[k] for k in range(self.group.reps)]
            self.start()


class Reducing:
    def __init__(self, group, second, first, axis=0):
        self.group = group
        self.second = second
        self.terms = [first]
        self.axis = axis
        self.size = first.shape[axis]
        self.stage = 0
        self.pending = {}

    def cut(self, start, size):
        total = None
        for term in self.terms:
            term = lax.slice_in_dim(term, start, start + size, axis=self.axis).astype(F32)
            total = term if total is None else total + term
        return total

    def start(self):
        levels = self.group.levels
        if self.stage == 0:
            self.pending[0] = self.group.cross(self.second, (1, 1))
        elif self.stage <= len(levels):
            self.size //= 2
            sent = self.cut(self.size, self.size).astype(LOW)
            self.pending[0] = self.group.cross(sent, levels[len(levels) - self.stage])
        self.stage += 1

    def settle(self, values):
        self.terms += values
        self.pending = {}

    def total(self):
        while True:
            self.settle(list(self.pending.values()))
            if self.stage > len(self.group.levels):
                return self.cut(0, self.size)
            self.start()


class Shifting:
    def __init__(self, group, block):
        self.count = group.shards
        self.block = block
        self.found = {}
        self.stage = 0
        self.pending = {}

    def start(self):
        count = self.count
        self.stage += 1

        def cycle(step):
            return [((i + step) % count, i) for i in range(count)]

        def move(value, pairs):
            return lax.ppermute(value, "shard", pairs)

        if count != 4:
            if self.stage == 1:
                self.pending = {k: move(self.block, cycle(k)) for k in range(1, count)}
        elif self.stage == 1:
            self.pending = {
                2: move(self.block, cycle(2)),
                "above": move(self.block, cycle(1)[:-1]),
                "below": move(self.block, cycle(3)[1:]),
            }
        elif self.stage == 2:
            self.pending = {"last": move(self.found[2], [(1, 0), (2, 3)])}

    def settle(self, values):
        self.found.update(zip(self.pending, values))
        self.pending = {}

    def result(self):
        self.settle(list(self.pending.values()))
        while self.stage < 2:
            self.start()
            self.settle(list(self.pending.values()))
        return list(self.found.items())

    def whole(self, position):
        found = dict(self.result())
        if self.count == 4:
            last = found.pop("last")
            found[1] = jnp.where(position == self.count - 1, last, found.pop("above"))
            found[3] = jnp.where(position == 0, last, found.pop("below"))
        return [(k, found[k]) for k in range(1, self.count)]


def phase(*items):
    values = []
    for item in items:
        values += list(item.pending.values()) if hasattr(item, "pending") else [item]
    values = list(lax.optimization_barrier(tuple(values)))
    arrays = []
    for item in items:
        if hasattr(item, "pending"):
            count = len(item.pending)
            item.settle(values[:count])
            values = values[count:]
        else:
            arrays.append(values.pop(0))
    return arrays


def head_probs(h, allowed, q_nope, q_rope, keyval, k_rope):
    width = q_rope.shape[1]
    base = h * (NOPE + VDIM)
    scores = dot_last(q_nope[:, h * NOPE : (h + 1) * NOPE], keyval[:, base : base + NOPE])
    scores = scores + dot_last(q_rope, k_rope[:, h * width : (h + 1) * width])
    scores = jnp.where(allowed, scores * SCORE_SCALE, NEG_FILL)
    unnormed = jnp.exp(scores - jnp.max(scores, -1, keepdims=True))
    return unnormed / jnp.sum(unnormed, -1, keepdims=True)


def same_segment(sc_ref, sr_ref):
    rows = sc_ref.shape[0]
    t = lax.broadcasted_iota(jnp.int32, (rows, rows), 0)
    u = lax.broadcasted_iota(jnp.int32, (rows, rows), 1)
    return (sc_ref[...] == sr_ref[0]) & (u <= t)


def turned(values):
    half = values.shape[1] // 2
    return jnp.concatenate([values[:, half:], values[:, :half]], 1)


def whole(a):
    return pl.BlockSpec(a.shape, lambda b, dev_ref: (0,) * a.ndim, pipeline_mode=pl.Buffered(1))


def attend_forward(
    devices, blocks, gain, latent_gain, query_up, heads, small_w, spread, cosine, sine, seg_col, seg_row
):
    count = len(blocks)
    rows, model = blocks[0].shape
    shards, slab, lanes = query_up.shape
    query_wide = lanes - 128
    lat = RANK // shards
    up_cols = heads * (NOPE + VDIM)
    half = 32 * heads
    width = 2 * half

    def kernel(dev_ref, *refs):
        parts = refs[:count]
        gain_ref, lgain_ref, qu_ref, sw_ref, spread_ref, cos_ref, sin_ref, sc_ref, sr_ref = (
            refs[count : count + 9]
        )
        normed_ref, qn_ref, qr_ref, kv_ref, kr_ref, low_ref, up_ref, own_ref, out_ref, held = refs[
            count + 9 :
        ]
        step = pl.program_id(0)
        for k in range(count):

            @pl.when(step == k)
            def _():
                held[...] = parts[k][...]

        @pl.when(step == 0)
        def _():
            for z in range(shards):
                for i in range(up_cols // 128):
                    up_ref[z * lat : (z + 1) * lat, i * 128 : (i + 1) * 128] = qu_ref[
                        z, i * lat : (i + 1) * lat, query_wide:
                    ]

        x = held[...].astype(F32)
        normed = (x * rms_scale(x) * gain_ref[...]).astype(LOW)
        normed_ref[...] = normed
        query = dot(normed, qu_ref[:, :, :query_wide].reshape(model, query_wide))
        at = [h * (NOPE + ROPE) for h in range(heads)]
        q_nope = jnp.concatenate([query[:, i : i + NOPE] for i in at], 1).astype(LOW)
        q_rope = jnp.concatenate(
            [query[:, i + NOPE + c : i + NOPE + c + 32] for c in (0, 32) for i in at], 1
        )
        cos = cos_ref[...]
        sin = sin_ref[...]
        q_rope = (q_rope * cos + turned(q_rope) * sin).astype(LOW)
        latent = dot(normed, sw_ref[...])

        @pl.when(step == 0)
        def _():
            own_ref[...] = latent

        compressed = latent[:, :RANK]
        low = (compressed * rms_scale(compressed) * lgain_ref[...]).astype(LOW)
        key = latent[:, RANK : RANK + ROPE]
        key = key * cos[:, :ROPE] + turned(key) * sin[:, half - 32 : half + 32]
        k_rope = dot(key.astype(LOW), spread_ref[...]).astype(LOW)
        keyval = dot(low, up_ref[...]).astype(LOW)
        qn_ref[...] = q_nope
        qr_ref[...] = q_rope
        kv_ref[...] = keyval
        kr_ref[...] = k_rope
        low_ref[...] = low
        allowed = same_segment(sc_ref, sr_ref)
        for h in range(heads):
            probs = head_probs(h, allowed, q_nope, q_rope, keyval, k_rope)
            base = h * (NOPE + VDIM) + NOPE
            out_ref[:, h * VDIM : (h + 1) * VDIM] = dot(
                probs.astype(LOW), keyval[:, base : base + VDIM]
            ).astype(LOW)

    def tok(cols):
        return pl.BlockSpec((rows, cols), lambda b, dev_ref: (b, 0))

    total = count * rows
    widths = [model, heads * NOPE, width, heads * (NOPE + VDIM), heads * width, RANK]
    return pl.pallas_call(
        kernel,
        grid_spec=pltpu.PrefetchScalarGridSpec(
            num_scalar_prefetch=1,
            grid=(count,),
            in_specs=[whole(a) for a in blocks]
            + [whole(a) for a in (gain, latent_gain, query_up, small_w, spread)]
            + [tok(width), tok(width), tok(1)]
            + [pl.BlockSpec((1, 1, rows), lambda b, dev_ref: (b, 0, 0))],
            out_specs=[tok(w) for w in widths]
            + [
                pl.BlockSpec((RANK, up_cols), lambda b, dev_ref: (0, 0)),
                pl.BlockSpec((rows, small_w.shape[1]), lambda b, dev_ref: (0, 0)),
            ]
            + [pl.BlockSpec((rows, heads * VDIM), lambda b, dev_ref: (dev_ref[b], 0))],
            scratch_shapes=[pltpu.VMEM((rows, model), LOW)],
        ),
        out_shape=[jax.ShapeDtypeStruct((total, w), LOW) for w in widths]
        + [
            jax.ShapeDtypeStruct((RANK, up_cols), LOW),
            jax.ShapeDtypeStruct((rows, small_w.shape[1]), F32),
        ]
        + [jax.ShapeDtypeStruct((total, heads * VDIM), LOW)],
        cost_estimate=cost(total * model * 6),
    )(devices, *blocks, gain, latent_gain, query_up, small_w, spread, cosine, sine, seg_col, seg_row)


def attend_backward(
    devices, kept, given, normed, low, query_up, up_w, cosine, sine, seg_col, seg_row, rows
):
    q_nope, q_rope, keyval, k_rope = kept
    total, model = normed.shape
    count = total // rows
    heads = up_w.shape[1] // (NOPE + VDIM)
    half = 32 * heads
    width = 2 * half
    nope = heads * NOPE
    middle = count // 2
    shards, slab, lanes = query_up.shape
    query_wide = lanes - 128
    lat = RANK // shards
    up_cols = up_w.shape[1]

    def kernel(
        dev_ref,
        qn_ref,
        qr_ref,
        kv_ref,
        kr_ref,
        da_ref,
        n_ref,
        low_ref,
        qu_ref,
        uw_ref,
        cos_ref,
        sin_ref,
        sc_ref,
        sr_ref,
        first_ref,
        second_ref,
        lat_first_ref,
        lat_second_ref,
        grad_ref,
        q_sum,
        u_sum,
    ):
        step = pl.program_id(0)
        allowed = same_segment(sc_ref, sr_ref)
        qn = qn_ref[...]
        qr = qr_ref[...]
        kv = kv_ref[...]
        kr = kr_ref[...]
        d_rope = None
        d_key = None
        d_nope = []
        d_keyval = []
        for h in range(heads):
            probs = head_probs(h, allowed, qn, qr, kv, kr)
            base = h * (NOPE + VDIM)
            keys = kv[:, base : base + NOPE]
            values = kv[:, base + NOPE : base + NOPE + VDIM]
            d_att = da_ref[:, h * VDIM : (h + 1) * VDIM]
            d_values = dot_rows(probs.astype(LOW), d_att)
            d_probs = dot_last(d_att, values)
            inner = jnp.sum(probs * d_probs, -1, keepdims=True)
            d_scores = (probs * (d_probs - inner)).astype(LOW)
            d_nope.append((dot(d_scores, keys) * SCORE_SCALE).astype(LOW))
            rope = dot(d_scores, kr[:, h * width : (h + 1) * width])
            d_rope = rope if d_rope is None else d_rope + rope
            d_keys = dot_rows(d_scores, qn[:, h * NOPE : (h + 1) * NOPE]) * SCORE_SCALE
            d_keyval += [d_keys.astype(LOW), d_values.astype(LOW)]
            turn = dot_rows(d_scores, qr)
            turn = jnp.concatenate(
                [turn[:, 32 * h : 32 * h + 32], turn[:, half + 32 * h : half + 32 * h + 32]], 1
            )
            d_key = turn if d_key is None else d_key + turn
        d_rope = d_rope * SCORE_SCALE
        d_rope = (d_rope * cos_ref[...] - turned(d_rope) * sin_ref[...]).astype(LOW)
        pieces = []
        for h in range(heads):
            pieces += [d_nope[h], d_rope[:, 32 * h : 32 * h + 32]]
            pieces.append(d_rope[:, half + 32 * h : half + 32 * h + 32])
        if query_wide > heads * (NOPE + ROPE):
            pieces.append(jnp.zeros((rows, query_wide - heads * (NOPE + ROPE)), LOW))
        d_query = jnp.concatenate(pieces, 1)
        d_keyval = jnp.concatenate(d_keyval, 1)
        d_key = (d_key * SCORE_SCALE).astype(LOW)
        d_normed = dot_last(
            d_query, qu_ref[:, :, :query_wide].reshape(model, query_wide)
        ).astype(LOW)
        d_low = dot_last(d_keyval, uw_ref[...]).astype(LOW)

        @pl.when(step < middle)
        def _():
            first_ref[...] = d_normed
            lat_first_ref[:, :RANK] = d_low
            lat_first_ref[:, RANK:] = d_key

        @pl.when(step >= middle)
        def _():
            second_ref[...] = d_normed
            lat_second_ref[:, :RANK] = d_low
            lat_second_ref[:, RANK:] = d_key

        q_add = dot_rows(n_ref[...], d_query)
        u_add = dot_rows(low_ref[...], d_keyval)

        @pl.when(step == 0)
        def _():
            q_sum[...] = q_add
            u_sum[...] = u_add

        @pl.when(step > 0)
        def _():
            q_sum[...] += q_add
            u_sum[...] += u_add

        @pl.when(step == count - 1)
        def _():
            grad_ref[...] = jnp.zeros(grad_ref.shape, LOW)
            for z in range(shards):
                grad_ref[z, :, :query_wide] = q_sum[z * slab : (z + 1) * slab].astype(LOW)
                for i in range(up_cols // 128):
                    grad_ref[z, i * lat : (i + 1) * lat, query_wide:] = u_sum[
                        z * lat : (z + 1) * lat, i * 128 : (i + 1) * 128
                    ].astype(LOW)

    def tok(a):
        return pl.BlockSpec((rows, a.shape[1]), lambda b, dev_ref: (b, 0))

    def low_half(cols):
        return pl.BlockSpec((rows, cols), lambda b, dev_ref: (jnp.minimum(b, middle - 1), 0))

    def high_half(cols):
        return pl.BlockSpec((rows, cols), lambda b, dev_ref: (jnp.maximum(b - middle, 0), 0))

    arrays = [q_nope, q_rope, keyval, k_rope]
    wide = RANK + ROPE
    return pl.pallas_call(
        kernel,
        grid_spec=pltpu.PrefetchScalarGridSpec(
            num_scalar_prefetch=1,
            grid=(count,),
            in_specs=[tok(a) for a in arrays]
            + [pl.BlockSpec((rows, given.shape[1]), lambda b, dev_ref: (dev_ref[b], 0))]
            + [tok(normed), tok(low), whole(query_up), whole(up_w), tok(cosine), tok(sine)]
            + [tok(seg_col), pl.BlockSpec((1, 1, rows), lambda b, dev_ref: (b, 0, 0))],
            out_specs=[low_half(model), high_half(model), low_half(wide), high_half(wide)]
            + [pl.BlockSpec(query_up.shape, lambda b, dev_ref: (0, 0, 0))],
            scratch_shapes=[pltpu.VMEM((model, query_wide), F32), pltpu.VMEM(up_w.shape, F32)],
        ),
        out_shape=[
            jax.ShapeDtypeStruct((total // 2, model), LOW),
            jax.ShapeDtypeStruct((total // 2, model), LOW),
            jax.ShapeDtypeStruct((total // 2, wide), LOW),
            jax.ShapeDtypeStruct((total // 2, wide), LOW),
            jax.ShapeDtypeStruct(query_up.shape, LOW),
        ],
        cost_estimate=cost(total * model * 6),
    )(devices, *arrays, given, normed, low, query_up, up_w, cosine, sine, seg_col, seg_row)


def experts(info, blocks, grad, counts, valid, small_w, gate_w, lower_w, is_expert):
    count = len(blocks)
    rows, model = blocks[0].shape
    hidden = gate_w.shape[1] // 2
    total = count * rows
    middle = count // 2
    lanes = counts.shape[1]
    router_at = small_w.shape[1] - lanes

    def kernel(info_ref, *refs):
        parts = refs[:count]
        grad_ref, counts_ref, valid_ref, sw_ref, gw_ref, lw_ref, ex_ref = refs[count : count + 7]
        (
            mixed_ref,
            hid_ref,
            dg_ref,
            dm_first,
            dm_second,
            out_first,
            out_second,
            dw_ref,
            sig_ref,
            held,
        ) = refs[count + 7 :]
        step = pl.program_id(0)
        for k in range(count):

            @pl.when(step == k)
            def _():
                held[...] = parts[k][...]

        mixed = held[...]
        mixed_ref[...] = mixed
        sig = jax.nn.sigmoid(dot(mixed, sw_ref[:, router_at:]))
        sig_count = sig * counts_ref[...].astype(F32)
        lane = lax.broadcasted_iota(jnp.int32, (rows, lanes), 1)
        picked = jnp.sum(jnp.where(lane == lanes - NEXP + info_ref[0], sig_count, 0.0), 1, keepdims=True)
        picked_total = jnp.sum(sig_count, 1, keepdims=True)
        weight = ROUTE_SCALE * picked / picked_total * valid_ref[...]

        @pl.when(step == 0)
        def _():
            sig_ref[...] = sig

        routed = ex_ref[...] > 0.0
        both = dot(mixed, gw_ref[...])
        gate = both[:, :hidden]
        lift = both[:, hidden:]
        d_hidden = dot_last(grad_ref[...], lw_ref[...])
        gate_sig = jax.nn.sigmoid(gate)
        gated = gate * gate_sig
        act = gated * lift
        wide = jnp.where(routed, weight, 1.0)
        hid = (act * wide).astype(LOW)
        hid_ref[...] = hid
        dw_ref[...] = jnp.sum(jnp.where(routed, act * d_hidden, 0.0), 1, keepdims=True)
        d_hidden = d_hidden * wide
        d_gate = (d_hidden * lift * gate_sig * (1.0 + gate * (1.0 - gate_sig))).astype(LOW)
        d_lift = (d_hidden * gated).astype(LOW)
        d_both = jnp.concatenate([d_gate, d_lift], 1)
        dg_ref[...] = d_both
        d_mixed = dot_last(d_both, gw_ref[...]).astype(LOW)
        out = dot(hid, lw_ref[...]).astype(LOW)

        @pl.when(step < middle)
        def _():
            dm_first[...] = d_mixed
            out_first[...] = out

        @pl.when(step >= middle)
        def _():
            dm_second[...] = d_mixed
            out_second[...] = out

    def tok(cols):
        return pl.BlockSpec((rows, cols), lambda b, info_ref: (b, 0))

    low_half = pl.BlockSpec((rows, model), lambda b, info_ref: (jnp.minimum(b, middle - 1), 0))
    high_half = pl.BlockSpec((rows, model), lambda b, info_ref: (jnp.maximum(b - middle, 0), 0))
    part = jax.ShapeDtypeStruct((total // 2, model), LOW)
    return pl.pallas_call(
        kernel,
        grid_spec=pltpu.PrefetchScalarGridSpec(
            num_scalar_prefetch=1,
            grid=(count,),
            in_specs=[whole(a) for a in blocks]
            + [tok(model), tok(lanes), tok(1)]
            + [whole(a) for a in (small_w, gate_w, lower_w, is_expert)],
            out_specs=[tok(model), tok(hidden), tok(2 * hidden)]
            + [low_half, high_half, low_half, high_half, tok(1)]
            + [pl.BlockSpec((rows, lanes), lambda b, info_ref: (0, 0))],
            scratch_shapes=[pltpu.VMEM((rows, model), LOW)],
        ),
        out_shape=[jax.ShapeDtypeStruct((total, model), LOW)]
        + [jax.ShapeDtypeStruct((total, w), LOW) for w in (hidden, 2 * hidden)]
        + [part] * 4
        + [jax.ShapeDtypeStruct((total, 1), F32), jax.ShapeDtypeStruct((rows, lanes), F32)],
        cost_estimate=cost(total * model * 12),
    )(info, *blocks, grad, counts, valid, small_w, gate_w, lower_w, is_expert)


def cost(size):
    return pl.CostEstimate(flops=0, bytes_accessed=size // 8, transcendentals=0)


def arrivals(steps, here, count):
    found = []
    for index, step in enumerate(steps):
        if step == "last":
            found.append((index, here == 0, count - 1))
            found.append((index, here == count - 1, 0))
        elif step == "above":
            found.append((index, here < count - 1, here + 1))
        elif step == "below":
            found.append((index, here > 0, here - 1))
        else:
            found.append((index, None, lax.rem(here + step, count)))
    return found


def each_arrival(steps, here, count, act):
    for index, condition, place in arrivals(steps, here, count):
        if condition is None:
            act(index, place)
        else:
            pl.when(condition)(functools.partial(act, index, place))


def scalars(*values):
    return jnp.stack([v.astype(jnp.int32) for v in values])


def shard_place(count, own, came, shard, start, size):
    steps = [k for k, _ in came]
    width = own.shape[1]
    tile = size
    while tile > 128 and tile % 2 == 0 and start % (tile // 2) == 0:
        tile //= 2

    def kernel(at_ref, own_ref, *refs):
        out = refs[-1]
        here = at_ref[0]
        out[here] = own_ref[...]

        def act(index, place):
            out[place] = refs[index][...]

        each_arrival(steps, here, count, act)

    return pl.pallas_call(
        kernel,
        grid_spec=pltpu.PrefetchScalarGridSpec(
            num_scalar_prefetch=1,
            grid=(size // tile,),
            in_specs=[pl.BlockSpec((tile, width), lambda b, at_ref: (b + start // tile, 0))]
            * (len(came) + 1),
            out_specs=pl.BlockSpec((count, tile, width), lambda b, at_ref: (0, b, 0)),
        ),
        out_shape=jax.ShapeDtypeStruct((count, size, width), LOW),
        cost_estimate=cost(4 * count * size * width),
    )(scalars(shard), own, *[piece for _, piece in came])


def strip_place(local, pieces, steps, shard, devices, start, tile):
    count = max(steps) + 1
    reps = len(pieces)
    rows, width = local.shape
    strip = pieces[0].shape[0] // len(steps)

    def kernel(at_ref, own_ref, *refs):
        out = refs[-1]
        here = at_ref[0]
        out[here] = own_ref[...]
        for j in range(reps):
            base = pl.multiple_of(at_ref[1 + j] * strip, strip)

            def act(index, place):
                out[place, pl.ds(base, strip)] = refs[j][index * strip : (index + 1) * strip]

            each_arrival(steps, here, count, act)

    return pl.pallas_call(
        kernel,
        grid_spec=pltpu.PrefetchScalarGridSpec(
            num_scalar_prefetch=1,
            grid=(width // tile,),
            in_specs=[pl.BlockSpec((rows, tile), lambda b, at_ref: (0, b))]
            + [
                pl.BlockSpec((pieces[0].shape[0], tile), lambda b, at_ref: (0, b + start // tile))
                for _ in pieces
            ],
            out_specs=pl.BlockSpec((count, rows, tile), lambda b, at_ref: (0, 0, b)),
        ),
        out_shape=jax.ShapeDtypeStruct((count, rows, width), LOW),
        cost_estimate=cost(4 * count * rows * width),
    )(jnp.concatenate([scalars(shard), devices]), local, *pieces).reshape(count * rows, width)


def merge_rows(blocks, act, extra, widths):
    rows = blocks[0].shape[0]
    count = len(blocks)
    outs = len(widths)

    def kernel(*refs):
        index = pl.program_id(0)
        more = [r[...] for r in refs[count:-outs]]
        for k in range(count):

            @pl.when(index == k)
            def _():
                for ref, value in zip(refs[-outs:], act(refs[k][...], *more)):
                    ref[...] = value

    return pl.pallas_call(
        kernel,
        grid=(count,),
        in_specs=[
            pl.BlockSpec(a.shape, lambda b: (0, 0), pipeline_mode=pl.Buffered(1)) for a in blocks
        ]
        + [pl.BlockSpec((rows, a.shape[1]), lambda b: (b, 0)) for a in extra],
        out_specs=[pl.BlockSpec((rows, w), lambda b: (b, 0)) for w in widths],
        out_shape=[jax.ShapeDtypeStruct((count * rows, w), LOW) for w in widths],
        cost_estimate=cost(count * rows * sum(widths) * 4),
    )(*blocks, *extra)


def assemble(blocks, devices, grid, block_shape, block_map, outs, place):
    reps = len(blocks)

    def kernel(dev_ref, *refs):
        held = refs[-1]
        for k in range(reps):
            held[dev_ref[k]] = refs[k][...].astype(F32)
        for j in range(reps):
            place(pl.program_id(0), j, held[j], refs[reps:-1])

    return pl.pallas_call(
        kernel,
        grid_spec=pltpu.PrefetchScalarGridSpec(
            num_scalar_prefetch=1,
            grid=(grid,),
            in_specs=[pl.BlockSpec(block_shape, lambda b, dev_ref: block_map(b)) for _ in blocks],
            out_specs=[
                pl.BlockSpec(shape, functools.partial(lambda m, b, dev_ref: m(b), where))
                for _, shape, where in outs
            ],
            scratch_shapes=[pltpu.VMEM((reps,) + block_shape, F32)],
        ),
        out_shape=[jax.ShapeDtypeStruct(shape, F32) for shape, _, _ in outs],
        cost_estimate=cost(reps * blocks[0].size * 6),
    )(devices, *blocks)


def layouts(lengths, seq_owner, devices, rows):
    count = lengths.shape[0]
    mine = seq_owner[None, :] == devices[:, None]
    own_length = jnp.where(mine, lengths[None, :], 0)
    numbers = jnp.arange(count, dtype=jnp.int32)
    ahead = numbers[:, None] < numbers[None, :]
    starts = jnp.sum(jnp.where(ahead[None], own_length[:, :, None], 0), 1)[:, None, :]
    ends = starts + own_length[:, None, :]
    row = jnp.arange(rows, dtype=jnp.int32)[None, :, None]
    inside = mine[:, None, :] & (row >= starts) & (row < ends)
    valid = jnp.any(inside, 2, keepdims=True)
    segment = jnp.sum(jnp.where(inside, numbers, 0), 2, keepdims=True)
    position = row - jnp.sum(jnp.where(inside, starts, 0), 2, keepdims=True)
    return jnp.where(valid, segment, count), position, valid


def make_local(reps, shards):
    group = Group(reps, shards)
    heads = HEADS // reps
    half = 32 * heads
    width = 2 * half

    def local(
        tokens,
        cotangent,
        lengths,
        seq_owner,
        expert_ids,
        attention_gain,
        query_weight,
        latent_down,
        latent_gain,
        latent_up,
        output_weight,
        feedforward_gain,
        router_weight,
        shared_gate,
        shared_up,
        shared_down,
        expert_gate,
        expert_up,
        expert_down,
    ):
        rows, model = tokens.shape
        rep = lax.axis_index("rep")
        shard = lax.axis_index("shard")
        devices = group.devices(rep)
        slab = model // shards
        strip = slab // reps
        lat = latent_gain.shape[0]
        cut = group.half * rows

        x_gather = Gathering(group, tokens)
        x_gather.start()
        small = jnp.concatenate(
            [
                lax.dynamic_slice_in_dim(latent_down, rep * strip, strip, 0),
                lax.dynamic_slice_in_dim(router_weight, rep * strip, strip, 0),
            ],
            1,
        )
        small = lax.all_gather(small, ("shard", "rep"), axis=0, tiled=True)
        output_shift = Shifting(
            group, lax.dynamic_slice_in_dim(output_weight, rep * strip, strip, 0)
        )
        output_shift.start()

        query_cols = heads * (NOPE + ROPE)
        up_cols = heads * (NOPE + VDIM)
        query_wide = round_up(query_cols, 128)
        query_part = lax.dynamic_slice_in_dim(query_weight, rep * query_cols, query_cols, 1)
        if query_wide > query_cols:
            query_part = jnp.pad(query_part, ((0, 0), (0, query_wide - query_cols)))
        up_part = lax.dynamic_slice_in_dim(latent_up, rep * up_cols, up_cols, 1)
        up_part = fold(up_part, slab)
        gain_rows = jnp.concatenate([attention_gain, feedforward_gain, latent_gain])
        gain_lanes = query_wide + 128
        gain_count = round_up(gain_rows.shape[0], 16 * gain_lanes)
        gain_rows = jnp.pad(gain_rows, (0, gain_count - gain_rows.shape[0])).reshape(-1, gain_lanes)
        query_part = jnp.concatenate(
            [jnp.concatenate([query_part, up_part], 1), gain_rows], 0
        )
        query_shift = Shifting(group, query_part)
        query_shift.start()

        part_s = shared_down.shape[0] // reps
        local_e = expert_down.shape[1]
        part_e = WINDOW * local_e // reps
        per = reps // WINDOW
        my_expert = rep // per
        used = part_s + part_e
        hidden = round_up(shards * used, 128)
        unit = hidden // shards
        place = jnp.arange(hidden, dtype=jnp.int32)
        within = place % unit
        is_shared = within < part_s
        is_expert = (within >= part_s) & (within < used)
        from_shared = jnp.where(
            is_shared, (place // unit) * shared_down.shape[0] + rep * part_s + within, -1
        )
        from_expert = jnp.where(
            is_expert, (place // unit) * local_e + (rep % per) * part_e + within - part_s, -1
        )
        pick_s = (
            jnp.arange(shared_gate.shape[1], dtype=jnp.int32)[:, None] == from_shared[None, :]
        ).astype(LOW)
        pick_e = (
            jnp.arange(expert_gate.shape[2], dtype=jnp.int32)[:, None] == from_expert[None, :]
        ).astype(LOW)

        def my_columns(shared, expert):
            expert = lax.dynamic_index_in_dim(expert, my_expert, 0, keepdims=False)
            return (dot(shared, pick_s) + dot(expert, pick_e)).astype(LOW)

        gate_all = jnp.concatenate(
            [my_columns(shared_gate, expert_gate), my_columns(shared_up, expert_up)], 1
        )
        lower_part = jnp.concatenate(
            [
                lax.dynamic_slice_in_dim(shared_down, rep * part_s, part_s, 0),
                lax.dynamic_slice(
                    expert_down, (my_expert, (rep % per) * part_e, 0), (1, part_e, model)
                )[0],
                jnp.zeros((unit - used, model), LOW),
            ],
            0,
        )

        segment, position, valid = layouts(lengths, seq_owner, devices * shards + shard, rows)
        total_rows = reps * rows
        seg_col = segment.reshape(total_rows, 1)
        seg_row = segment.reshape(reps, 1, rows)
        valid_all = valid.reshape(total_rows, 1).astype(F32)
        valid_own = valid_all[:rows]
        frequency = jnp.power(ROPE_BASE, -2.0 * jnp.arange(32, dtype=F32) / ROPE)
        angles = position.reshape(total_rows, 1).astype(F32) * jnp.tile(frequency, 2 * heads)[None]
        cosine = jnp.cos(angles)
        side = jnp.where(jnp.arange(width) < half, -1.0, 1.0).astype(F32)
        sine = jnp.sin(angles) * side[None, :]

        hidden_in = tokens.astype(F32)
        counts = jnp.sum(
            (expert_ids[:, :, None] == jnp.arange(NEXP, dtype=jnp.int32)).astype(F32), 1
        )
        given = jnp.concatenate(
            [cotangent, jnp.zeros((rows, 128 - NEXP), LOW), counts.astype(LOW)], 1
        )

        phase(x_gather, query_shift, output_shift)
        x_gather.start()
        query_shift.start()
        output_shift.start()
        (gate_all,) = phase(x_gather, query_shift, output_shift, gate_all)
        gate_all = lax.all_gather(gate_all, "shard", axis=0, tiled=True)
        x_gather.start()
        output_came = output_shift.whole(shard)
        shard_steps = [k for k, _ in output_came]
        output_gather = Gathering(group, jnp.concatenate([piece for _, piece in output_came], 0))
        output_gather.start()
        query_up = shard_place(shards, query_part, query_shift.result(), shard, 0, slab)
        gains = shard_place(
            shards, query_part, query_shift.result(), shard, slab, gain_rows.shape[0]
        )
        gains = gains.reshape(shards, -1).astype(F32)
        attention_gain_all = gains[:, :slab].reshape(1, model)
        mixer_gain_all = gains[:, slab : 2 * slab].reshape(1, model)
        latent_gain_all = gains[:, 2 * slab : 2 * slab + lat].reshape(1, RANK)

        lane = jnp.arange(heads * width, dtype=jnp.int32)
        head = lane // width
        spot = lane % width
        source = jnp.where(
            (spot % half) // 32 == head, (spot // half) * 32 + spot % 32, -1
        )
        spread = (jnp.arange(ROPE, dtype=jnp.int32)[:, None] == source[None, :]).astype(LOW)
        cols = heads * VDIM
        normed_all, qn, qr, keyval, kr, latent_low, up_all, latent_own, attended = attend_forward(
            devices,
            x_gather.list(),
            attention_gain_all,
            latent_gain_all,
            query_up,
            heads,
            small,
            spread,
            cosine,
            sine,
            seg_col,
            seg_row,
        )
        attended, given, lower_part = phase(attended, output_gather, given, lower_part)
        output_gather.start()
        lower_all = lax.all_gather(lower_part, "shard", axis=0, tiled=True)
        attended_own = lax.all_to_all(
            attended.reshape(reps, rows, cols), "rep", 0, 0, tiled=True
        )
        (attended_own,) = phase(attended_own, output_gather)
        output_gather.start()
        given_gather = Gathering(group, given)
        given_gather.start()
        output_all = strip_place(
            output_weight, output_gather.list(), shard_steps, shard, devices, 0, 256
        )
        attended_own = jnp.transpose(attended_own, (1, 0, 2)).reshape(rows, HEADS * VDIM)
        mid = hidden_in + dot(attended_own, output_all)
        mixed_scale = rms_scale(mid)
        mixed = (mid * mixed_scale * mixer_gain_all).astype(LOW)

        mixed_gather = Gathering(group, mixed)
        mixed_gather.start()
        (gate_all,) = phase(mixed_gather, given_gather, gate_all)
        mixed_gather.start()
        given_gather.start()
        phase(mixed_gather, given_gather)
        mixed_gather.start()
        given_gather.start()
        grad_all, counts_all = merge_rows(
            given_gather.list(),
            lambda block, ok: (
                (block[:, :model].astype(F32) * ok).astype(LOW),
                block[:, model:],
            ),
            [valid_all],
            [model, 128],
        )
        grad_all, counts_all = phase(mixed_gather, grad_all, counts_all)
        (
            mixed_all,
            hidden_low,
            d_both,
            d_mixed_first,
            d_mixed_second,
            ffn_first,
            ffn_second,
            d_weight,
            sig_own,
        ) = experts(
            jnp.reshape(my_expert, (1,)).astype(jnp.int32),
            mixed_gather.list(),
            grad_all,
            counts_all,
            valid_all,
            small,
            gate_all,
            lower_all,
            is_expert.astype(F32)[None, :],
        )
        sig_own = sig_own[:, -NEXP:]
        numbers = jnp.arange(reps, dtype=jnp.int32)
        by_device = jnp.sum(
            jnp.where(
                (devices[None, :] == numbers[:, None])[:, :, None],
                d_weight.reshape(1, reps, rows),
                0.0,
            ),
            1,
        )
        d_weight_own = lax.all_to_all(by_device, "rep", 0, 0, tiled=True)
        d_weight_own = jnp.sum(d_weight_own.reshape(WINDOW, per, rows), 1)
        mixed_sum = Reducing(group, d_mixed_second, d_mixed_first)
        mixed_sum.start()
        mixed_all, d_both, hidden_low, ffn_second = phase(
            mixed_sum, mixed_all, d_both, hidden_low, ffn_second
        )
        mixed_sum.start()
        ffn_sum = Reducing(group, ffn_second, ffn_first)
        ffn_sum.start()
        both_grad = dot_rows(mixed_all, d_both).astype(LOW)
        _, hidden_low, d_weight_own = phase(
            mixed_sum, ffn_sum, both_grad, hidden_low, d_weight_own
        )
        both_grad = lax.psum_scatter(both_grad, "shard", scatter_dimension=0, tiled=True)
        mixed_sum.start()
        lower_grad = dot_rows(hidden_low, grad_all).astype(LOW)
        phase(mixed_sum, lower_grad)
        lower_grad = lax.psum_scatter(lower_grad, "shard", scatter_dimension=0, tiled=True)[:used]
        d_mixed = mixed_sum.total()

        total_own = jnp.sum(sig_own * counts, 1, keepdims=True)
        hit = counts[:, :WINDOW]
        d_route = jnp.concatenate(
            [valid_own * d_weight_own.T * hit, jnp.zeros((rows, NEXP - WINDOW), F32)], 1
        )
        inner = jnp.sum(d_route * sig_own, 1, keepdims=True)
        d_sig = ROUTE_SCALE * (d_route / total_own - counts * inner / (total_own * total_own))
        d_logits = (d_sig * sig_own * (1.0 - sig_own)).astype(LOW)
        d_mixed = d_mixed + dot_last(d_logits, small[:, RANK + ROPE :])
        grad_own = cotangent.astype(F32) * valid_own
        d_mid = grad_own + rms_back(mid, mixed_scale, mixer_gain_all, d_mixed)
        d_branch = d_mid.astype(LOW)

        out_cols = model // reps

        def output_part(index):
            picked = [
                lax.dynamic_slice_in_dim(d_branch, devices[k] * out_cols, out_cols, 1)
                for k in index
            ]
            return dot_rows(attended_own, jnp.concatenate(picked, 1)).astype(LOW)

        output_sum = Reducing(
            group,
            output_part(range(group.half, reps)),
            output_part(range(group.half)),
            axis=1,
        )
        output_sum.start()

        d_attended = dot_last(d_branch, output_all).astype(LOW)
        d_attended = jnp.transpose(d_attended.reshape(rows, reps, cols), (1, 0, 2))
        d_attended = lax.all_to_all(d_attended, "rep", 0, 0, tiled=True)
        (d_attended,) = phase(d_attended, output_sum)
        output_sum.start()
        ffn_sum.start()
        d_attended = d_attended.reshape(total_rows, cols)
        (
            d_normed_first,
            d_normed_second,
            latent_first,
            latent_second,
            attention_grad,
        ) = attend_backward(
            devices,
            (qn, qr, keyval, kr),
            d_attended,
            normed_all,
            latent_low,
            query_up,
            up_all,
            cosine,
            sine,
            seg_col,
            seg_row,
            rows,
        )
        latent_second, d_normed_second = phase(
            latent_second, d_normed_second, output_sum, ffn_sum
        )
        attention_grad = lax.psum_scatter(
            attention_grad, "shard", scatter_dimension=0, tiled=True
        ).reshape(slab, query_wide + 128)
        latent_sum = Reducing(group, latent_second, latent_first)
        latent_sum.start()
        normed_sum = Reducing(group, d_normed_second, d_normed_first)
        normed_sum.start()
        output_sum.start()
        ffn_sum.start()
        phase(latent_sum, normed_sum, output_sum)
        latent_sum.start()
        normed_sum.start()
        output_grad = lax.psum_scatter(
            output_sum.total().astype(LOW), "shard", scatter_dimension=0, tiled=True
        )
        phase(latent_sum)
        latent_sum.start()
        (both_grad,) = phase(latent_sum, normed_sum, both_grad, ffn_sum)
        layer_out = (valid_own * (mid + ffn_sum.total())).astype(LOW)
        normed_sum.start()
        both_gather = Gathering(group, both_grad)
        both_gather.start()
        d_latent_sum = latent_sum.total()
        compressed = latent_own[:, :RANK]
        d_compressed = rms_back(
            compressed, rms_scale(compressed), latent_gain_all, d_latent_sum[:, :RANK]
        )
        kg_first = d_latent_sum[:, RANK : RANK + 32]
        kg_second = d_latent_sum[:, RANK + 32 :]
        cos_own = cosine[:rows, :32]
        sin_own = sine[:rows, half : half + 32]
        d_latent = jnp.concatenate(
            [
                d_compressed,
                kg_first * cos_own + kg_second * sin_own,
                kg_second * cos_own - kg_first * sin_own,
            ],
            1,
        ).astype(LOW)
        row_gather = Gathering(group, jnp.concatenate([d_latent, d_logits], 1))
        row_gather.start()
        (lower_grad,) = phase(row_gather, normed_sum, lower_grad)
        row_gather.start()
        d_normed = normed_sum.total() + dot_last(d_latent, small[:, : RANK + ROPE])
        token_grad = d_mid + rms_back(
            hidden_in, rms_scale(hidden_in), attention_gain_all, d_normed
        )

        phase(row_gather)
        row_gather.start()
        (attention_grad,) = phase(row_gather, attention_grad)
        (row_grads,) = merge_rows(
            row_gather.list(),
            lambda block: (block,),
            [],
            [RANK + ROPE + NEXP],
        )

        def my_strip(values):
            return jnp.concatenate(
                [
                    lax.dynamic_slice_in_dim(values, s * slab + rep * strip, strip, 1)
                    for s in range(shards)
                ],
                1,
            )

        strip_grad = jnp.concatenate(
            [
                dot_rows(my_strip(normed_all), row_grads[:, : RANK + ROPE]),
                dot_rows(my_strip(mixed_all), row_grads[:, RANK + ROPE :]),
            ],
            1,
        ).astype(LOW)

        strip_sum = lax.psum_scatter(strip_grad, "shard", scatter_dimension=0, tiled=True)
        _, output_grad = phase(both_gather, strip_grad, output_grad)
        both_gather.start()
        phase(both_gather)
        both_gather.start()
        lower_gather = Gathering(group, lower_grad)
        lower_gather.start()
        phase(both_gather, lower_gather)
        lower_gather.start()

        tile = min(slab, 64)

        def place_columns(step, j, block, refs):
            for side in (0, 1):
                for s in range(shards):
                    base = side * hidden + s * unit
                    at = s * part_s * reps + j * part_s
                    refs[2 * side][:, at : at + part_s] = block[:, base : base + part_s]
                    at = s * part_e * per + (j % per) * part_e
                    refs[2 * side + 1][j // per, :, at : at + part_e] = block[
                        :, base + part_s : base + used
                    ]

        wide_s = shared_gate.shape
        wide_e = expert_gate.shape
        sgate_grad, egate_grad, sup_grad, eup_grad = assemble(
            both_gather.list(),
            devices,
            slab // tile,
            (tile, 2 * hidden),
            lambda b: (b, 0),
            [
                (wide_s, (tile, wide_s[1]), lambda b: (b, 0)),
                (wide_e, (WINDOW, tile, wide_e[2]), lambda b: (0, b, 0)),
            ]
            * 2,
            place_columns,
        )

        def place_rows(step, j, block, refs):
            refs[0][j * part_s : (j + 1) * part_s] = block[:part_s]
            at = (j % per) * part_e
            refs[1][j // per, at : at + part_e] = block[part_s:]

        phase(lower_gather, sgate_grad)
        lower_gather.start()
        query_gather = Gathering(group, attention_grad)
        query_gather.start()
        phase(lower_gather, query_gather)
        query_gather.start()
        lane_tile = 256
        sdown_grad, edown_grad = assemble(
            lower_gather.list(),
            devices,
            model // lane_tile,
            (used, lane_tile),
            lambda b: (0, b),
            [
                (shared_down.shape, (shared_down.shape[0], lane_tile), lambda b: (0, b)),
                (expert_down.shape, (WINDOW, local_e, lane_tile), lambda b: (0, 0, b)),
            ],
            place_rows,
        )

        phase(query_gather, sdown_grad)
        query_gather.start()
        output_gather = Gathering(group, output_grad)
        output_gather.start()
        (strip_sum,) = phase(query_gather, output_gather, strip_sum)
        output_gather.start()
        strip_gather = Gathering(group, strip_sum)
        strip_gather.start()

        def place_attention(step, j, block, refs):
            refs[0][:, j * query_cols : (j + 1) * query_cols] = block[:, :query_cols]

            @pl.when(step < up_cols // 128)
            def _():
                at = pl.multiple_of(j * up_cols + step * 128, 128)
                refs[1][:, pl.ds(at, 128)] = block[:, query_wide:]

        query_grad, up_grad = assemble(
            query_gather.list(),
            devices,
            slab // lat,
            (lat, query_wide + 128),
            lambda b: (b, 0),
            [
                (query_weight.shape, (lat, query_weight.shape[1]), lambda b: (b, 0)),
                (latent_up.shape, latent_up.shape, lambda b: (0, 0)),
            ],
            place_attention,
        )

        def place_output(step, j, block, refs):
            refs[0][:, j * out_cols : (j + 1) * out_cols] = block

        phase(output_gather, strip_gather, query_grad)
        output_gather.start()
        strip_gather.start()
        phase(output_gather, strip_gather)
        strip_gather.start()
        (output_grad,) = assemble(
            output_gather.list(),
            devices,
            slab // lat,
            (lat, out_cols),
            lambda b: (b, 0),
            [(output_weight.shape, (lat, model), lambda b: (b, 0))],
            place_output,
        )

        def place_strip(step, j, block, refs):
            refs[0][j * strip : (j + 1) * strip] = block[:, : RANK + ROPE]
            refs[1][j * strip : (j + 1) * strip] = block[:, RANK + ROPE :]

        down_grad, router_grad = assemble(
            strip_gather.list(),
            devices,
            1,
            (strip, RANK + ROPE + NEXP),
            lambda b: (0, 0),
            [
                (latent_down.shape, latent_down.shape, lambda b: (0, 0)),
                (router_weight.shape, router_weight.shape, lambda b: (0, 0)),
            ],
            place_strip,
        )

        def row_sum(weight, grad):
            return jnp.sum(weight.astype(F32) * grad, -1)

        attention_gain_grad = (
            row_sum(query_weight, query_grad) + row_sum(latent_down, down_grad)
        ) / attention_gain.astype(F32)
        latent_gain_grad = row_sum(latent_up, up_grad) / latent_gain.astype(F32)
        mixer_gain_grad = (
            row_sum(router_weight, router_grad)
            + row_sum(shared_gate, sgate_grad)
            + row_sum(shared_up, sup_grad)
            + jnp.sum(row_sum(expert_gate, egate_grad) + row_sum(expert_up, eup_grad), 0)
        ) / feedforward_gain.astype(F32)

        return (
            layer_out,
            token_grad,
            attention_gain_grad,
            query_grad,
            down_grad,
            latent_gain_grad,
            up_grad,
            output_grad,
            mixer_gain_grad,
            router_grad,
            sgate_grad,
            sup_grad,
            sdown_grad,
            egate_grad,
            eup_grad,
            edown_grad,
        )

    return local


def fold(value, rows):
    count = value.shape[1] // 128
    parts = [value[:, i * 128 : (i + 1) * 128] for i in range(count)]
    left = rows - count * value.shape[0]
    if left:
        parts.append(jnp.zeros((left, 128), value.dtype))
    return jnp.concatenate(parts, 0)


def solution(mesh):
    tokens = P(("rep", "shard"), None)
    vector = P("shard")
    matrix = P("shard", None)
    stack = P(None, "shard", None)
    in_specs = (
        (tokens, tokens, P(), P(), tokens, vector, matrix, matrix, vector, matrix, matrix, vector)
        + (matrix,) * 4
        + (stack,) * 3
    )
    out_specs = (
        (tokens, tokens, vector, matrix, matrix, vector, matrix, matrix, vector)
        + (matrix,) * 4
        + (stack,) * 3
    )
    local = make_local(mesh.shape["rep"], mesh.shape["shard"])
    return jax.shard_map(local, mesh=mesh, in_specs=in_specs, out_specs=out_specs, check_vma=False)
```

```python
import functools

import jax
import jax.numpy as jnp
from jax import lax
from jax.experimental import pallas as pl
from jax.experimental.pallas import tpu as pltpu
from jax.sharding import PartitionSpec as P

HEADS = 16
NOPE = 128
ROPE = 64
VDIM = 128
RANK = 512
NEXP = 64
WINDOW = 2

EPSILON = 1e-06
ROPE_BASE = 50000.0
ROUTE_SCALE = 2.446
NEG_FILL = -1e30
SCORE_SCALE = (NOPE + ROPE) ** (-0.5)

F32 = jnp.float32
LOW = jnp.bfloat16


def dot(left, right):
    return jnp.dot(left, right, preferred_element_type=F32)


def dot_rows(left, right):
    return lax.dot_general(left, right, (((0,), (0,)), ((), ())), preferred_element_type=F32)


def dot_last(left, right):
    return lax.dot_general(left, right, (((1,), (1,)), ((), ())), preferred_element_type=F32)


def rms_scale(values):
    return lax.rsqrt(jnp.mean(values * values, -1, keepdims=True) + EPSILON)


def rms_back(values, scale, gain, upstream):
    gained = upstream * gain
    inner = jnp.mean(values * gained, -1, keepdims=True)
    return scale * gained - values * scale * scale * scale * inner


def round_up(value, unit):
    return -(-value // unit) * unit


class Group:
    def __init__(self, reps, shards):
        self.reps = reps
        self.shards = shards
        bits = reps.bit_length() - 1
        assert bits >= 1 and 1 << bits == reps
        self.levels = [(1 << b, 1 << (bits - b)) for b in range(1, bits)]
        self.half = reps // 2

    def devices(self, rep):
        lists = []
        for side in (0, 1):
            masks = [0]
            for level in self.levels:
                masks = masks + [m ^ level[side] for m in masks]
            lists.append(masks)
        first = lists[0] + [m ^ 1 for m in lists[1]]
        second = lists[1] + [m ^ 1 for m in lists[0]]
        masks = jnp.where(
            rep % 2 == 0, jnp.array(first, jnp.int32), jnp.array(second, jnp.int32)
        )
        return rep.astype(jnp.int32) ^ masks

    def cross(self, value, level):
        pairs = [(i, i ^ level[i & 1]) for i in range(self.reps)]
        return lax.ppermute(value, "rep", pairs)


class Gathering:
    def __init__(self, group, block):
        self.group = group
        self.blocks = {0: block}
        self.stage = 0
        self.pending = {}

    def start(self):
        group = self.group
        self.stage += 1
        if self.stage <= len(group.levels):
            for k in range(group.half):
                if bin(k).count("1") == self.stage:
                    top = k.bit_length() - 1
                    self.pending[k] = group.cross(self.blocks[k ^ (1 << top)], group.levels[top])
        elif self.stage == len(group.levels) + 1:
            for k in range(group.half):
                self.pending[group.half + k] = group.cross(self.blocks[k], (1, 1))

    def settle(self, values):
        self.blocks.update(zip(self.pending, values))
        self.pending = {}

    def list(self):
        while True:
            self.settle(list(self.pending.values()))
            if len(self.blocks) == self.group.reps:
                return [self.blocks[k] for k in range(self.group.reps)]
            self.start()


class Reducing:
    def __init__(self, group, second, first, axis=0):
        self.group = group
        self.second = second
        self.terms = [first]
        self.axis = axis
        self.size = first.shape[axis]
        self.stage = 0
        self.pending = {}

    def cut(self, start, size):
        total = None
        for term in self.terms:
            term = lax.slice_in_dim(term, start, start + size, axis=self.axis).astype(F32)
            total = term if total is None else total + term
        return total

    def start(self):
        levels = self.group.levels
        if self.stage == 0:
            self.pending[0] = self.group.cross(self.second, (1, 1))
        elif self.stage <= len(levels):
            self.size //= 2
            sent = self.cut(self.size, self.size).astype(LOW)
            self.sent = sent
            self.pending[0] = self.group.cross(sent, levels[len(levels) - self.stage])
        self.stage += 1

    def settle(self, values):
        self.terms += values
        self.pending = {}

    def total(self):
        while True:
            self.settle(list(self.pending.values()))
            if self.stage > len(self.group.levels):
                return self.cut(0, self.size)
            self.start()


class Shifting:
    def __init__(self, group, block):
        self.count = group.shards
        self.block = block
        self.found = {}
        self.stage = 0
        self.pending = {}

    def start(self):
        count = self.count
        self.stage += 1

        def cycle(step):
            return [((i + step) % count, i) for i in range(count)]

        def move(value, pairs):
            return lax.ppermute(value, "shard", pairs)

        if count != 4:
            if self.stage == 1:
                self.pending = {k: move(self.block, cycle(k)) for k in range(1, count)}
        elif self.stage == 1:
            self.pending = {
                2: move(self.block, cycle(2)),
                "above": move(self.block, cycle(1)[:-1]),
                "below": move(self.block, cycle(3)[1:]),
            }
        elif self.stage == 2:
            self.pending = {"last": move(self.found[2], [(1, 0), (2, 3)])}

    def settle(self, values):
        self.found.update(zip(self.pending, values))
        self.pending = {}

    def result(self):
        self.settle(list(self.pending.values()))
        while self.stage < 2:
            self.start()
            self.settle(list(self.pending.values()))
        return list(self.found.items())

    def whole(self, position):
        found = dict(self.result())
        if self.count == 4:
            last = found.pop("last")
            found[1] = jnp.where(position == self.count - 1, last, found.pop("above"))
            found[3] = jnp.where(position == 0, last, found.pop("below"))
        return [(k, found[k]) for k in range(1, self.count)]


def phase(*items):
    values = []
    for item in items:
        values += list(item.pending.values()) if hasattr(item, "pending") else [item]
    values = list(lax.optimization_barrier(tuple(values)))
    arrays = []
    for item in items:
        if hasattr(item, "pending"):
            count = len(item.pending)
            item.settle(values[:count])
            values = values[count:]
        else:
            arrays.append(values.pop(0))
    return arrays


def head_probs(h, allowed, q_nope, q_rope, keyval, k_rope):
    width = q_rope.shape[1]
    base = h * (NOPE + VDIM)
    scores = dot_last(q_nope[:, h * NOPE : (h + 1) * NOPE], keyval[:, base : base + NOPE])
    scores = scores + dot_last(q_rope, k_rope[:, h * width : (h + 1) * width])
    scores = jnp.where(allowed, scores * SCORE_SCALE, NEG_FILL)
    unnormed = jnp.exp(scores - jnp.max(scores, -1, keepdims=True))
    return unnormed / jnp.sum(unnormed, -1, keepdims=True)


def same_segment(sc_ref, sr_ref):
    rows = sc_ref.shape[0]
    t = lax.broadcasted_iota(jnp.int32, (rows, rows), 0)
    u = lax.broadcasted_iota(jnp.int32, (rows, rows), 1)
    return (sc_ref[...] == sr_ref[0]) & (u <= t)


def turned(values):
    half = values.shape[1] // 2
    return jnp.concatenate([values[:, half:], values[:, :half]], 1)


def whole(a):
    return pl.BlockSpec(a.shape, lambda b, dev_ref: (0,) * a.ndim, pipeline_mode=pl.Buffered(1))


def attend_forward(
    devices, blocks, gain, latent_gain, query_up, heads, small_w, spread, cosine, sine, seg_col, seg_row
):
    count = len(blocks)
    rows, model = blocks[0].shape
    shards, slab, lanes = query_up.shape
    query_wide = lanes - 128
    lat = RANK // shards
    up_cols = heads * (NOPE + VDIM)
    half = 32 * heads
    width = 2 * half

    def kernel(dev_ref, *refs):
        parts = refs[:count]
        gain_ref, lgain_ref, qu_ref, sw_ref, spread_ref, cos_ref, sin_ref, sc_ref, sr_ref = (
            refs[count : count + 9]
        )
        normed_ref, qn_ref, qr_ref, kv_ref, kr_ref, low_ref, up_ref, own_ref, out_ref, held = refs[
            count + 9 :
        ]
        step = pl.program_id(0)
        for k in range(count):

            @pl.when(step == k)
            def _():
                held[...] = parts[k][...]

        @pl.when(step == 0)
        def _():
            for z in range(shards):
                for i in range(up_cols // 128):
                    up_ref[z * lat : (z + 1) * lat, i * 128 : (i + 1) * 128] = qu_ref[
                        z, i * lat : (i + 1) * lat, query_wide:
                    ]

        x = held[...].astype(F32)
        normed = (x * rms_scale(x) * gain_ref[...]).astype(LOW)
        normed_ref[...] = normed
        query = dot(normed, qu_ref[:, :, :query_wide].reshape(model, query_wide))
        at = [h * (NOPE + ROPE) for h in range(heads)]
        q_nope = jnp.concatenate([query[:, i : i + NOPE] for i in at], 1).astype(LOW)
        q_rope = jnp.concatenate(
            [query[:, i + NOPE + c : i + NOPE + c + 32] for c in (0, 32) for i in at], 1
        )
        cos = cos_ref[...]
        sin = sin_ref[...]
        q_rope = (q_rope * cos + turned(q_rope) * sin).astype(LOW)
        latent = dot(normed, sw_ref[...])

        @pl.when(step == 0)
        def _():
            own_ref[...] = latent

        compressed = latent[:, :RANK]
        low = (compressed * rms_scale(compressed) * lgain_ref[...]).astype(LOW)
        key = latent[:, RANK : RANK + ROPE]
        key = key * cos[:, :ROPE] + turned(key) * sin[:, half - 32 : half + 32]
        k_rope = dot(key.astype(LOW), spread_ref[...]).astype(LOW)
        keyval = dot(low, up_ref[...]).astype(LOW)
        qn_ref[...] = q_nope
        qr_ref[...] = q_rope
        kv_ref[...] = keyval
        kr_ref[...] = k_rope
        low_ref[...] = low
        allowed = same_segment(sc_ref, sr_ref)
        for h in range(heads):
            probs = head_probs(h, allowed, q_nope, q_rope, keyval, k_rope)
            base = h * (NOPE + VDIM) + NOPE
            out_ref[:, h * VDIM : (h + 1) * VDIM] = dot(
                probs.astype(LOW), keyval[:, base : base + VDIM]
            ).astype(LOW)

    def tok(cols):
        return pl.BlockSpec((rows, cols), lambda b, dev_ref: (b, 0))

    total = count * rows
    widths = [model, heads * NOPE, width, heads * (NOPE + VDIM), heads * width, RANK]
    return pl.pallas_call(
        kernel,
        grid_spec=pltpu.PrefetchScalarGridSpec(
            num_scalar_prefetch=1,
            grid=(count,),
            in_specs=[whole(a) for a in blocks]
            + [whole(a) for a in (gain, latent_gain, query_up, small_w, spread)]
            + [tok(width), tok(width), tok(1)]
            + [pl.BlockSpec((1, 1, rows), lambda b, dev_ref: (b, 0, 0))],
            out_specs=[tok(w) for w in widths]
            + [
                pl.BlockSpec((RANK, up_cols), lambda b, dev_ref: (0, 0)),
                pl.BlockSpec((rows, small_w.shape[1]), lambda b, dev_ref: (0, 0)),
            ]
            + [pl.BlockSpec((rows, heads * VDIM), lambda b, dev_ref: (dev_ref[b], 0))],
            scratch_shapes=[pltpu.VMEM((rows, model), LOW)],
        ),
        out_shape=[jax.ShapeDtypeStruct((total, w), LOW) for w in widths]
        + [
            jax.ShapeDtypeStruct((RANK, up_cols), LOW),
            jax.ShapeDtypeStruct((rows, small_w.shape[1]), F32),
        ]
        + [jax.ShapeDtypeStruct((total, heads * VDIM), LOW)],
        cost_estimate=cost(total * model * 6),
    )(devices, *blocks, gain, latent_gain, query_up, small_w, spread, cosine, sine, seg_col, seg_row)


def attend_backward(
    devices, kept, given, normed, low, query_up, up_w, cosine, sine, seg_col, seg_row, rows
):
    q_nope, q_rope, keyval, k_rope = kept
    total, model = normed.shape
    count = total // rows
    heads = up_w.shape[1] // (NOPE + VDIM)
    half = 32 * heads
    width = 2 * half
    nope = heads * NOPE
    middle = count // 2
    shards, slab, lanes = query_up.shape
    query_wide = lanes - 128
    lat = RANK // shards
    up_cols = up_w.shape[1]
    wide = RANK + round_up(ROPE, 128)

    def kernel(
        dev_ref,
        qn_ref,
        qr_ref,
        kv_ref,
        kr_ref,
        da_ref,
        n_ref,
        low_ref,
        qu_ref,
        uw_ref,
        cos_ref,
        sin_ref,
        sc_ref,
        sr_ref,
        first_ref,
        second_ref,
        lat_first_ref,
        lat_second_ref,
        grad_ref,
        q_sum,
        u_sum,
    ):
        step = pl.program_id(0)
        allowed = same_segment(sc_ref, sr_ref)
        qn = qn_ref[...]
        qr = qr_ref[...]
        kv = kv_ref[...]
        kr = kr_ref[...]
        d_rope = None
        d_key = None
        d_nope = []
        d_keyval = []
        for h in range(heads):
            probs = head_probs(h, allowed, qn, qr, kv, kr)
            base = h * (NOPE + VDIM)
            keys = kv[:, base : base + NOPE]
            values = kv[:, base + NOPE : base + NOPE + VDIM]
            d_att = da_ref[:, h * VDIM : (h + 1) * VDIM]
            d_values = dot_rows(probs.astype(LOW), d_att)
            d_probs = dot_last(d_att, values)
            inner = jnp.sum(probs * d_probs, -1, keepdims=True)
            d_scores = (probs * (d_probs - inner)).astype(LOW)
            d_nope.append((dot(d_scores, keys) * SCORE_SCALE).astype(LOW))
            rope = dot(d_scores, kr[:, h * width : (h + 1) * width])
            d_rope = rope if d_rope is None else d_rope + rope
            d_keys = dot_rows(d_scores, qn[:, h * NOPE : (h + 1) * NOPE]) * SCORE_SCALE
            d_keyval += [d_keys.astype(LOW), d_values.astype(LOW)]
            turn = dot_rows(d_scores, qr)
            turn = jnp.concatenate(
                [turn[:, 32 * h : 32 * h + 32], turn[:, half + 32 * h : half + 32 * h + 32]], 1
            )
            d_key = turn if d_key is None else d_key + turn
        d_rope = d_rope * SCORE_SCALE
        d_rope = (d_rope * cos_ref[...] - turned(d_rope) * sin_ref[...]).astype(LOW)
        pieces = []
        for h in range(heads):
            pieces += [d_nope[h], d_rope[:, 32 * h : 32 * h + 32]]
            pieces.append(d_rope[:, half + 32 * h : half + 32 * h + 32])
        if query_wide > heads * (NOPE + ROPE):
            pieces.append(jnp.zeros((rows, query_wide - heads * (NOPE + ROPE)), LOW))
        d_query = jnp.concatenate(pieces, 1)
        d_keyval = jnp.concatenate(d_keyval, 1)
        d_key = (d_key * SCORE_SCALE).astype(LOW)
        d_key = jnp.concatenate([d_key, jnp.zeros((rows, wide - RANK - ROPE), LOW)], 1)
        d_normed = dot_last(
            d_query, qu_ref[:, :, :query_wide].reshape(model, query_wide)
        ).astype(LOW)
        d_low = dot_last(d_keyval, uw_ref[...]).astype(LOW)

        @pl.when(step < middle)
        def _():
            first_ref[...] = d_normed
            lat_first_ref[:, :RANK] = d_low
            lat_first_ref[:, RANK:] = d_key

        @pl.when(step >= middle)
        def _():
            second_ref[...] = d_normed
            lat_second_ref[:, :RANK] = d_low
            lat_second_ref[:, RANK:] = d_key

        q_add = dot_rows(n_ref[...], d_query)
        u_add = dot_rows(low_ref[...], d_keyval)

        @pl.when(step == 0)
        def _():
            q_sum[...] = q_add
            u_sum[...] = u_add

        @pl.when(step > 0)
        def _():
            q_sum[...] += q_add
            u_sum[...] += u_add

        @pl.when(step == count - 1)
        def _():
            grad_ref[...] = jnp.zeros(grad_ref.shape, LOW)
            for z in range(shards):
                grad_ref[z, :, :query_wide] = q_sum[z * slab : (z + 1) * slab].astype(LOW)
                for i in range(up_cols // 128):
                    grad_ref[z, i * lat : (i + 1) * lat, query_wide:] = u_sum[
                        z * lat : (z + 1) * lat, i * 128 : (i + 1) * 128
                    ].astype(LOW)

    def tok(a):
        return pl.BlockSpec((rows, a.shape[1]), lambda b, dev_ref: (b, 0))

    def low_half(cols):
        return pl.BlockSpec((rows, cols), lambda b, dev_ref: (jnp.minimum(b, middle - 1), 0))

    def high_half(cols):
        return pl.BlockSpec((rows, cols), lambda b, dev_ref: (jnp.maximum(b - middle, 0), 0))

    arrays = [q_nope, q_rope, keyval, k_rope]
    return pl.pallas_call(
        kernel,
        grid_spec=pltpu.PrefetchScalarGridSpec(
            num_scalar_prefetch=1,
            grid=(count,),
            in_specs=[tok(a) for a in arrays]
            + [pl.BlockSpec((rows, given.shape[1]), lambda b, dev_ref: (dev_ref[b], 0))]
            + [tok(normed), tok(low), whole(query_up), whole(up_w), tok(cosine), tok(sine)]
            + [tok(seg_col), pl.BlockSpec((1, 1, rows), lambda b, dev_ref: (b, 0, 0))],
            out_specs=[low_half(model), high_half(model), low_half(wide), high_half(wide)]
            + [pl.BlockSpec(query_up.shape, lambda b, dev_ref: (0, 0, 0))],
            scratch_shapes=[pltpu.VMEM((model, query_wide), F32), pltpu.VMEM(up_w.shape, F32)],
        ),
        out_shape=[
            jax.ShapeDtypeStruct((total // 2, model), LOW),
            jax.ShapeDtypeStruct((total // 2, model), LOW),
            jax.ShapeDtypeStruct((total // 2, wide), LOW),
            jax.ShapeDtypeStruct((total // 2, wide), LOW),
            jax.ShapeDtypeStruct(query_up.shape, LOW),
        ],
        cost_estimate=cost(total * model * 6),
    )(devices, *arrays, given, normed, low, query_up, up_w, cosine, sine, seg_col, seg_row)


def experts(info, blocks, grad, counts, valid, small_w, gate_w, lower_w, is_expert):
    count = len(blocks)
    rows, model = blocks[0].shape
    hidden = gate_w.shape[1] // 2
    total = count * rows
    middle = count // 2
    lanes = counts.shape[1]
    router_at = small_w.shape[1] - lanes

    def kernel(info_ref, *refs):
        parts = refs[:count]
        grad_ref, counts_ref, valid_ref, sw_ref, gw_ref, lw_ref, ex_ref = refs[count : count + 7]
        (
            mixed_ref,
            hid_ref,
            dg_ref,
            dm_first,
            dm_second,
            out_first,
            out_second,
            dw_ref,
            sig_ref,
            held,
        ) = refs[count + 7 :]
        step = pl.program_id(0)
        for k in range(count):

            @pl.when(step == k)
            def _():
                held[...] = parts[k][...]

        mixed = held[...]
        mixed_ref[...] = mixed
        sig = jax.nn.sigmoid(dot(mixed, sw_ref[:, router_at:]))
        sig_count = sig * counts_ref[...].astype(F32)
        lane = lax.broadcasted_iota(jnp.int32, (rows, lanes), 1)
        picked = jnp.sum(jnp.where(lane == lanes - NEXP + info_ref[0], sig_count, 0.0), 1, keepdims=True)
        picked_total = jnp.sum(sig_count, 1, keepdims=True)
        weight = ROUTE_SCALE * picked / picked_total * valid_ref[...]

        @pl.when(step == 0)
        def _():
            sig_ref[...] = sig

        routed = ex_ref[...] > 0.0
        both = dot(mixed, gw_ref[...])
        gate = both[:, :hidden]
        lift = both[:, hidden:]
        d_hidden = dot_last(grad_ref[...], lw_ref[...])
        gate_sig = jax.nn.sigmoid(gate)
        gated = gate * gate_sig
        act = gated * lift
        wide = jnp.where(routed, weight, 1.0)
        hid = (act * wide).astype(LOW)
        hid_ref[...] = hid
        dw_ref[...] = jnp.sum(jnp.where(routed, act * d_hidden, 0.0), 1, keepdims=True)
        d_hidden = d_hidden * wide
        d_gate = (d_hidden * lift * gate_sig * (1.0 + gate * (1.0 - gate_sig))).astype(LOW)
        d_lift = (d_hidden * gated).astype(LOW)
        d_both = jnp.concatenate([d_gate, d_lift], 1)
        dg_ref[...] = d_both
        d_mixed = dot_last(d_both, gw_ref[...]).astype(LOW)
        out = dot(hid, lw_ref[...]).astype(LOW)

        @pl.when(step < middle)
        def _():
            dm_first[...] = d_mixed
            out_first[...] = out

        @pl.when(step >= middle)
        def _():
            dm_second[...] = d_mixed
            out_second[...] = out

    def tok(cols):
        return pl.BlockSpec((rows, cols), lambda b, info_ref: (b, 0))

    low_half = pl.BlockSpec((rows, model), lambda b, info_ref: (jnp.minimum(b, middle - 1), 0))
    high_half = pl.BlockSpec((rows, model), lambda b, info_ref: (jnp.maximum(b - middle, 0), 0))
    part = jax.ShapeDtypeStruct((total // 2, model), LOW)
    return pl.pallas_call(
        kernel,
        grid_spec=pltpu.PrefetchScalarGridSpec(
            num_scalar_prefetch=1,
            grid=(count,),
            in_specs=[whole(a) for a in blocks]
            + [tok(model), tok(lanes), tok(1)]
            + [whole(a) for a in (small_w, gate_w, lower_w, is_expert)],
            out_specs=[tok(model), tok(hidden), tok(2 * hidden)]
            + [low_half, high_half, low_half, high_half, tok(1)]
            + [pl.BlockSpec((rows, lanes), lambda b, info_ref: (0, 0))],
            scratch_shapes=[pltpu.VMEM((rows, model), LOW)],
        ),
        out_shape=[jax.ShapeDtypeStruct((total, model), LOW)]
        + [jax.ShapeDtypeStruct((total, w), LOW) for w in (hidden, 2 * hidden)]
        + [part] * 4
        + [jax.ShapeDtypeStruct((total, 1), F32), jax.ShapeDtypeStruct((rows, lanes), F32)],
        cost_estimate=cost(total * model * 12),
    )(info, *blocks, grad, counts, valid, small_w, gate_w, lower_w, is_expert)


def cost(size):
    return pl.CostEstimate(flops=0, bytes_accessed=size // 8, transcendentals=0)


def arrivals(steps, here, count):
    found = []
    for index, step in enumerate(steps):
        if step == "last":
            found.append((index, here == 0, count - 1))
            found.append((index, here == count - 1, 0))
        elif step == "above":
            found.append((index, here < count - 1, here + 1))
        elif step == "below":
            found.append((index, here > 0, here - 1))
        else:
            found.append((index, None, lax.rem(here + step, count)))
    return found


def each_arrival(steps, here, count, act):
    for index, condition, place in arrivals(steps, here, count):
        if condition is None:
            act(index, place)
        else:
            pl.when(condition)(functools.partial(act, index, place))


def scalars(*values):
    return jnp.stack([v.astype(jnp.int32) for v in values])


def shard_place(count, own, came, shard, start, size):
    steps = [k for k, _ in came]
    width = own.shape[1]
    tile = size
    while tile > 128 and tile % 2 == 0 and start % (tile // 2) == 0:
        tile //= 2

    def kernel(at_ref, own_ref, *refs):
        out = refs[-1]
        here = at_ref[0]
        out[here] = own_ref[...]

        def act(index, place):
            out[place] = refs[index][...]

        each_arrival(steps, here, count, act)

    return pl.pallas_call(
        kernel,
        grid_spec=pltpu.PrefetchScalarGridSpec(
            num_scalar_prefetch=1,
            grid=(size // tile,),
            in_specs=[pl.BlockSpec((tile, width), lambda b, at_ref: (b + start // tile, 0))]
            * (len(came) + 1),
            out_specs=pl.BlockSpec((count, tile, width), lambda b, at_ref: (0, b, 0)),
        ),
        out_shape=jax.ShapeDtypeStruct((count, size, width), LOW),
        cost_estimate=cost(4 * count * size * width),
    )(scalars(shard), own, *[piece for _, piece in came])


def strip_place(local, pieces, steps, shard, devices, start, tile):
    count = max(steps) + 1
    reps = len(pieces)
    rows, width = local.shape
    strip = pieces[0].shape[0] // len(steps)

    def kernel(at_ref, own_ref, *refs):
        out = refs[-1]
        here = at_ref[0]
        out[here] = own_ref[...]
        for j in range(reps):
            base = pl.multiple_of(at_ref[1 + j] * strip, strip)

            def act(index, place):
                out[place, pl.ds(base, strip)] = refs[j][index * strip : (index + 1) * strip]

            each_arrival(steps, here, count, act)

    return pl.pallas_call(
        kernel,
        grid_spec=pltpu.PrefetchScalarGridSpec(
            num_scalar_prefetch=1,
            grid=(width // tile,),
            in_specs=[pl.BlockSpec((rows, tile), lambda b, at_ref: (0, b))]
            + [
                pl.BlockSpec((pieces[0].shape[0], tile), lambda b, at_ref: (0, b + start // tile))
                for _ in pieces
            ],
            out_specs=pl.BlockSpec((count, rows, tile), lambda b, at_ref: (0, 0, b)),
        ),
        out_shape=jax.ShapeDtypeStruct((count, rows, width), LOW),
        cost_estimate=cost(4 * count * rows * width),
    )(jnp.concatenate([scalars(shard), devices]), local, *pieces).reshape(count * rows, width)


def merge_rows(blocks, act, extra, widths):
    rows = blocks[0].shape[0]
    count = len(blocks)
    outs = len(widths)

    def kernel(*refs):
        index = pl.program_id(0)
        more = [r[...] for r in refs[count:-outs]]
        for k in range(count):

            @pl.when(index == k)
            def _():
                for ref, value in zip(refs[-outs:], act(refs[k][...], *more)):
                    ref[...] = value

    return pl.pallas_call(
        kernel,
        grid=(count,),
        in_specs=[
            pl.BlockSpec(a.shape, lambda b: (0, 0), pipeline_mode=pl.Buffered(1)) for a in blocks
        ]
        + [pl.BlockSpec((rows, a.shape[1]), lambda b: (b, 0)) for a in extra],
        out_specs=[pl.BlockSpec((rows, w), lambda b: (b, 0)) for w in widths],
        out_shape=[jax.ShapeDtypeStruct((count * rows, w), LOW) for w in widths],
        cost_estimate=cost(count * rows * sum(widths) * 4),
    )(*blocks, *extra)


def assemble(blocks, devices, grid, block_shape, block_map, outs, place, weights=()):
    reps = len(blocks)
    count = len(weights)

    def kernel(dev_ref, *refs):
        held = refs[-1]
        out_refs = refs[reps + count : -1]
        for k in range(reps):
            held[dev_ref[k]] = refs[k][...].astype(F32)
        for j in range(reps):
            place(pl.program_id(0), j, held[j], out_refs)
        total = None
        for i in range(count):
            value = refs[reps + i][...].astype(F32) * out_refs[i][...]
            value = jnp.sum(value, -1, keepdims=True)
            if value.ndim == 3:
                value = jnp.sum(value, 0)
            total = value if total is None else total + value
        if count:
            out_refs[-1][...] = total

    specs = [
        pl.BlockSpec(shape, functools.partial(lambda m, b, dev_ref: m(b), where))
        for _, shape, where in outs
    ]
    sums = []
    if count:
        rows = outs[0][1][0]
        sums = [((grid * rows, 1), (rows, 1), lambda b: (b, 0))]
    return pl.pallas_call(
        kernel,
        grid_spec=pltpu.PrefetchScalarGridSpec(
            num_scalar_prefetch=1,
            grid=(grid,),
            in_specs=[pl.BlockSpec(block_shape, lambda b, dev_ref: block_map(b)) for _ in blocks]
            + specs[:count],
            out_specs=specs
            + [pl.BlockSpec(shape, lambda b, dev_ref: (b, 0)) for _, shape, _ in sums],
            scratch_shapes=[pltpu.VMEM((reps,) + block_shape, F32)],
        ),
        out_shape=[jax.ShapeDtypeStruct(shape, F32) for shape, _, _ in outs + sums],
        cost_estimate=cost(reps * blocks[0].size * 6),
    )(devices, *blocks, *weights)


def layouts(lengths, seq_owner, devices, rows):
    count = lengths.shape[0]
    mine = seq_owner[None, :] == devices[:, None]
    own_length = jnp.where(mine, lengths[None, :], 0)
    numbers = jnp.arange(count, dtype=jnp.int32)
    ahead = numbers[:, None] < numbers[None, :]
    starts = jnp.sum(jnp.where(ahead[None], own_length[:, :, None], 0), 1)[:, None, :]
    ends = starts + own_length[:, None, :]
    row = jnp.arange(rows, dtype=jnp.int32)[None, :, None]
    inside = mine[:, None, :] & (row >= starts) & (row < ends)
    valid = jnp.any(inside, 2, keepdims=True)
    segment = jnp.sum(jnp.where(inside, numbers, 0), 2, keepdims=True)
    position = row - jnp.sum(jnp.where(inside, starts, 0), 2, keepdims=True)
    return jnp.where(valid, segment, count), position, valid


def make_local(reps, shards):
    group = Group(reps, shards)
    heads = HEADS // reps
    half = 32 * heads
    width = 2 * half

    def local(
        tokens,
        cotangent,
        lengths,
        seq_owner,
        expert_ids,
        attention_gain,
        query_weight,
        latent_down,
        latent_gain,
        latent_up,
        output_weight,
        feedforward_gain,
        router_weight,
        shared_gate,
        shared_up,
        shared_down,
        expert_gate,
        expert_up,
        expert_down,
    ):
        rows, model = tokens.shape
        rep = lax.axis_index("rep")
        shard = lax.axis_index("shard")
        devices = group.devices(rep)
        slab = model // shards
        strip = slab // reps
        lat = latent_gain.shape[0]
        cut = group.half * rows

        x_gather = Gathering(group, tokens)
        x_gather.start()
        small = jnp.concatenate(
            [
                lax.dynamic_slice_in_dim(latent_down, rep * strip, strip, 0),
                lax.dynamic_slice_in_dim(router_weight, rep * strip, strip, 0),
            ],
            1,
        )
        small = lax.all_gather(small, ("shard", "rep"), axis=0, tiled=True)
        output_shift = Shifting(
            group, lax.dynamic_slice_in_dim(output_weight, rep * strip, strip, 0)
        )
        output_shift.start()

        query_cols = heads * (NOPE + ROPE)
        up_cols = heads * (NOPE + VDIM)
        query_wide = round_up(query_cols, 128)
        query_part = lax.dynamic_slice_in_dim(query_weight, rep * query_cols, query_cols, 1)
        if query_wide > query_cols:
            query_part = jnp.pad(query_part, ((0, 0), (0, query_wide - query_cols)))
        up_part = lax.dynamic_slice_in_dim(latent_up, rep * up_cols, up_cols, 1)
        up_part = fold(up_part, slab)
        gain_rows = jnp.concatenate([attention_gain, feedforward_gain, latent_gain])
        gain_lanes = query_wide + 128
        gain_count = round_up(gain_rows.shape[0], 16 * gain_lanes)
        gain_rows = jnp.pad(gain_rows, (0, gain_count - gain_rows.shape[0])).reshape(-1, gain_lanes)
        query_part = jnp.concatenate(
            [jnp.concatenate([query_part, up_part], 1), gain_rows], 0
        )
        query_shift = Shifting(group, query_part)
        query_shift.start()

        part_s = shared_down.shape[0] // reps
        local_e = expert_down.shape[1]
        part_e = WINDOW * local_e // reps
        per = reps // WINDOW
        my_expert = rep // per
        used = part_s + part_e
        hidden = round_up(shards * used, 128)
        unit = hidden // shards
        place = jnp.arange(hidden, dtype=jnp.int32)
        within = place % unit
        is_shared = within < part_s
        is_expert = (within >= part_s) & (within < used)
        from_shared = jnp.where(
            is_shared, (place // unit) * shared_down.shape[0] + rep * part_s + within, -1
        )
        from_expert = jnp.where(
            is_expert, (place // unit) * local_e + (rep % per) * part_e + within - part_s, -1
        )
        pick_s = (
            jnp.arange(shared_gate.shape[1], dtype=jnp.int32)[:, None] == from_shared[None, :]
        ).astype(LOW)
        pick_e = (
            jnp.arange(expert_gate.shape[2], dtype=jnp.int32)[:, None] == from_expert[None, :]
        ).astype(LOW)

        def my_columns(shared, expert):
            expert = lax.dynamic_index_in_dim(expert, my_expert, 0, keepdims=False)
            return (dot(shared, pick_s) + dot(expert, pick_e)).astype(LOW)

        gate_all = jnp.concatenate(
            [my_columns(shared_gate, expert_gate), my_columns(shared_up, expert_up)], 1
        )
        lower_part = jnp.concatenate(
            [
                lax.dynamic_slice_in_dim(shared_down, rep * part_s, part_s, 0),
                lax.dynamic_slice(
                    expert_down, (my_expert, (rep % per) * part_e, 0), (1, part_e, model)
                )[0],
                jnp.zeros((unit - used, model), LOW),
            ],
            0,
        )

        segment, position, valid = layouts(lengths, seq_owner, devices * shards + shard, rows)
        total_rows = reps * rows
        seg_col = segment.reshape(total_rows, 1)
        seg_row = segment.reshape(reps, 1, rows)
        valid_all = valid.reshape(total_rows, 1).astype(F32)
        valid_own = valid_all[:rows]
        frequency = jnp.power(ROPE_BASE, -2.0 * jnp.arange(32, dtype=F32) / ROPE)
        angles = position.reshape(total_rows, 1).astype(F32) * jnp.tile(frequency, 2 * heads)[None]
        cosine = jnp.cos(angles)
        side = jnp.where(jnp.arange(width) < half, -1.0, 1.0).astype(F32)
        sine = jnp.sin(angles) * side[None, :]

        hidden_in = tokens.astype(F32)
        counts = jnp.sum(
            (expert_ids[:, :, None] == jnp.arange(NEXP, dtype=jnp.int32)).astype(F32), 1
        )
        given = jnp.concatenate(
            [cotangent, jnp.zeros((rows, 128 - NEXP), LOW), counts.astype(LOW)], 1
        )

        phase(x_gather, query_shift, output_shift)
        x_gather.start()
        query_shift.start()
        output_shift.start()
        (gate_all,) = phase(x_gather, query_shift, output_shift, gate_all)
        gate_all = lax.all_gather(gate_all, "shard", axis=0, tiled=True)
        x_gather.start()
        output_came = output_shift.whole(shard)
        shard_steps = [k for k, _ in output_came]
        output_gather = Gathering(group, jnp.concatenate([piece for _, piece in output_came], 0))
        output_gather.start()
        query_up = shard_place(shards, query_part, query_shift.result(), shard, 0, slab)
        gains = shard_place(
            shards, query_part, query_shift.result(), shard, slab, gain_rows.shape[0]
        )
        gains = gains.reshape(shards, -1).astype(F32)
        attention_gain_all = gains[:, :slab].reshape(1, model)
        mixer_gain_all = gains[:, slab : 2 * slab].reshape(1, model)
        latent_gain_all = gains[:, 2 * slab : 2 * slab + lat].reshape(1, RANK)

        lane = jnp.arange(heads * width, dtype=jnp.int32)
        head = lane // width
        spot = lane % width
        source = jnp.where(
            (spot % half) // 32 == head, (spot // half) * 32 + spot % 32, -1
        )
        spread = (jnp.arange(ROPE, dtype=jnp.int32)[:, None] == source[None, :]).astype(LOW)
        cols = heads * VDIM
        normed_all, qn, qr, keyval, kr, latent_low, up_all, latent_own, attended = attend_forward(
            devices,
            x_gather.list(),
            attention_gain_all,
            latent_gain_all,
            query_up,
            heads,
            small,
            spread,
            cosine,
            sine,
            seg_col,
            seg_row,
        )
        attended, given, lower_part = phase(attended, output_gather, given, lower_part)
        output_gather.start()
        lower_all = lax.all_gather(lower_part, "shard", axis=0, tiled=True)
        attended_own = lax.all_to_all(
            attended.reshape(reps, rows, cols), "rep", 0, 0, tiled=True
        )
        (attended_own,) = phase(attended_own, output_gather)
        output_gather.start()
        given_gather = Gathering(group, given)
        given_gather.start()
        output_all = strip_place(
            output_weight, output_gather.list(), shard_steps, shard, devices, 0, 256
        )
        attended_own = jnp.transpose(attended_own, (1, 0, 2)).reshape(rows, HEADS * VDIM)
        mid = hidden_in + dot(attended_own, output_all)
        mixed_scale = rms_scale(mid)
        mixed = (mid * mixed_scale * mixer_gain_all).astype(LOW)

        mixed_gather = Gathering(group, mixed)
        mixed_gather.start()
        (gate_all,) = phase(mixed_gather, given_gather, gate_all)
        mixed_gather.start()
        given_gather.start()
        phase(mixed_gather, given_gather)
        mixed_gather.start()
        given_gather.start()
        grad_all, counts_all = merge_rows(
            given_gather.list(),
            lambda block, ok: (
                (block[:, :model].astype(F32) * ok).astype(LOW),
                block[:, model:],
            ),
            [valid_all],
            [model, 128],
        )
        grad_all, counts_all = phase(mixed_gather, grad_all, counts_all)
        (
            mixed_all,
            hidden_low,
            d_both,
            d_mixed_first,
            d_mixed_second,
            ffn_first,
            ffn_second,
            d_weight,
            sig_own,
        ) = experts(
            jnp.reshape(my_expert, (1,)).astype(jnp.int32),
            mixed_gather.list(),
            grad_all,
            counts_all,
            valid_all,
            small,
            gate_all,
            lower_all,
            is_expert.astype(F32)[None, :],
        )
        sig_own = sig_own[:, -NEXP:]
        mixed_sum = Reducing(group, d_mixed_second, d_mixed_first)
        mixed_sum.start()
        both_grad = dot_rows(mixed_all, d_both).astype(LOW)
        ffn_second, d_weight, hidden_low, _ = phase(
            mixed_sum, ffn_second, d_weight, hidden_low, both_grad
        )
        mixed_sum.start()
        numbers = jnp.arange(reps, dtype=jnp.int32)
        by_device = jnp.sum(
            jnp.where(
                (devices[None, :] == numbers[:, None])[:, :, None],
                d_weight.reshape(1, reps, rows),
                0.0,
            ),
            1,
        )
        d_weight_own = lax.all_to_all(by_device, "rep", 0, 0, tiled=True)
        d_weight_own = jnp.sum(d_weight_own.reshape(WINDOW, per, rows), 1)
        ffn_sum = Reducing(group, ffn_second, ffn_first)
        ffn_sum.start()
        hidden_low, d_weight_own = phase(mixed_sum, ffn_sum, hidden_low, d_weight_own)
        both_grad = lax.psum_scatter(both_grad, "shard", scatter_dimension=0, tiled=True)
        mixed_sum.start()
        lower_grad = dot_rows(hidden_low, grad_all).astype(LOW)
        phase(mixed_sum, lower_grad)
        lower_grad = lax.psum_scatter(lower_grad, "shard", scatter_dimension=0, tiled=True)[:used]
        d_mixed = mixed_sum.total()

        total_own = jnp.sum(sig_own * counts, 1, keepdims=True)
        hit = counts[:, :WINDOW]
        d_route = jnp.concatenate(
            [valid_own * d_weight_own.T * hit, jnp.zeros((rows, NEXP - WINDOW), F32)], 1
        )
        inner = jnp.sum(d_route * sig_own, 1, keepdims=True)
        d_sig = ROUTE_SCALE * (d_route / total_own - counts * inner / (total_own * total_own))
        d_logits = (d_sig * sig_own * (1.0 - sig_own)).astype(LOW)
        d_mixed = d_mixed + dot_last(d_logits, small[:, RANK + ROPE :])
        grad_own = cotangent.astype(F32) * valid_own
        d_mid = grad_own + rms_back(mid, mixed_scale, mixer_gain_all, d_mixed)
        d_branch = d_mid.astype(LOW)

        out_cols = model // reps

        def output_part(index):
            picked = [
                lax.dynamic_slice_in_dim(d_branch, devices[k] * out_cols, out_cols, 1)
                for k in index
            ]
            return dot_rows(attended_own, jnp.concatenate(picked, 1)).astype(LOW)

        output_sum = Reducing(
            group,
            output_part(range(group.half, reps)),
            output_part(range(group.half)),
            axis=1,
        )
        output_sum.start()

        d_attended = dot_last(d_branch, output_all).astype(LOW)
        d_attended = jnp.transpose(d_attended.reshape(rows, reps, cols), (1, 0, 2))
        d_attended = lax.all_to_all(d_attended, "rep", 0, 0, tiled=True)
        (d_attended,) = phase(d_attended, output_sum)
        output_sum.start()
        ffn_sum.start()
        d_attended = d_attended.reshape(total_rows, cols)
        (
            d_normed_first,
            d_normed_second,
            latent_first,
            latent_second,
            attention_grad,
        ) = attend_backward(
            devices,
            (qn, qr, keyval, kr),
            d_attended,
            normed_all,
            latent_low,
            query_up,
            up_all,
            cosine,
            sine,
            seg_col,
            seg_row,
            rows,
        )
        latent_second, d_normed_second = phase(
            latent_second, d_normed_second, output_sum, ffn_sum
        )
        attention_grad = lax.psum_scatter(
            attention_grad, "shard", scatter_dimension=0, tiled=True
        ).reshape(slab, query_wide + 128)
        latent_sum = Reducing(group, latent_second, latent_first)
        latent_sum.start()
        output_sum.start()
        both_gather = Gathering(group, both_grad)
        both_gather.start()
        (d_normed_second,) = phase(latent_sum, d_normed_second)
        latent_sum.start()
        normed_sum = Reducing(group, d_normed_second, d_normed_first)
        normed_sum.start()
        phase(latent_sum, output_sum)
        latent_sum.start()
        output_grad = lax.psum_scatter(
            output_sum.total().astype(LOW), "shard", scatter_dimension=0, tiled=True
        )
        phase(latent_sum)
        d_latent_sum = latent_sum.total()
        compressed = latent_own[:, :RANK]
        d_compressed = rms_back(
            compressed, rms_scale(compressed), latent_gain_all, d_latent_sum[:, :RANK]
        )
        kg_first = d_latent_sum[:, RANK : RANK + 32]
        kg_second = d_latent_sum[:, RANK + 32 : RANK + ROPE]
        cos_own = cosine[:rows, :32]
        sin_own = sine[:rows, half : half + 32]
        d_latent = jnp.concatenate(
            [
                d_compressed,
                kg_first * cos_own + kg_second * sin_own,
                kg_second * cos_own - kg_first * sin_own,
            ],
            1,
        ).astype(LOW)
        row_gather = Gathering(group, jnp.concatenate([d_latent, d_logits], 1))
        row_gather.start()
        (lower_grad,) = phase(row_gather, both_gather, lower_grad)
        row_gather.start()
        both_gather.start()
        phase(row_gather, normed_sum)
        row_gather.start()
        normed_sum.start()
        (attention_grad,) = phase(row_gather, both_gather, attention_grad)
        both_gather.start()
        lower_gather = Gathering(group, lower_grad)
        lower_gather.start()
        rows_given = row_gather.list()
        d_down = dot_last(d_latent, small[:, : RANK + ROPE])
        (row_grads,) = merge_rows(
            rows_given,
            lambda block: (block,),
            [],
            [RANK + ROPE + NEXP],
        )

        def my_strip(values):
            return jnp.concatenate(
                [
                    lax.dynamic_slice_in_dim(values, s * slab + rep * strip, strip, 1)
                    for s in range(shards)
                ],
                1,
            )

        strip_grad = jnp.concatenate(
            [
                dot_rows(my_strip(normed_all), row_grads[:, : RANK + ROPE]),
                dot_rows(my_strip(mixed_all), row_grads[:, RANK + ROPE :]),
            ],
            1,
        ).astype(LOW)

        strip_sum = lax.psum_scatter(strip_grad, "shard", scatter_dimension=0, tiled=True)
        _, output_grad = phase(both_gather, lower_gather, strip_grad, output_grad)
        lower_gather.start()
        query_gather = Gathering(group, attention_grad)
        query_gather.start()
        tile = min(slab, 64)

        def place_columns(step, j, block, refs):
            for side in (0, 1):
                for s in range(shards):
                    base = side * hidden + s * unit
                    at = s * part_s * reps + j * part_s
                    refs[2 * side][:, at : at + part_s] = block[:, base : base + part_s]
                    at = s * part_e * per + (j % per) * part_e
                    refs[2 * side + 1][j // per, :, at : at + part_e] = block[
                        :, base + part_s : base + used
                    ]

        wide_s = shared_gate.shape
        wide_e = expert_gate.shape
        sgate_grad, egate_grad, sup_grad, eup_grad, mixer_sum = assemble(
            both_gather.list(),
            devices,
            slab // tile,
            (tile, 2 * hidden),
            lambda b: (b, 0),
            [
                (wide_s, (tile, wide_s[1]), lambda b: (b, 0)),
                (wide_e, (WINDOW, tile, wide_e[2]), lambda b: (0, b, 0)),
            ]
            * 2,
            place_columns,
            (shared_gate, expert_gate, shared_up, expert_up),
        )

        phase(lower_gather, query_gather, normed_sum, sgate_grad)
        lower_gather.start()
        query_gather.start()
        normed_sum.start()
        ffn_sum.start()
        output_gather = Gathering(group, output_grad)
        output_gather.start()
        (strip_sum,) = phase(lower_gather, query_gather, output_gather, strip_sum)
        query_gather.start()
        output_gather.start()
        strip_gather = Gathering(group, strip_sum)
        strip_gather.start()
        def place_rows(step, j, block, refs):
            refs[0][j * part_s : (j + 1) * part_s] = block[:part_s]
            at = (j % per) * part_e
            refs[1][j // per, at : at + part_e] = block[part_s:]

        lane_tile = 256
        sdown_grad, edown_grad = assemble(
            lower_gather.list(),
            devices,
            model // lane_tile,
            (used, lane_tile),
            lambda b: (0, b),
            [
                (shared_down.shape, (shared_down.shape[0], lane_tile), lambda b: (0, b)),
                (expert_down.shape, (WINDOW, local_e, lane_tile), lambda b: (0, 0, b)),
            ],
            place_rows,
        )

        phase(query_gather, output_gather, strip_gather, sdown_grad, normed_sum, ffn_sum)
        output_gather.start()
        strip_gather.start()
        layer_out = (valid_own * (mid + ffn_sum.total())).astype(LOW)
        d_normed = normed_sum.total() + d_down
        token_grad = d_mid + rms_back(
            hidden_in, rms_scale(hidden_in), attention_gain_all, d_normed
        )

        def place_attention(step, j, block, refs):
            refs[0][:, j * query_cols : (j + 1) * query_cols] = block[:, :query_cols]

            @pl.when(step < up_cols // 128)
            def _():
                at = pl.multiple_of(j * up_cols + step * 128, 128)
                refs[1][:, pl.ds(at, 128)] = block[:, query_wide:]

        query_grad, up_grad, query_sum = assemble(
            query_gather.list(),
            devices,
            slab // lat,
            (lat, query_wide + 128),
            lambda b: (b, 0),
            [
                (query_weight.shape, (lat, query_weight.shape[1]), lambda b: (b, 0)),
                (latent_up.shape, latent_up.shape, lambda b: (0, 0)),
            ],
            place_attention,
            (query_weight,),
        )

        def place_output(step, j, block, refs):
            refs[0][:, j * out_cols : (j + 1) * out_cols] = block

        phase(output_gather, strip_gather, query_grad)
        strip_gather.start()
        (output_grad,) = assemble(
            output_gather.list(),
            devices,
            slab // lat,
            (lat, out_cols),
            lambda b: (b, 0),
            [(output_weight.shape, (lat, model), lambda b: (b, 0))],
            place_output,
        )

        def place_strip(step, j, block, refs):
            refs[0][:, j * strip : (j + 1) * strip] = block[:, : RANK + ROPE].T
            refs[1][:, j * strip : (j + 1) * strip] = block[:, RANK + ROPE :].T

        down_grad, router_grad = assemble(
            strip_gather.list(),
            devices,
            1,
            (strip, RANK + ROPE + NEXP),
            lambda b: (0, 0),
            [
                ((RANK + ROPE, slab), (RANK + ROPE, slab), lambda b: (0, 0)),
                ((NEXP, slab), (NEXP, slab), lambda b: (0, 0)),
            ],
            place_strip,
        )

        down_grad = down_grad.T
        router_grad = router_grad.T

        def row_sum(weight, grad):
            return jnp.sum(weight.astype(F32) * grad, -1)

        attention_gain_grad = (
            query_sum[:, 0] + row_sum(latent_down, down_grad)
        ) / attention_gain.astype(F32)
        latent_gain_grad = row_sum(latent_up, up_grad) / latent_gain.astype(F32)
        mixer_gain_grad = (
            row_sum(router_weight, router_grad) + mixer_sum[:, 0]
        ) / feedforward_gain.astype(F32)

        return (
            layer_out,
            token_grad,
            attention_gain_grad,
            query_grad,
            down_grad,
            latent_gain_grad,
            up_grad,
            output_grad,
            mixer_gain_grad,
            router_grad,
            sgate_grad,
            sup_grad,
            sdown_grad,
            egate_grad,
            eup_grad,
            edown_grad,
        )

    return local


def fold(value, rows):
    count = value.shape[1] // 128
    parts = [value[:, i * 128 : (i + 1) * 128] for i in range(count)]
    left = rows - count * value.shape[0]
    if left:
        parts.append(jnp.zeros((left, 128), value.dtype))
    return jnp.concatenate(parts, 0)


def solution(mesh):
    tokens = P(("rep", "shard"), None)
    vector = P("shard")
    matrix = P("shard", None)
    stack = P(None, "shard", None)
    in_specs = (
        (tokens, tokens, P(), P(), tokens, vector, matrix, matrix, vector, matrix, matrix, vector)
        + (matrix,) * 4
        + (stack,) * 3
    )
    out_specs = (
        (tokens, tokens, vector, matrix, matrix, vector, matrix, matrix, vector)
        + (matrix,) * 4
        + (stack,) * 3
    )
    local = make_local(mesh.shape["rep"], mesh.shape["shard"])
    return jax.shard_map(local, mesh=mesh, in_specs=in_specs, out_specs=out_specs, check_vma=False)
```

```python
import functools

import jax
import jax.numpy as jnp
from jax import lax
from jax.experimental import pallas as pl
from jax.experimental.pallas import tpu as pltpu
from jax.sharding import PartitionSpec as P

HEADS = 16
NOPE = 128
ROPE = 64
VDIM = 128
RANK = 512
NEXP = 64
WINDOW = 2

EPSILON = 1e-06
ROPE_BASE = 50000.0
ROUTE_SCALE = 2.446
NEG_FILL = -1e30
SCORE_SCALE = (NOPE + ROPE) ** (-0.5)

F32 = jnp.float32
LOW = jnp.bfloat16


def dot(left, right):
    return jnp.dot(left, right, preferred_element_type=F32)


def dot_rows(left, right):
    return lax.dot_general(left, right, (((0,), (0,)), ((), ())), preferred_element_type=F32)


def dot_last(left, right):
    return lax.dot_general(left, right, (((1,), (1,)), ((), ())), preferred_element_type=F32)


def rms_scale(values):
    return lax.rsqrt(jnp.mean(values * values, -1, keepdims=True) + EPSILON)


def rms_back(values, scale, gain, upstream):
    gained = upstream * gain
    inner = jnp.mean(values * gained, -1, keepdims=True)
    return scale * gained - values * scale * scale * scale * inner


def round_up(value, unit):
    return -(-value // unit) * unit


class Group:
    def __init__(self, reps, shards):
        self.reps = reps
        self.shards = shards
        bits = reps.bit_length() - 1
        assert bits >= 1 and 1 << bits == reps
        self.levels = [(1 << b, 1 << (bits - b)) for b in range(1, bits)]
        self.half = reps // 2

    def devices(self, rep):
        lists = []
        for side in (0, 1):
            masks = [0]
            for level in self.levels:
                masks = masks + [m ^ level[side] for m in masks]
            lists.append(masks)
        first = lists[0] + [m ^ 1 for m in lists[1]]
        second = lists[1] + [m ^ 1 for m in lists[0]]
        masks = jnp.where(
            rep % 2 == 0, jnp.array(first, jnp.int32), jnp.array(second, jnp.int32)
        )
        return rep.astype(jnp.int32) ^ masks

    def cross(self, value, level):
        pairs = [(i, i ^ level[i & 1]) for i in range(self.reps)]
        return lax.ppermute(value, "rep", pairs)


class Gathering:
    def __init__(self, group, block, early=False):
        self.group = group
        self.blocks = {0: block}
        self.stage = 0
        self.pending = {}
        self.early = early

    def start(self):
        group = self.group
        self.stage += 1
        if self.stage <= len(group.levels):
            for k in range(group.half):
                if bin(k).count("1") == self.stage:
                    top = k.bit_length() - 1
                    self.pending[k] = group.cross(self.blocks[k ^ (1 << top)], group.levels[top])
        last = self.stage == len(group.levels) + 1
        for k in range(group.half):
            fresh = bin(k).count("1") == self.stage - 1
            if (self.early and fresh) or (last and not self.early):
                self.pending[group.half + k] = group.cross(self.blocks[k], (1, 1))

    def settle(self, values):
        self.blocks.update(zip(self.pending, values))
        self.pending = {}

    def list(self):
        while True:
            self.settle(list(self.pending.values()))
            if len(self.blocks) == self.group.reps:
                return [self.blocks[k] for k in range(self.group.reps)]
            self.start()


class Reducing:
    def __init__(self, group, second, first, axis=0):
        self.group = group
        self.second = second
        self.terms = [first]
        self.axis = axis
        self.size = first.shape[axis]
        self.stage = 0
        self.pending = {}

    def cut(self, start, size):
        total = None
        for term in self.terms:
            term = lax.slice_in_dim(term, start, start + size, axis=self.axis).astype(F32)
            total = term if total is None else total + term
        return total

    def start(self):
        levels = self.group.levels
        if self.stage == 0:
            self.pending[0] = self.group.cross(self.second, (1, 1))
        elif self.stage <= len(levels):
            self.size //= 2
            sent = self.cut(self.size, self.size).astype(LOW)
            self.sent = sent
            self.pending[0] = self.group.cross(sent, levels[len(levels) - self.stage])
        self.stage += 1

    def settle(self, values):
        self.terms += values
        self.pending = {}

    def total(self):
        while True:
            self.settle(list(self.pending.values()))
            if self.stage > len(self.group.levels):
                return self.cut(0, self.size)
            self.start()


class Shifting:
    def __init__(self, group, block):
        self.count = group.shards
        self.block = block
        self.found = {}
        self.stage = 0
        self.pending = {}

    def start(self):
        count = self.count
        self.stage += 1

        def cycle(step):
            return [((i + step) % count, i) for i in range(count)]

        def move(value, pairs):
            return lax.ppermute(value, "shard", pairs)

        if count != 4:
            if self.stage == 1:
                self.pending = {k: move(self.block, cycle(k)) for k in range(1, count)}
        elif self.stage == 1:
            self.pending = {
                2: move(self.block, cycle(2)),
                "above": move(self.block, cycle(1)[:-1]),
                "below": move(self.block, cycle(3)[1:]),
            }
        elif self.stage == 2:
            self.pending = {"last": move(self.found[2], [(1, 0), (2, 3)])}

    def settle(self, values):
        self.found.update(zip(self.pending, values))
        self.pending = {}

    def result(self):
        self.settle(list(self.pending.values()))
        while self.stage < 2:
            self.start()
            self.settle(list(self.pending.values()))
        return list(self.found.items())

    def whole(self, position):
        found = dict(self.result())
        if self.count == 4:
            last = found.pop("last")
            found[1] = jnp.where(position == self.count - 1, last, found.pop("above"))
            found[3] = jnp.where(position == 0, last, found.pop("below"))
        return [(k, found[k]) for k in range(1, self.count)]


def phase(*items):
    values = []
    for item in items:
        values += list(item.pending.values()) if hasattr(item, "pending") else [item]
    values = list(lax.optimization_barrier(tuple(values)))
    arrays = []
    for item in items:
        if hasattr(item, "pending"):
            count = len(item.pending)
            item.settle(values[:count])
            values = values[count:]
        else:
            arrays.append(values.pop(0))
    return arrays


def head_probs(h, allowed, q_nope, q_rope, keyval, k_rope):
    width = q_rope.shape[1]
    base = h * (NOPE + VDIM)
    scores = dot_last(q_nope[:, h * NOPE : (h + 1) * NOPE], keyval[:, base : base + NOPE])
    scores = scores + dot_last(q_rope, k_rope[:, h * width : (h + 1) * width])
    scores = jnp.where(allowed, scores * SCORE_SCALE, NEG_FILL)
    unnormed = jnp.exp(scores - jnp.max(scores, -1, keepdims=True))
    return unnormed / jnp.sum(unnormed, -1, keepdims=True)


def same_segment(sc_ref, sr_ref):
    rows = sc_ref.shape[0]
    t = lax.broadcasted_iota(jnp.int32, (rows, rows), 0)
    u = lax.broadcasted_iota(jnp.int32, (rows, rows), 1)
    return (sc_ref[...] == sr_ref[0]) & (u <= t)


def turned(values):
    half = values.shape[1] // 2
    return jnp.concatenate([values[:, half:], values[:, :half]], 1)


def whole(a):
    return pl.BlockSpec(a.shape, lambda b, dev_ref: (0,) * a.ndim, pipeline_mode=pl.Buffered(1))


def attend_forward(
    devices, blocks, gain, latent_gain, query_up, heads, small_w, spread, cosine, sine, seg_col, seg_row
):
    count = len(blocks)
    rows, model = blocks[0].shape
    shards, slab, lanes = query_up.shape
    query_wide = lanes - 128
    lat = RANK // shards
    up_cols = heads * (NOPE + VDIM)
    half = 32 * heads
    width = 2 * half

    def kernel(dev_ref, *refs):
        parts = refs[:count]
        gain_ref, lgain_ref, qu_ref, sw_ref, spread_ref, cos_ref, sin_ref, sc_ref, sr_ref = (
            refs[count : count + 9]
        )
        normed_ref, qn_ref, qr_ref, kv_ref, kr_ref, low_ref, up_ref, own_ref, out_ref, held = refs[
            count + 9 :
        ]
        step = pl.program_id(0)
        for k in range(count):

            @pl.when(step == k)
            def _():
                held[...] = parts[k][...]

        @pl.when(step == 0)
        def _():
            for z in range(shards):
                for i in range(up_cols // 128):
                    up_ref[z * lat : (z + 1) * lat, i * 128 : (i + 1) * 128] = qu_ref[
                        z, i * lat : (i + 1) * lat, query_wide:
                    ]

        x = held[...].astype(F32)
        normed = (x * rms_scale(x) * gain_ref[...]).astype(LOW)
        normed_ref[...] = normed
        query = dot(normed, qu_ref[:, :, :query_wide].reshape(model, query_wide))
        at = [h * (NOPE + ROPE) for h in range(heads)]
        q_nope = jnp.concatenate([query[:, i : i + NOPE] for i in at], 1).astype(LOW)
        q_rope = jnp.concatenate(
            [query[:, i + NOPE + c : i + NOPE + c + 32] for c in (0, 32) for i in at], 1
        )
        cos = cos_ref[...]
        sin = sin_ref[...]
        q_rope = (q_rope * cos + turned(q_rope) * sin).astype(LOW)
        latent = dot(normed, sw_ref[...])

        @pl.when(step == 0)
        def _():
            own_ref[...] = latent

        compressed = latent[:, :RANK]
        low = (compressed * rms_scale(compressed) * lgain_ref[...]).astype(LOW)
        key = latent[:, RANK : RANK + ROPE]
        key = key * cos[:, :ROPE] + turned(key) * sin[:, half - 32 : half + 32]
        k_rope = dot(key.astype(LOW), spread_ref[...]).astype(LOW)
        keyval = dot(low, up_ref[...]).astype(LOW)
        qn_ref[...] = q_nope
        qr_ref[...] = q_rope
        kv_ref[...] = keyval
        kr_ref[...] = k_rope
        low_ref[...] = low
        allowed = same_segment(sc_ref, sr_ref)
        for h in range(heads):
            probs = head_probs(h, allowed, q_nope, q_rope, keyval, k_rope)
            base = h * (NOPE + VDIM) + NOPE
            out_ref[:, h * VDIM : (h + 1) * VDIM] = dot(
                probs.astype(LOW), keyval[:, base : base + VDIM]
            ).astype(LOW)

    def tok(cols):
        return pl.BlockSpec((rows, cols), lambda b, dev_ref: (b, 0))

    total = count * rows
    widths = [model, heads * NOPE, width, heads * (NOPE + VDIM), heads * width, RANK]
    return pl.pallas_call(
        kernel,
        grid_spec=pltpu.PrefetchScalarGridSpec(
            num_scalar_prefetch=1,
            grid=(count,),
            in_specs=[whole(a) for a in blocks]
            + [whole(a) for a in (gain, latent_gain, query_up, small_w, spread)]
            + [tok(width), tok(width), tok(1)]
            + [pl.BlockSpec((1, 1, rows), lambda b, dev_ref: (b, 0, 0))],
            out_specs=[tok(w) for w in widths]
            + [
                pl.BlockSpec((RANK, up_cols), lambda b, dev_ref: (0, 0)),
                pl.BlockSpec((rows, small_w.shape[1]), lambda b, dev_ref: (0, 0)),
            ]
            + [pl.BlockSpec((rows, heads * VDIM), lambda b, dev_ref: (dev_ref[b], 0))],
            scratch_shapes=[pltpu.VMEM((rows, model), LOW)],
        ),
        out_shape=[jax.ShapeDtypeStruct((total, w), LOW) for w in widths]
        + [
            jax.ShapeDtypeStruct((RANK, up_cols), LOW),
            jax.ShapeDtypeStruct((rows, small_w.shape[1]), F32),
        ]
        + [jax.ShapeDtypeStruct((total, heads * VDIM), LOW)],
        cost_estimate=cost(total * model * 6),
    )(devices, *blocks, gain, latent_gain, query_up, small_w, spread, cosine, sine, seg_col, seg_row)


def attend_backward(
    devices, kept, given, normed, low, query_up, up_w, cosine, sine, seg_col, seg_row, rows
):
    q_nope, q_rope, keyval, k_rope = kept
    total, model = normed.shape
    count = total // rows
    heads = up_w.shape[1] // (NOPE + VDIM)
    half = 32 * heads
    width = 2 * half
    nope = heads * NOPE
    middle = count // 2
    shards, slab, lanes = query_up.shape
    query_wide = lanes - 128
    lat = RANK // shards
    up_cols = up_w.shape[1]
    wide = RANK + round_up(ROPE, 128)

    def kernel(
        dev_ref,
        qn_ref,
        qr_ref,
        kv_ref,
        kr_ref,
        da_ref,
        n_ref,
        low_ref,
        qu_ref,
        uw_ref,
        cos_ref,
        sin_ref,
        sc_ref,
        sr_ref,
        first_ref,
        second_ref,
        lat_first_ref,
        lat_second_ref,
        grad_ref,
        q_sum,
        u_sum,
    ):
        step = pl.program_id(0)
        allowed = same_segment(sc_ref, sr_ref)
        qn = qn_ref[...]
        qr = qr_ref[...]
        kv = kv_ref[...]
        kr = kr_ref[...]
        d_rope = None
        d_key = None
        d_nope = []
        d_keyval = []
        for h in range(heads):
            probs = head_probs(h, allowed, qn, qr, kv, kr)
            base = h * (NOPE + VDIM)
            keys = kv[:, base : base + NOPE]
            values = kv[:, base + NOPE : base + NOPE + VDIM]
            d_att = da_ref[:, h * VDIM : (h + 1) * VDIM]
            d_values = dot_rows(probs.astype(LOW), d_att)
            d_probs = dot_last(d_att, values)
            inner = jnp.sum(probs * d_probs, -1, keepdims=True)
            d_scores = (probs * (d_probs - inner)).astype(LOW)
            d_nope.append((dot(d_scores, keys) * SCORE_SCALE).astype(LOW))
            rope = dot(d_scores, kr[:, h * width : (h + 1) * width])
            d_rope = rope if d_rope is None else d_rope + rope
            d_keys = dot_rows(d_scores, qn[:, h * NOPE : (h + 1) * NOPE]) * SCORE_SCALE
            d_keyval += [d_keys.astype(LOW), d_values.astype(LOW)]
            turn = dot_rows(d_scores, qr)
            turn = jnp.concatenate(
                [turn[:, 32 * h : 32 * h + 32], turn[:, half + 32 * h : half + 32 * h + 32]], 1
            )
            d_key = turn if d_key is None else d_key + turn
        d_rope = d_rope * SCORE_SCALE
        d_rope = (d_rope * cos_ref[...] - turned(d_rope) * sin_ref[...]).astype(LOW)
        pieces = []
        for h in range(heads):
            pieces += [d_nope[h], d_rope[:, 32 * h : 32 * h + 32]]
            pieces.append(d_rope[:, half + 32 * h : half + 32 * h + 32])
        if query_wide > heads * (NOPE + ROPE):
            pieces.append(jnp.zeros((rows, query_wide - heads * (NOPE + ROPE)), LOW))
        d_query = jnp.concatenate(pieces, 1)
        d_keyval = jnp.concatenate(d_keyval, 1)
        d_key = (d_key * SCORE_SCALE).astype(LOW)
        d_key = jnp.concatenate([d_key, jnp.zeros((rows, wide - RANK - ROPE), LOW)], 1)
        d_normed = dot_last(
            d_query, qu_ref[:, :, :query_wide].reshape(model, query_wide)
        ).astype(LOW)
        d_low = dot_last(d_keyval, uw_ref[...]).astype(LOW)

        @pl.when(step < middle)
        def _():
            first_ref[...] = d_normed
            lat_first_ref[:, :RANK] = d_low
            lat_first_ref[:, RANK:] = d_key

        @pl.when(step >= middle)
        def _():
            second_ref[...] = d_normed
            lat_second_ref[:, :RANK] = d_low
            lat_second_ref[:, RANK:] = d_key

        q_add = dot_rows(n_ref[...], d_query)
        u_add = dot_rows(low_ref[...], d_keyval)

        @pl.when(step == 0)
        def _():
            q_sum[...] = q_add
            u_sum[...] = u_add

        @pl.when(step > 0)
        def _():
            q_sum[...] += q_add
            u_sum[...] += u_add

        @pl.when(step == count - 1)
        def _():
            grad_ref[...] = jnp.zeros(grad_ref.shape, LOW)
            for z in range(shards):
                grad_ref[z, :, :query_wide] = q_sum[z * slab : (z + 1) * slab].astype(LOW)
                for i in range(up_cols // 128):
                    grad_ref[z, i * lat : (i + 1) * lat, query_wide:] = u_sum[
                        z * lat : (z + 1) * lat, i * 128 : (i + 1) * 128
                    ].astype(LOW)

    def tok(a):
        return pl.BlockSpec((rows, a.shape[1]), lambda b, dev_ref: (b, 0))

    def low_half(cols):
        return pl.BlockSpec((rows, cols), lambda b, dev_ref: (jnp.minimum(b, middle - 1), 0))

    def high_half(cols):
        return pl.BlockSpec((rows, cols), lambda b, dev_ref: (jnp.maximum(b - middle, 0), 0))

    arrays = [q_nope, q_rope, keyval, k_rope]
    return pl.pallas_call(
        kernel,
        grid_spec=pltpu.PrefetchScalarGridSpec(
            num_scalar_prefetch=1,
            grid=(count,),
            in_specs=[tok(a) for a in arrays]
            + [pl.BlockSpec((rows, given.shape[1]), lambda b, dev_ref: (dev_ref[b], 0))]
            + [tok(normed), tok(low), whole(query_up), whole(up_w), tok(cosine), tok(sine)]
            + [tok(seg_col), pl.BlockSpec((1, 1, rows), lambda b, dev_ref: (b, 0, 0))],
            out_specs=[low_half(model), high_half(model), low_half(wide), high_half(wide)]
            + [pl.BlockSpec(query_up.shape, lambda b, dev_ref: (0, 0, 0))],
            scratch_shapes=[pltpu.VMEM((model, query_wide), F32), pltpu.VMEM(up_w.shape, F32)],
        ),
        out_shape=[
            jax.ShapeDtypeStruct((total // 2, model), LOW),
            jax.ShapeDtypeStruct((total // 2, model), LOW),
            jax.ShapeDtypeStruct((total // 2, wide), LOW),
            jax.ShapeDtypeStruct((total // 2, wide), LOW),
            jax.ShapeDtypeStruct(query_up.shape, LOW),
        ],
        cost_estimate=cost(total * model * 6),
    )(devices, *arrays, given, normed, low, query_up, up_w, cosine, sine, seg_col, seg_row)


def experts(info, blocks, grad, counts, valid, small_w, gate_w, lower_w, is_expert):
    count = len(blocks)
    rows, model = blocks[0].shape
    hidden = gate_w.shape[1] // 2
    total = count * rows
    middle = count // 2
    lanes = counts.shape[1]
    router_at = small_w.shape[1] - lanes

    def kernel(info_ref, *refs):
        parts = refs[:count]
        grad_ref, counts_ref, valid_ref, sw_ref, gw_ref, lw_ref, ex_ref = refs[count : count + 7]
        (
            mixed_ref,
            hid_ref,
            dg_ref,
            dm_first,
            dm_second,
            out_first,
            out_second,
            dw_ref,
            sig_ref,
            held,
        ) = refs[count + 7 :]
        step = pl.program_id(0)
        for k in range(count):

            @pl.when(step == k)
            def _():
                held[...] = parts[k][...]

        mixed = held[...]
        mixed_ref[...] = mixed
        sig = jax.nn.sigmoid(dot(mixed, sw_ref[:, router_at:]))
        sig_count = sig * counts_ref[...].astype(F32)
        lane = lax.broadcasted_iota(jnp.int32, (rows, lanes), 1)
        picked = jnp.sum(jnp.where(lane == lanes - NEXP + info_ref[0], sig_count, 0.0), 1, keepdims=True)
        picked_total = jnp.sum(sig_count, 1, keepdims=True)
        weight = ROUTE_SCALE * picked / picked_total * valid_ref[...]

        @pl.when(step == 0)
        def _():
            sig_ref[...] = sig

        routed = ex_ref[...] > 0.0
        both = dot(mixed, gw_ref[...])
        gate = both[:, :hidden]
        lift = both[:, hidden:]
        d_hidden = dot_last(grad_ref[...], lw_ref[...])
        gate_sig = jax.nn.sigmoid(gate)
        gated = gate * gate_sig
        act = gated * lift
        wide = jnp.where(routed, weight, 1.0)
        hid = (act * wide).astype(LOW)
        hid_ref[...] = hid
        dw_ref[...] = jnp.sum(jnp.where(routed, act * d_hidden, 0.0), 1, keepdims=True)
        d_hidden = d_hidden * wide
        d_gate = (d_hidden * lift * gate_sig * (1.0 + gate * (1.0 - gate_sig))).astype(LOW)
        d_lift = (d_hidden * gated).astype(LOW)
        d_both = jnp.concatenate([d_gate, d_lift], 1)
        dg_ref[...] = d_both
        d_mixed = dot_last(d_both, gw_ref[...]).astype(LOW)
        out = dot(hid, lw_ref[...]).astype(LOW)

        @pl.when(step < middle)
        def _():
            dm_first[...] = d_mixed
            out_first[...] = out

        @pl.when(step >= middle)
        def _():
            dm_second[...] = d_mixed
            out_second[...] = out

    def tok(cols):
        return pl.BlockSpec((rows, cols), lambda b, info_ref: (b, 0))

    low_half = pl.BlockSpec((rows, model), lambda b, info_ref: (jnp.minimum(b, middle - 1), 0))
    high_half = pl.BlockSpec((rows, model), lambda b, info_ref: (jnp.maximum(b - middle, 0), 0))
    part = jax.ShapeDtypeStruct((total // 2, model), LOW)
    return pl.pallas_call(
        kernel,
        grid_spec=pltpu.PrefetchScalarGridSpec(
            num_scalar_prefetch=1,
            grid=(count,),
            in_specs=[whole(a) for a in blocks]
            + [tok(model), tok(lanes), tok(1)]
            + [whole(a) for a in (small_w, gate_w, lower_w, is_expert)],
            out_specs=[tok(model), tok(hidden), tok(2 * hidden)]
            + [low_half, high_half, low_half, high_half, tok(1)]
            + [pl.BlockSpec((rows, lanes), lambda b, info_ref: (0, 0))],
            scratch_shapes=[pltpu.VMEM((rows, model), LOW)],
        ),
        out_shape=[jax.ShapeDtypeStruct((total, model), LOW)]
        + [jax.ShapeDtypeStruct((total, w), LOW) for w in (hidden, 2 * hidden)]
        + [part] * 4
        + [jax.ShapeDtypeStruct((total, 1), F32), jax.ShapeDtypeStruct((rows, lanes), F32)],
        cost_estimate=cost(total * model * 12),
    )(info, *blocks, grad, counts, valid, small_w, gate_w, lower_w, is_expert)


def cost(size):
    return pl.CostEstimate(flops=0, bytes_accessed=size // 8, transcendentals=0)


def arrivals(steps, here, count):
    found = []
    for index, step in enumerate(steps):
        if step == "last":
            found.append((index, here == 0, count - 1))
            found.append((index, here == count - 1, 0))
        elif step == "above":
            found.append((index, here < count - 1, here + 1))
        elif step == "below":
            found.append((index, here > 0, here - 1))
        else:
            found.append((index, None, lax.rem(here + step, count)))
    return found


def each_arrival(steps, here, count, act):
    for index, condition, place in arrivals(steps, here, count):
        if condition is None:
            act(index, place)
        else:
            pl.when(condition)(functools.partial(act, index, place))


def scalars(*values):
    return jnp.stack([v.astype(jnp.int32) for v in values])


def shard_place(count, own, came, shard, start, size):
    steps = [k for k, _ in came]
    width = own.shape[1]
    tile = size
    while tile > 128 and tile % 2 == 0 and start % (tile // 2) == 0:
        tile //= 2

    def kernel(at_ref, own_ref, *refs):
        out = refs[-1]
        here = at_ref[0]
        out[here] = own_ref[...]

        def act(index, place):
            out[place] = refs[index][...]

        each_arrival(steps, here, count, act)

    return pl.pallas_call(
        kernel,
        grid_spec=pltpu.PrefetchScalarGridSpec(
            num_scalar_prefetch=1,
            grid=(size // tile,),
            in_specs=[pl.BlockSpec((tile, width), lambda b, at_ref: (b + start // tile, 0))]
            * (len(came) + 1),
            out_specs=pl.BlockSpec((count, tile, width), lambda b, at_ref: (0, b, 0)),
        ),
        out_shape=jax.ShapeDtypeStruct((count, size, width), LOW),
        cost_estimate=cost(4 * count * size * width),
    )(scalars(shard), own, *[piece for _, piece in came])


def strip_place(local, pieces, steps, shard, devices, start, tile):
    count = max(steps) + 1
    reps = len(pieces)
    rows, width = local.shape
    strip = pieces[0].shape[0] // len(steps)

    def kernel(at_ref, own_ref, *refs):
        out = refs[-1]
        here = at_ref[0]
        out[here] = own_ref[...]
        for j in range(reps):
            base = pl.multiple_of(at_ref[1 + j] * strip, strip)

            def act(index, place):
                out[place, pl.ds(base, strip)] = refs[j][index * strip : (index + 1) * strip]

            each_arrival(steps, here, count, act)

    return pl.pallas_call(
        kernel,
        grid_spec=pltpu.PrefetchScalarGridSpec(
            num_scalar_prefetch=1,
            grid=(width // tile,),
            in_specs=[pl.BlockSpec((rows, tile), lambda b, at_ref: (0, b))]
            + [
                pl.BlockSpec((pieces[0].shape[0], tile), lambda b, at_ref: (0, b + start // tile))
                for _ in pieces
            ],
            out_specs=pl.BlockSpec((count, rows, tile), lambda b, at_ref: (0, 0, b)),
        ),
        out_shape=jax.ShapeDtypeStruct((count, rows, width), LOW),
        cost_estimate=cost(4 * count * rows * width),
    )(jnp.concatenate([scalars(shard), devices]), local, *pieces).reshape(count * rows, width)


def merge_rows(blocks, act, extra, widths):
    rows = blocks[0].shape[0]
    count = len(blocks)
    outs = len(widths)

    def kernel(*refs):
        index = pl.program_id(0)
        more = [r[...] for r in refs[count:-outs]]
        for k in range(count):

            @pl.when(index == k)
            def _():
                for ref, value in zip(refs[-outs:], act(refs[k][...], *more)):
                    ref[...] = value

    return pl.pallas_call(
        kernel,
        grid=(count,),
        in_specs=[
            pl.BlockSpec(a.shape, lambda b: (0, 0), pipeline_mode=pl.Buffered(1)) for a in blocks
        ]
        + [pl.BlockSpec((rows, a.shape[1]), lambda b: (b, 0)) for a in extra],
        out_specs=[pl.BlockSpec((rows, w), lambda b: (b, 0)) for w in widths],
        out_shape=[jax.ShapeDtypeStruct((count * rows, w), LOW) for w in widths],
        cost_estimate=cost(count * rows * sum(widths) * 4),
    )(*blocks, *extra)


def assemble(blocks, devices, grid, block_shape, block_map, outs, place, weights=()):
    reps = len(blocks)
    count = len(weights)

    def kernel(dev_ref, *refs):
        held = refs[-1]
        out_refs = refs[reps + count : -1]
        for k in range(reps):
            held[dev_ref[k]] = refs[k][...].astype(F32)
        for j in range(reps):
            place(pl.program_id(0), j, held[j], out_refs)
        total = None
        for i in range(count):
            value = refs[reps + i][...].astype(F32) * out_refs[i][...]
            value = jnp.sum(value, -1, keepdims=True)
            if value.ndim == 3:
                value = jnp.sum(value, 0)
            total = value if total is None else total + value
        if count:
            out_refs[-1][...] = total

    specs = [
        pl.BlockSpec(shape, functools.partial(lambda m, b, dev_ref: m(b), where))
        for _, shape, where in outs
    ]
    sums = []
    if count:
        rows = outs[0][1][0]
        sums = [((grid * rows, 1), (rows, 1), lambda b: (b, 0))]
    return pl.pallas_call(
        kernel,
        grid_spec=pltpu.PrefetchScalarGridSpec(
            num_scalar_prefetch=1,
            grid=(grid,),
            in_specs=[pl.BlockSpec(block_shape, lambda b, dev_ref: block_map(b)) for _ in blocks]
            + specs[:count],
            out_specs=specs
            + [pl.BlockSpec(shape, lambda b, dev_ref: (b, 0)) for _, shape, _ in sums],
            scratch_shapes=[pltpu.VMEM((reps,) + block_shape, F32)],
        ),
        out_shape=[jax.ShapeDtypeStruct(shape, F32) for shape, _, _ in outs + sums],
        cost_estimate=cost(reps * blocks[0].size * 6),
    )(devices, *blocks, *weights)


def layouts(lengths, seq_owner, devices, rows):
    count = lengths.shape[0]
    mine = seq_owner[None, :] == devices[:, None]
    own_length = jnp.where(mine, lengths[None, :], 0)
    numbers = jnp.arange(count, dtype=jnp.int32)
    ahead = numbers[:, None] < numbers[None, :]
    starts = jnp.sum(jnp.where(ahead[None], own_length[:, :, None], 0), 1)[:, None, :]
    ends = starts + own_length[:, None, :]
    row = jnp.arange(rows, dtype=jnp.int32)[None, :, None]
    inside = mine[:, None, :] & (row >= starts) & (row < ends)
    valid = jnp.any(inside, 2, keepdims=True)
    segment = jnp.sum(jnp.where(inside, numbers, 0), 2, keepdims=True)
    position = row - jnp.sum(jnp.where(inside, starts, 0), 2, keepdims=True)
    return jnp.where(valid, segment, count), position, valid


def make_local(reps, shards):
    group = Group(reps, shards)
    heads = HEADS // reps
    half = 32 * heads
    width = 2 * half

    def local(
        tokens,
        cotangent,
        lengths,
        seq_owner,
        expert_ids,
        attention_gain,
        query_weight,
        latent_down,
        latent_gain,
        latent_up,
        output_weight,
        feedforward_gain,
        router_weight,
        shared_gate,
        shared_up,
        shared_down,
        expert_gate,
        expert_up,
        expert_down,
    ):
        rows, model = tokens.shape
        rep = lax.axis_index("rep")
        shard = lax.axis_index("shard")
        devices = group.devices(rep)
        slab = model // shards
        strip = slab // reps
        lat = latent_gain.shape[0]
        cut = group.half * rows

        x_gather = Gathering(group, tokens)
        x_gather.start()
        small = jnp.concatenate(
            [
                lax.dynamic_slice_in_dim(latent_down, rep * strip, strip, 0),
                lax.dynamic_slice_in_dim(router_weight, rep * strip, strip, 0),
            ],
            1,
        )
        small = lax.all_gather(small, ("shard", "rep"), axis=0, tiled=True)
        output_shift = Shifting(
            group, lax.dynamic_slice_in_dim(output_weight, rep * strip, strip, 0)
        )
        output_shift.start()

        query_cols = heads * (NOPE + ROPE)
        up_cols = heads * (NOPE + VDIM)
        query_wide = round_up(query_cols, 128)
        query_part = lax.dynamic_slice_in_dim(query_weight, rep * query_cols, query_cols, 1)
        if query_wide > query_cols:
            query_part = jnp.pad(query_part, ((0, 0), (0, query_wide - query_cols)))
        up_part = lax.dynamic_slice_in_dim(latent_up, rep * up_cols, up_cols, 1)
        up_part = fold(up_part, slab)
        gain_rows = jnp.concatenate([attention_gain, feedforward_gain, latent_gain])
        gain_lanes = query_wide + 128
        gain_count = round_up(gain_rows.shape[0], 16 * gain_lanes)
        gain_rows = jnp.pad(gain_rows, (0, gain_count - gain_rows.shape[0])).reshape(-1, gain_lanes)
        query_part = jnp.concatenate(
            [jnp.concatenate([query_part, up_part], 1), gain_rows], 0
        )
        query_shift = Shifting(group, query_part)
        query_shift.start()

        part_s = shared_down.shape[0] // reps
        local_e = expert_down.shape[1]
        part_e = WINDOW * local_e // reps
        per = reps // WINDOW
        my_expert = rep // per
        used = part_s + part_e
        hidden = round_up(shards * used, 128)
        unit = hidden // shards
        place = jnp.arange(hidden, dtype=jnp.int32)
        within = place % unit
        is_shared = within < part_s
        is_expert = (within >= part_s) & (within < used)
        from_shared = jnp.where(
            is_shared, (place // unit) * shared_down.shape[0] + rep * part_s + within, -1
        )
        from_expert = jnp.where(
            is_expert, (place // unit) * local_e + (rep % per) * part_e + within - part_s, -1
        )
        pick_s = (
            jnp.arange(shared_gate.shape[1], dtype=jnp.int32)[:, None] == from_shared[None, :]
        ).astype(LOW)
        pick_e = (
            jnp.arange(expert_gate.shape[2], dtype=jnp.int32)[:, None] == from_expert[None, :]
        ).astype(LOW)

        def my_columns(shared, expert):
            expert = lax.dynamic_index_in_dim(expert, my_expert, 0, keepdims=False)
            return (dot(shared, pick_s) + dot(expert, pick_e)).astype(LOW)

        gate_all = jnp.concatenate(
            [my_columns(shared_gate, expert_gate), my_columns(shared_up, expert_up)], 1
        )
        lower_part = jnp.concatenate(
            [
                lax.dynamic_slice_in_dim(shared_down, rep * part_s, part_s, 0),
                lax.dynamic_slice(
                    expert_down, (my_expert, (rep % per) * part_e, 0), (1, part_e, model)
                )[0],
                jnp.zeros((unit - used, model), LOW),
            ],
            0,
        )

        segment, position, valid = layouts(lengths, seq_owner, devices * shards + shard, rows)
        total_rows = reps * rows
        seg_col = segment.reshape(total_rows, 1)
        seg_row = segment.reshape(reps, 1, rows)
        valid_all = valid.reshape(total_rows, 1).astype(F32)
        valid_own = valid_all[:rows]
        frequency = jnp.power(ROPE_BASE, -2.0 * jnp.arange(32, dtype=F32) / ROPE)
        angles = position.reshape(total_rows, 1).astype(F32) * jnp.tile(frequency, 2 * heads)[None]
        cosine = jnp.cos(angles)
        side = jnp.where(jnp.arange(width) < half, -1.0, 1.0).astype(F32)
        sine = jnp.sin(angles) * side[None, :]

        hidden_in = tokens.astype(F32)
        counts = jnp.sum(
            (expert_ids[:, :, None] == jnp.arange(NEXP, dtype=jnp.int32)).astype(F32), 1
        )
        given = jnp.concatenate(
            [cotangent, jnp.zeros((rows, 128 - NEXP), LOW), counts.astype(LOW)], 1
        )

        phase(x_gather, query_shift, output_shift)
        x_gather.start()
        query_shift.start()
        output_shift.start()
        (gate_all,) = phase(x_gather, query_shift, output_shift, gate_all)
        gate_all = lax.all_gather(gate_all, "shard", axis=0, tiled=True)
        x_gather.start()
        output_came = output_shift.whole(shard)
        shard_steps = [k for k, _ in output_came]
        output_gather = Gathering(group, jnp.concatenate([piece for _, piece in output_came], 0))
        output_gather.start()
        query_up = shard_place(shards, query_part, query_shift.result(), shard, 0, slab)
        gains = shard_place(
            shards, query_part, query_shift.result(), shard, slab, gain_rows.shape[0]
        )
        gains = gains.reshape(shards, -1).astype(F32)
        attention_gain_all = gains[:, :slab].reshape(1, model)
        mixer_gain_all = gains[:, slab : 2 * slab].reshape(1, model)
        latent_gain_all = gains[:, 2 * slab : 2 * slab + lat].reshape(1, RANK)

        lane = jnp.arange(heads * width, dtype=jnp.int32)
        head = lane // width
        spot = lane % width
        source = jnp.where(
            (spot % half) // 32 == head, (spot // half) * 32 + spot % 32, -1
        )
        spread = (jnp.arange(ROPE, dtype=jnp.int32)[:, None] == source[None, :]).astype(LOW)
        cols = heads * VDIM
        normed_all, qn, qr, keyval, kr, latent_low, up_all, latent_own, attended = attend_forward(
            devices,
            x_gather.list(),
            attention_gain_all,
            latent_gain_all,
            query_up,
            heads,
            small,
            spread,
            cosine,
            sine,
            seg_col,
            seg_row,
        )
        attended, given, lower_part = phase(attended, output_gather, given, lower_part)
        output_gather.start()
        lower_all = lax.all_gather(lower_part, "shard", axis=0, tiled=True)
        attended_own = lax.all_to_all(
            attended.reshape(reps, rows, cols), "rep", 0, 0, tiled=True
        )
        (attended_own,) = phase(attended_own, output_gather)
        output_gather.start()
        given_gather = Gathering(group, given)
        given_gather.start()
        output_all = strip_place(
            output_weight, output_gather.list(), shard_steps, shard, devices, 0, 256
        )
        attended_own = jnp.transpose(attended_own, (1, 0, 2)).reshape(rows, HEADS * VDIM)
        mid = hidden_in + dot(attended_own, output_all)
        mixed_scale = rms_scale(mid)
        mixed = (mid * mixed_scale * mixer_gain_all).astype(LOW)

        mixed_gather = Gathering(group, mixed)
        mixed_gather.start()
        (gate_all,) = phase(mixed_gather, given_gather, gate_all)
        mixed_gather.start()
        given_gather.start()
        phase(mixed_gather, given_gather)
        mixed_gather.start()
        given_gather.start()
        grad_all, counts_all = merge_rows(
            given_gather.list(),
            lambda block, ok: (
                (block[:, :model].astype(F32) * ok).astype(LOW),
                block[:, model:],
            ),
            [valid_all],
            [model, 128],
        )
        grad_all, counts_all = phase(mixed_gather, grad_all, counts_all)
        (
            mixed_all,
            hidden_low,
            d_both,
            d_mixed_first,
            d_mixed_second,
            ffn_first,
            ffn_second,
            d_weight,
            sig_own,
        ) = experts(
            jnp.reshape(my_expert, (1,)).astype(jnp.int32),
            mixed_gather.list(),
            grad_all,
            counts_all,
            valid_all,
            small,
            gate_all,
            lower_all,
            is_expert.astype(F32)[None, :],
        )
        sig_own = sig_own[:, -NEXP:]
        mixed_sum = Reducing(group, d_mixed_second, d_mixed_first)
        mixed_sum.start()
        both_grad = dot_rows(mixed_all, d_both).astype(LOW)
        ffn_second, d_weight, hidden_low, _ = phase(
            mixed_sum, ffn_second, d_weight, hidden_low, both_grad
        )
        mixed_sum.start()
        numbers = jnp.arange(reps, dtype=jnp.int32)
        by_device = jnp.sum(
            jnp.where(
                (devices[None, :] == numbers[:, None])[:, :, None],
                d_weight.reshape(1, reps, rows),
                0.0,
            ),
            1,
        )
        d_weight_own = lax.all_to_all(by_device, "rep", 0, 0, tiled=True)
        d_weight_own = jnp.sum(d_weight_own.reshape(WINDOW, per, rows), 1)
        ffn_sum = Reducing(group, ffn_second, ffn_first)
        ffn_sum.start()
        hidden_low, d_weight_own = phase(mixed_sum, ffn_sum, hidden_low, d_weight_own)
        both_grad = lax.psum_scatter(both_grad, "shard", scatter_dimension=0, tiled=True)
        mixed_sum.start()
        lower_grad = dot_rows(hidden_low, grad_all).astype(LOW)
        phase(mixed_sum, lower_grad)
        lower_grad = lax.psum_scatter(lower_grad, "shard", scatter_dimension=0, tiled=True)[:used]
        d_mixed = mixed_sum.total()

        total_own = jnp.sum(sig_own * counts, 1, keepdims=True)
        hit = counts[:, :WINDOW]
        d_route = jnp.concatenate(
            [valid_own * d_weight_own.T * hit, jnp.zeros((rows, NEXP - WINDOW), F32)], 1
        )
        inner = jnp.sum(d_route * sig_own, 1, keepdims=True)
        d_sig = ROUTE_SCALE * (d_route / total_own - counts * inner / (total_own * total_own))
        d_logits = (d_sig * sig_own * (1.0 - sig_own)).astype(LOW)
        d_mixed = d_mixed + dot_last(d_logits, small[:, RANK + ROPE :])
        grad_own = cotangent.astype(F32) * valid_own
        d_mid = grad_own + rms_back(mid, mixed_scale, mixer_gain_all, d_mixed)
        d_branch = d_mid.astype(LOW)

        out_cols = model // reps

        def output_part(index):
            picked = [
                lax.dynamic_slice_in_dim(d_branch, devices[k] * out_cols, out_cols, 1)
                for k in index
            ]
            return dot_rows(attended_own, jnp.concatenate(picked, 1)).astype(LOW)

        output_sum = Reducing(
            group,
            output_part(range(group.half, reps)),
            output_part(range(group.half)),
            axis=1,
        )
        output_sum.start()

        d_attended = dot_last(d_branch, output_all).astype(LOW)
        d_attended = jnp.transpose(d_attended.reshape(rows, reps, cols), (1, 0, 2))
        d_attended = lax.all_to_all(d_attended, "rep", 0, 0, tiled=True)
        (d_attended,) = phase(d_attended, output_sum)
        output_sum.start()
        ffn_sum.start()
        d_attended = d_attended.reshape(total_rows, cols)
        (
            d_normed_first,
            d_normed_second,
            latent_first,
            latent_second,
            attention_grad,
        ) = attend_backward(
            devices,
            (qn, qr, keyval, kr),
            d_attended,
            normed_all,
            latent_low,
            query_up,
            up_all,
            cosine,
            sine,
            seg_col,
            seg_row,
            rows,
        )
        latent_second, d_normed_second = phase(
            latent_second, d_normed_second, output_sum, ffn_sum
        )
        attention_grad = lax.psum_scatter(
            attention_grad, "shard", scatter_dimension=0, tiled=True
        ).reshape(slab, query_wide + 128)
        latent_sum = Reducing(group, latent_second, latent_first)
        latent_sum.start()
        output_sum.start()
        both_gather = Gathering(group, both_grad, early=True)
        both_gather.start()
        (d_normed_second,) = phase(latent_sum, d_normed_second)
        latent_sum.start()
        normed_sum = Reducing(group, d_normed_second, d_normed_first)
        normed_sum.start()
        phase(latent_sum, output_sum)
        latent_sum.start()
        output_grad = lax.psum_scatter(
            output_sum.total().astype(LOW), "shard", scatter_dimension=0, tiled=True
        )
        phase(latent_sum)
        d_latent_sum = latent_sum.total()
        compressed = latent_own[:, :RANK]
        d_compressed = rms_back(
            compressed, rms_scale(compressed), latent_gain_all, d_latent_sum[:, :RANK]
        )
        kg_first = d_latent_sum[:, RANK : RANK + 32]
        kg_second = d_latent_sum[:, RANK + 32 : RANK + ROPE]
        cos_own = cosine[:rows, :32]
        sin_own = sine[:rows, half : half + 32]
        d_latent = jnp.concatenate(
            [
                d_compressed,
                kg_first * cos_own + kg_second * sin_own,
                kg_second * cos_own - kg_first * sin_own,
            ],
            1,
        ).astype(LOW)
        row_gather = Gathering(group, jnp.concatenate([d_latent, d_logits], 1))
        row_gather.start()
        (lower_grad,) = phase(row_gather, both_gather, lower_grad)
        row_gather.start()
        both_gather.start()
        phase(row_gather, normed_sum)
        row_gather.start()
        normed_sum.start()
        (attention_grad,) = phase(row_gather, both_gather, attention_grad)
        both_gather.start()
        lower_gather = Gathering(group, lower_grad)
        lower_gather.start()
        rows_given = row_gather.list()
        d_down = dot_last(d_latent, small[:, : RANK + ROPE])
        (row_grads,) = merge_rows(
            rows_given,
            lambda block: (block,),
            [],
            [RANK + ROPE + NEXP],
        )

        def my_strip(values):
            return jnp.concatenate(
                [
                    lax.dynamic_slice_in_dim(values, s * slab + rep * strip, strip, 1)
                    for s in range(shards)
                ],
                1,
            )

        strip_grad = jnp.concatenate(
            [
                dot_rows(my_strip(normed_all), row_grads[:, : RANK + ROPE]),
                dot_rows(my_strip(mixed_all), row_grads[:, RANK + ROPE :]),
            ],
            1,
        ).astype(LOW)

        strip_sum = lax.psum_scatter(strip_grad, "shard", scatter_dimension=0, tiled=True)
        tile = min(slab, 64)

        def place_columns(step, j, block, refs):
            for side in (0, 1):
                for s in range(shards):
                    base = side * hidden + s * unit
                    at = s * part_s * reps + j * part_s
                    refs[2 * side][:, at : at + part_s] = block[:, base : base + part_s]
                    at = s * part_e * per + (j % per) * part_e
                    refs[2 * side + 1][j // per, :, at : at + part_e] = block[
                        :, base + part_s : base + used
                    ]

        wide_s = shared_gate.shape
        wide_e = expert_gate.shape
        sgate_grad, egate_grad, sup_grad, eup_grad, mixer_sum = assemble(
            both_gather.list(),
            devices,
            slab // tile,
            (tile, 2 * hidden),
            lambda b: (b, 0),
            [
                (wide_s, (tile, wide_s[1]), lambda b: (b, 0)),
                (wide_e, (WINDOW, tile, wide_e[2]), lambda b: (0, b, 0)),
            ]
            * 2,
            place_columns,
            (shared_gate, expert_gate, shared_up, expert_up),
        )

        _, _, output_grad = phase(lower_gather, strip_grad, sgate_grad, output_grad)
        lower_gather.start()
        query_gather = Gathering(group, attention_grad)
        query_gather.start()
        phase(lower_gather, query_gather, normed_sum)
        lower_gather.start()
        query_gather.start()
        normed_sum.start()
        ffn_sum.start()
        output_gather = Gathering(group, output_grad)
        output_gather.start()
        (strip_sum,) = phase(lower_gather, query_gather, output_gather, strip_sum)
        query_gather.start()
        output_gather.start()
        strip_gather = Gathering(group, strip_sum)
        strip_gather.start()
        def place_rows(step, j, block, refs):
            refs[0][j * part_s : (j + 1) * part_s] = block[:part_s]
            at = (j % per) * part_e
            refs[1][j // per, at : at + part_e] = block[part_s:]

        lane_tile = 256
        sdown_grad, edown_grad = assemble(
            lower_gather.list(),
            devices,
            model // lane_tile,
            (used, lane_tile),
            lambda b: (0, b),
            [
                (shared_down.shape, (shared_down.shape[0], lane_tile), lambda b: (0, b)),
                (expert_down.shape, (WINDOW, local_e, lane_tile), lambda b: (0, 0, b)),
            ],
            place_rows,
        )

        phase(
            query_gather, output_gather, strip_gather, sdown_grad, normed_sum, ffn_sum
        )
        output_gather.start()
        strip_gather.start()
        layer_out = (valid_own * (mid + ffn_sum.total())).astype(LOW)
        d_normed = normed_sum.total() + d_down
        token_grad = d_mid + rms_back(
            hidden_in, rms_scale(hidden_in), attention_gain_all, d_normed
        )

        def place_attention(step, j, block, refs):
            refs[0][:, j * query_cols : (j + 1) * query_cols] = block[:, :query_cols]

            @pl.when(step < up_cols // 128)
            def _():
                at = pl.multiple_of(j * up_cols + step * 128, 128)
                refs[1][:, pl.ds(at, 128)] = block[:, query_wide:]

        query_grad, up_grad, query_sum = assemble(
            query_gather.list(),
            devices,
            slab // lat,
            (lat, query_wide + 128),
            lambda b: (b, 0),
            [
                (query_weight.shape, (lat, query_weight.shape[1]), lambda b: (b, 0)),
                (latent_up.shape, latent_up.shape, lambda b: (0, 0)),
            ],
            place_attention,
            (query_weight,),
        )

        def place_output(step, j, block, refs):
            refs[0][:, j * out_cols : (j + 1) * out_cols] = block

        phase(output_gather, strip_gather, query_grad)
        strip_gather.start()
        (output_grad,) = assemble(
            output_gather.list(),
            devices,
            slab // lat,
            (lat, out_cols),
            lambda b: (b, 0),
            [(output_weight.shape, (lat, model), lambda b: (b, 0))],
            place_output,
        )

        def place_strip(step, j, block, refs):
            refs[0][:, j * strip : (j + 1) * strip] = block[:, : RANK + ROPE].T
            refs[1][:, j * strip : (j + 1) * strip] = block[:, RANK + ROPE :].T

        down_grad, router_grad = assemble(
            strip_gather.list(),
            devices,
            1,
            (strip, RANK + ROPE + NEXP),
            lambda b: (0, 0),
            [
                ((RANK + ROPE, slab), (RANK + ROPE, slab), lambda b: (0, 0)),
                ((NEXP, slab), (NEXP, slab), lambda b: (0, 0)),
            ],
            place_strip,
        )

        down_grad = down_grad.T
        router_grad = router_grad.T

        def row_sum(weight, grad):
            return jnp.sum(weight.astype(F32) * grad, -1)

        attention_gain_grad = (
            query_sum[:, 0] + row_sum(latent_down, down_grad)
        ) / attention_gain.astype(F32)
        latent_gain_grad = row_sum(latent_up, up_grad) / latent_gain.astype(F32)
        mixer_gain_grad = (
            row_sum(router_weight, router_grad) + mixer_sum[:, 0]
        ) / feedforward_gain.astype(F32)

        return (
            layer_out,
            token_grad,
            attention_gain_grad,
            query_grad,
            down_grad,
            latent_gain_grad,
            up_grad,
            output_grad,
            mixer_gain_grad,
            router_grad,
            sgate_grad,
            sup_grad,
            sdown_grad,
            egate_grad,
            eup_grad,
            edown_grad,
        )

    return local


def fold(value, rows):
    count = value.shape[1] // 128
    parts = [value[:, i * 128 : (i + 1) * 128] for i in range(count)]
    left = rows - count * value.shape[0]
    if left:
        parts.append(jnp.zeros((left, 128), value.dtype))
    return jnp.concatenate(parts, 0)


def solution(mesh):
    tokens = P(("rep", "shard"), None)
    vector = P("shard")
    matrix = P("shard", None)
    stack = P(None, "shard", None)
    in_specs = (
        (tokens, tokens, P(), P(), tokens, vector, matrix, matrix, vector, matrix, matrix, vector)
        + (matrix,) * 4
        + (stack,) * 3
    )
    out_specs = (
        (tokens, tokens, vector, matrix, matrix, vector, matrix, matrix, vector)
        + (matrix,) * 4
        + (stack,) * 3
    )
    local = make_local(mesh.shape["rep"], mesh.shape["shard"])
    return jax.shard_map(local, mesh=mesh, in_specs=in_specs, out_specs=out_specs, check_vma=False)
```

```python
import functools

import jax
import jax.numpy as jnp
from jax import lax
from jax.experimental import pallas as pl
from jax.experimental.pallas import tpu as pltpu
from jax.sharding import PartitionSpec as P

HEADS = 16
NOPE = 128
ROPE = 64
VDIM = 128
RANK = 512
NEXP = 64
WINDOW = 2

EPSILON = 1e-06
ROPE_BASE = 50000.0
ROUTE_SCALE = 2.446
NEG_FILL = -1e30
SCORE_SCALE = (NOPE + ROPE) ** (-0.5)

F32 = jnp.float32
LOW = jnp.bfloat16


def dot(left, right):
    return jnp.dot(left, right, preferred_element_type=F32)


def dot_rows(left, right):
    return lax.dot_general(left, right, (((0,), (0,)), ((), ())), preferred_element_type=F32)


def dot_last(left, right):
    return lax.dot_general(left, right, (((1,), (1,)), ((), ())), preferred_element_type=F32)


def rms_scale(values):
    return lax.rsqrt(jnp.mean(values * values, -1, keepdims=True) + EPSILON)


def rms_back(values, scale, gain, upstream):
    gained = upstream * gain
    inner = jnp.mean(values * gained, -1, keepdims=True)
    return scale * gained - values * scale * scale * scale * inner


def round_up(value, unit):
    return -(-value // unit) * unit


class Group:
    def __init__(self, reps, shards):
        self.reps = reps
        self.shards = shards
        bits = reps.bit_length() - 1
        assert bits >= 1 and 1 << bits == reps
        self.levels = [(1 << b, 1 << (bits - b)) for b in range(1, bits)]
        self.half = reps // 2

    def devices(self, rep):
        lists = []
        for side in (0, 1):
            masks = [0]
            for level in self.levels:
                masks = masks + [m ^ level[side] for m in masks]
            lists.append(masks)
        first = lists[0] + [m ^ 1 for m in lists[1]]
        second = lists[1] + [m ^ 1 for m in lists[0]]
        masks = jnp.where(
            rep % 2 == 0, jnp.array(first, jnp.int32), jnp.array(second, jnp.int32)
        )
        return rep.astype(jnp.int32) ^ masks

    def cross(self, value, level):
        pairs = [(i, i ^ level[i & 1]) for i in range(self.reps)]
        return lax.ppermute(value, "rep", pairs)


class Gathering:
    def __init__(self, group, block, early=False):
        self.group = group
        self.blocks = {0: block}
        self.stage = 0
        self.pending = {}
        self.early = early

    def start(self):
        group = self.group
        self.stage += 1
        if self.stage <= len(group.levels):
            for k in range(group.half):
                if bin(k).count("1") == self.stage:
                    top = k.bit_length() - 1
                    self.pending[k] = group.cross(self.blocks[k ^ (1 << top)], group.levels[top])
        last = self.stage == len(group.levels) + 1
        for k in range(group.half):
            fresh = bin(k).count("1") == self.stage - 1
            if (self.early and fresh) or (last and not self.early):
                self.pending[group.half + k] = group.cross(self.blocks[k], (1, 1))

    def settle(self, values):
        self.blocks.update(zip(self.pending, values))
        self.pending = {}

    def list(self):
        while True:
            self.settle(list(self.pending.values()))
            if len(self.blocks) == self.group.reps:
                return [self.blocks[k] for k in range(self.group.reps)]
            self.start()


class Reducing:
    def __init__(self, group, second, first, axis=0):
        self.group = group
        self.second = second
        self.terms = [first]
        self.axis = axis
        self.size = first.shape[axis]
        self.stage = 0
        self.pending = {}

    def cut(self, start, size):
        total = None
        for term in self.terms:
            term = lax.slice_in_dim(term, start, start + size, axis=self.axis).astype(F32)
            total = term if total is None else total + term
        return total

    def start(self):
        levels = self.group.levels
        if self.stage == 0:
            self.pending[0] = self.group.cross(self.second, (1, 1))
        elif self.stage <= len(levels):
            self.size //= 2
            sent = self.cut(self.size, self.size).astype(LOW)
            self.sent = sent
            self.pending[0] = self.group.cross(sent, levels[len(levels) - self.stage])
        self.stage += 1

    def settle(self, values):
        self.terms += values
        self.pending = {}

    def total(self):
        while True:
            self.settle(list(self.pending.values()))
            if self.stage > len(self.group.levels):
                return self.cut(0, self.size)
            self.start()


class Shifting:
    def __init__(self, group, block):
        self.count = group.shards
        self.block = block
        self.found = {}
        self.stage = 0
        self.pending = {}

    def start(self):
        count = self.count
        self.stage += 1

        def cycle(step):
            return [((i + step) % count, i) for i in range(count)]

        def move(value, pairs):
            return lax.ppermute(value, "shard", pairs)

        if count != 4:
            if self.stage == 1:
                self.pending = {k: move(self.block, cycle(k)) for k in range(1, count)}
        elif self.stage == 1:
            self.pending = {
                2: move(self.block, cycle(2)),
                "above": move(self.block, cycle(1)[:-1]),
                "below": move(self.block, cycle(3)[1:]),
            }
        elif self.stage == 2:
            self.pending = {"last": move(self.found[2], [(1, 0), (2, 3)])}

    def settle(self, values):
        self.found.update(zip(self.pending, values))
        self.pending = {}

    def result(self):
        self.settle(list(self.pending.values()))
        while self.stage < 2:
            self.start()
            self.settle(list(self.pending.values()))
        return list(self.found.items())

    def whole(self, position):
        found = dict(self.result())
        if self.count == 4:
            last = found.pop("last")
            found[1] = jnp.where(position == self.count - 1, last, found.pop("above"))
            found[3] = jnp.where(position == 0, last, found.pop("below"))
        return [(k, found[k]) for k in range(1, self.count)]


def phase(*items):
    values = []
    for item in items:
        values += list(item.pending.values()) if hasattr(item, "pending") else [item]
    values = list(lax.optimization_barrier(tuple(values)))
    arrays = []
    for item in items:
        if hasattr(item, "pending"):
            count = len(item.pending)
            item.settle(values[:count])
            values = values[count:]
        else:
            arrays.append(values.pop(0))
    return arrays


def head_probs(h, allowed, q_nope, q_rope, keyval, k_rope):
    width = q_rope.shape[1]
    base = h * (NOPE + VDIM)
    scores = dot_last(q_nope[:, h * NOPE : (h + 1) * NOPE], keyval[:, base : base + NOPE])
    scores = scores + dot_last(q_rope, k_rope[:, h * width : (h + 1) * width])
    scores = jnp.where(allowed, scores * SCORE_SCALE, NEG_FILL)
    unnormed = jnp.exp(scores - jnp.max(scores, -1, keepdims=True))
    return unnormed / jnp.sum(unnormed, -1, keepdims=True)


def same_segment(sc_ref, sr_ref):
    rows = sc_ref.shape[0]
    t = lax.broadcasted_iota(jnp.int32, (rows, rows), 0)
    u = lax.broadcasted_iota(jnp.int32, (rows, rows), 1)
    return (sc_ref[...] == sr_ref[0]) & (u <= t)


def turned(values):
    half = values.shape[1] // 2
    return jnp.concatenate([values[:, half:], values[:, :half]], 1)


def whole(a):
    return pl.BlockSpec(a.shape, lambda b, dev_ref: (0,) * a.ndim, pipeline_mode=pl.Buffered(1))


def attend_forward(
    devices, blocks, gain, latent_gain, query_up, heads, small_w, spread, cosine, sine, seg_col, seg_row
):
    count = len(blocks)
    rows, model = blocks[0].shape
    shards, slab, lanes = query_up.shape
    query_wide = lanes - 128
    lat = RANK // shards
    up_cols = heads * (NOPE + VDIM)
    half = 32 * heads
    width = 2 * half

    def kernel(dev_ref, *refs):
        parts = refs[:count]
        gain_ref, lgain_ref, qu_ref, sw_ref, spread_ref, cos_ref, sin_ref, sc_ref, sr_ref = (
            refs[count : count + 9]
        )
        normed_ref, qn_ref, qr_ref, kv_ref, kr_ref, low_ref, up_ref, own_ref, out_ref, held = refs[
            count + 9 :
        ]
        step = pl.program_id(0)
        for k in range(count):

            @pl.when(step == k)
            def _():
                held[...] = parts[k][...]

        @pl.when(step == 0)
        def _():
            for z in range(shards):
                for i in range(up_cols // 128):
                    up_ref[z * lat : (z + 1) * lat, i * 128 : (i + 1) * 128] = qu_ref[
                        z, i * lat : (i + 1) * lat, query_wide:
                    ]

        x = held[...].astype(F32)
        normed = (x * rms_scale(x) * gain_ref[...]).astype(LOW)
        normed_ref[...] = normed
        query = dot(normed, qu_ref[:, :, :query_wide].reshape(model, query_wide))
        at = [h * (NOPE + ROPE) for h in range(heads)]
        q_nope = jnp.concatenate([query[:, i : i + NOPE] for i in at], 1).astype(LOW)
        q_rope = jnp.concatenate(
            [query[:, i + NOPE + c : i + NOPE + c + 32] for c in (0, 32) for i in at], 1
        )
        cos = cos_ref[...]
        sin = sin_ref[...]
        q_rope = (q_rope * cos + turned(q_rope) * sin).astype(LOW)
        latent = dot(normed, sw_ref[...])

        @pl.when(step == 0)
        def _():
            own_ref[...] = latent

        compressed = latent[:, :RANK]
        low = (compressed * rms_scale(compressed) * lgain_ref[...]).astype(LOW)
        key = latent[:, RANK : RANK + ROPE]
        key = key * cos[:, :ROPE] + turned(key) * sin[:, half - 32 : half + 32]
        k_rope = dot(key.astype(LOW), spread_ref[...]).astype(LOW)
        keyval = dot(low, up_ref[...]).astype(LOW)
        qn_ref[...] = q_nope
        qr_ref[...] = q_rope
        kv_ref[...] = keyval
        kr_ref[...] = k_rope
        low_ref[...] = low
        allowed = same_segment(sc_ref, sr_ref)
        for h in range(heads):
            probs = head_probs(h, allowed, q_nope, q_rope, keyval, k_rope)
            base = h * (NOPE + VDIM) + NOPE
            out_ref[:, h * VDIM : (h + 1) * VDIM] = dot(
                probs.astype(LOW), keyval[:, base : base + VDIM]
            ).astype(LOW)

    def tok(cols):
        return pl.BlockSpec((rows, cols), lambda b, dev_ref: (b, 0))

    total = count * rows
    widths = [model, heads * NOPE, width, heads * (NOPE + VDIM), heads * width, RANK]
    return pl.pallas_call(
        kernel,
        grid_spec=pltpu.PrefetchScalarGridSpec(
            num_scalar_prefetch=1,
            grid=(count,),
            in_specs=[whole(a) for a in blocks]
            + [whole(a) for a in (gain, latent_gain, query_up, small_w, spread)]
            + [tok(width), tok(width), tok(1)]
            + [pl.BlockSpec((1, 1, rows), lambda b, dev_ref: (b, 0, 0))],
            out_specs=[tok(w) for w in widths]
            + [
                pl.BlockSpec((RANK, up_cols), lambda b, dev_ref: (0, 0)),
                pl.BlockSpec((rows, small_w.shape[1]), lambda b, dev_ref: (0, 0)),
            ]
            + [pl.BlockSpec((rows, heads * VDIM), lambda b, dev_ref: (dev_ref[b], 0))],
            scratch_shapes=[pltpu.VMEM((rows, model), LOW)],
        ),
        out_shape=[jax.ShapeDtypeStruct((total, w), LOW) for w in widths]
        + [
            jax.ShapeDtypeStruct((RANK, up_cols), LOW),
            jax.ShapeDtypeStruct((rows, small_w.shape[1]), F32),
        ]
        + [jax.ShapeDtypeStruct((total, heads * VDIM), LOW)],
        cost_estimate=cost(total * model * 6),
    )(devices, *blocks, gain, latent_gain, query_up, small_w, spread, cosine, sine, seg_col, seg_row)


def attend_backward(
    devices, kept, given, normed, low, query_up, up_w, cosine, sine, seg_col, seg_row, rows
):
    q_nope, q_rope, keyval, k_rope = kept
    total, model = normed.shape
    count = total // rows
    heads = up_w.shape[1] // (NOPE + VDIM)
    half = 32 * heads
    width = 2 * half
    nope = heads * NOPE
    middle = count // 2
    shards, slab, lanes = query_up.shape
    query_wide = lanes - 128
    lat = RANK // shards
    up_cols = up_w.shape[1]
    wide = RANK + round_up(ROPE, 128)

    def kernel(
        dev_ref,
        qn_ref,
        qr_ref,
        kv_ref,
        kr_ref,
        da_ref,
        n_ref,
        low_ref,
        qu_ref,
        uw_ref,
        cos_ref,
        sin_ref,
        sc_ref,
        sr_ref,
        first_ref,
        second_ref,
        lat_first_ref,
        lat_second_ref,
        grad_ref,
        q_sum,
        u_sum,
    ):
        step = pl.program_id(0)
        allowed = same_segment(sc_ref, sr_ref)
        qn = qn_ref[...]
        qr = qr_ref[...]
        kv = kv_ref[...]
        kr = kr_ref[...]
        d_rope = None
        d_key = None
        d_nope = []
        d_keyval = []
        for h in range(heads):
            probs = head_probs(h, allowed, qn, qr, kv, kr)
            base = h * (NOPE + VDIM)
            keys = kv[:, base : base + NOPE]
            values = kv[:, base + NOPE : base + NOPE + VDIM]
            d_att = da_ref[:, h * VDIM : (h + 1) * VDIM]
            d_values = dot_rows(probs.astype(LOW), d_att)
            d_probs = dot_last(d_att, values)
            inner = jnp.sum(probs * d_probs, -1, keepdims=True)
            d_scores = (probs * (d_probs - inner)).astype(LOW)
            d_nope.append((dot(d_scores, keys) * SCORE_SCALE).astype(LOW))
            rope = dot(d_scores, kr[:, h * width : (h + 1) * width])
            d_rope = rope if d_rope is None else d_rope + rope
            d_keys = dot_rows(d_scores, qn[:, h * NOPE : (h + 1) * NOPE]) * SCORE_SCALE
            d_keyval += [d_keys.astype(LOW), d_values.astype(LOW)]
            turn = dot_rows(d_scores, qr)
            turn = jnp.concatenate(
                [turn[:, 32 * h : 32 * h + 32], turn[:, half + 32 * h : half + 32 * h + 32]], 1
            )
            d_key = turn if d_key is None else d_key + turn
        d_rope = d_rope * SCORE_SCALE
        d_rope = (d_rope * cos_ref[...] - turned(d_rope) * sin_ref[...]).astype(LOW)
        pieces = []
        for h in range(heads):
            pieces += [d_nope[h], d_rope[:, 32 * h : 32 * h + 32]]
            pieces.append(d_rope[:, half + 32 * h : half + 32 * h + 32])
        if query_wide > heads * (NOPE + ROPE):
            pieces.append(jnp.zeros((rows, query_wide - heads * (NOPE + ROPE)), LOW))
        d_query = jnp.concatenate(pieces, 1)
        d_keyval = jnp.concatenate(d_keyval, 1)
        d_key = (d_key * SCORE_SCALE).astype(LOW)
        d_key = jnp.concatenate([d_key, jnp.zeros((rows, wide - RANK - ROPE), LOW)], 1)
        d_normed = dot_last(
            d_query, qu_ref[:, :, :query_wide].reshape(model, query_wide)
        ).astype(LOW)
        d_low = dot_last(d_keyval, uw_ref[...]).astype(LOW)

        @pl.when(step < middle)
        def _():
            first_ref[...] = d_normed
            lat_first_ref[:, :RANK] = d_low
            lat_first_ref[:, RANK:] = d_key

        @pl.when(step >= middle)
        def _():
            second_ref[...] = d_normed
            lat_second_ref[:, :RANK] = d_low
            lat_second_ref[:, RANK:] = d_key

        q_add = dot_rows(n_ref[...], d_query)
        u_add = dot_rows(low_ref[...], d_keyval)

        @pl.when(step == 0)
        def _():
            q_sum[...] = q_add
            u_sum[...] = u_add

        @pl.when(step > 0)
        def _():
            q_sum[...] += q_add
            u_sum[...] += u_add

        @pl.when(step == count - 1)
        def _():
            grad_ref[...] = jnp.zeros(grad_ref.shape, LOW)
            for z in range(shards):
                grad_ref[z, :, :query_wide] = q_sum[z * slab : (z + 1) * slab].astype(LOW)
                for i in range(up_cols // 128):
                    grad_ref[z, i * lat : (i + 1) * lat, query_wide:] = u_sum[
                        z * lat : (z + 1) * lat, i * 128 : (i + 1) * 128
                    ].astype(LOW)

    def tok(a):
        return pl.BlockSpec((rows, a.shape[1]), lambda b, dev_ref: (b, 0))

    def low_half(cols):
        return pl.BlockSpec((rows, cols), lambda b, dev_ref: (jnp.minimum(b, middle - 1), 0))

    def high_half(cols):
        return pl.BlockSpec((rows, cols), lambda b, dev_ref: (jnp.maximum(b - middle, 0), 0))

    arrays = [q_nope, q_rope, keyval, k_rope]
    return pl.pallas_call(
        kernel,
        grid_spec=pltpu.PrefetchScalarGridSpec(
            num_scalar_prefetch=1,
            grid=(count,),
            in_specs=[tok(a) for a in arrays]
            + [pl.BlockSpec((rows, given.shape[1]), lambda b, dev_ref: (dev_ref[b], 0))]
            + [tok(normed), tok(low), whole(query_up), whole(up_w), tok(cosine), tok(sine)]
            + [tok(seg_col), pl.BlockSpec((1, 1, rows), lambda b, dev_ref: (b, 0, 0))],
            out_specs=[low_half(model), high_half(model), low_half(wide), high_half(wide)]
            + [pl.BlockSpec(query_up.shape, lambda b, dev_ref: (0, 0, 0))],
            scratch_shapes=[pltpu.VMEM((model, query_wide), F32), pltpu.VMEM(up_w.shape, F32)],
        ),
        out_shape=[
            jax.ShapeDtypeStruct((total // 2, model), LOW),
            jax.ShapeDtypeStruct((total // 2, model), LOW),
            jax.ShapeDtypeStruct((total // 2, wide), LOW),
            jax.ShapeDtypeStruct((total // 2, wide), LOW),
            jax.ShapeDtypeStruct(query_up.shape, LOW),
        ],
        cost_estimate=cost(total * model * 6),
    )(devices, *arrays, given, normed, low, query_up, up_w, cosine, sine, seg_col, seg_row)


def experts(info, blocks, grad, counts, valid, small_w, gate_w, lower_w, is_expert):
    count = len(blocks)
    rows, model = blocks[0].shape
    hidden = gate_w.shape[1] // 2
    total = count * rows
    middle = count // 2
    lanes = counts.shape[1]
    router_at = small_w.shape[1] - lanes

    def kernel(info_ref, *refs):
        parts = refs[:count]
        grad_ref, counts_ref, valid_ref, sw_ref, gw_ref, lw_ref, ex_ref = refs[count : count + 7]
        (
            mixed_ref,
            hid_ref,
            dg_ref,
            dm_first,
            dm_second,
            out_first,
            out_second,
            dw_ref,
            sig_ref,
            held,
        ) = refs[count + 7 :]
        step = pl.program_id(0)
        for k in range(count):

            @pl.when(step == k)
            def _():
                held[...] = parts[k][...]

        mixed = held[...]
        mixed_ref[...] = mixed
        sig = jax.nn.sigmoid(dot(mixed, sw_ref[:, router_at:]))
        sig_count = sig * counts_ref[...].astype(F32)
        lane = lax.broadcasted_iota(jnp.int32, (rows, lanes), 1)
        picked = jnp.sum(jnp.where(lane == lanes - NEXP + info_ref[0], sig_count, 0.0), 1, keepdims=True)
        picked_total = jnp.sum(sig_count, 1, keepdims=True)
        weight = ROUTE_SCALE * picked / picked_total * valid_ref[...]

        @pl.when(step == 0)
        def _():
            sig_ref[...] = sig

        routed = ex_ref[...] > 0.0
        both = dot(mixed, gw_ref[...])
        gate = both[:, :hidden]
        lift = both[:, hidden:]
        d_hidden = dot_last(grad_ref[...], lw_ref[...])
        gate_sig = jax.nn.sigmoid(gate)
        gated = gate * gate_sig
        act = gated * lift
        wide = jnp.where(routed, weight, 1.0)
        hid = (act * wide).astype(LOW)
        hid_ref[...] = hid
        dw_ref[...] = jnp.sum(jnp.where(routed, act * d_hidden, 0.0), 1, keepdims=True)
        d_hidden = d_hidden * wide
        d_gate = (d_hidden * lift * gate_sig * (1.0 + gate * (1.0 - gate_sig))).astype(LOW)
        d_lift = (d_hidden * gated).astype(LOW)
        d_both = jnp.concatenate([d_gate, d_lift], 1)
        dg_ref[...] = d_both
        d_mixed = dot_last(d_both, gw_ref[...]).astype(LOW)
        out = dot(hid, lw_ref[...]).astype(LOW)

        @pl.when(step < middle)
        def _():
            dm_first[...] = d_mixed
            out_first[...] = out

        @pl.when(step >= middle)
        def _():
            dm_second[...] = d_mixed
            out_second[...] = out

    def tok(cols):
        return pl.BlockSpec((rows, cols), lambda b, info_ref: (b, 0))

    low_half = pl.BlockSpec((rows, model), lambda b, info_ref: (jnp.minimum(b, middle - 1), 0))
    high_half = pl.BlockSpec((rows, model), lambda b, info_ref: (jnp.maximum(b - middle, 0), 0))
    part = jax.ShapeDtypeStruct((total // 2, model), LOW)
    return pl.pallas_call(
        kernel,
        grid_spec=pltpu.PrefetchScalarGridSpec(
            num_scalar_prefetch=1,
            grid=(count,),
            in_specs=[whole(a) for a in blocks]
            + [tok(model), tok(lanes), tok(1)]
            + [whole(a) for a in (small_w, gate_w, lower_w, is_expert)],
            out_specs=[tok(model), tok(hidden), tok(2 * hidden)]
            + [low_half, high_half, low_half, high_half, tok(1)]
            + [pl.BlockSpec((rows, lanes), lambda b, info_ref: (0, 0))],
            scratch_shapes=[pltpu.VMEM((rows, model), LOW)],
        ),
        out_shape=[jax.ShapeDtypeStruct((total, model), LOW)]
        + [jax.ShapeDtypeStruct((total, w), LOW) for w in (hidden, 2 * hidden)]
        + [part] * 4
        + [jax.ShapeDtypeStruct((total, 1), F32), jax.ShapeDtypeStruct((rows, lanes), F32)],
        cost_estimate=cost(total * model * 12),
    )(info, *blocks, grad, counts, valid, small_w, gate_w, lower_w, is_expert)


def cost(size):
    return pl.CostEstimate(flops=0, bytes_accessed=size // 8, transcendentals=0)


def arrivals(steps, here, count):
    found = []
    for index, step in enumerate(steps):
        if step == "last":
            found.append((index, here == 0, count - 1))
            found.append((index, here == count - 1, 0))
        elif step == "above":
            found.append((index, here < count - 1, here + 1))
        elif step == "below":
            found.append((index, here > 0, here - 1))
        else:
            found.append((index, None, lax.rem(here + step, count)))
    return found


def each_arrival(steps, here, count, act):
    for index, condition, place in arrivals(steps, here, count):
        if condition is None:
            act(index, place)
        else:
            pl.when(condition)(functools.partial(act, index, place))


def scalars(*values):
    return jnp.stack([v.astype(jnp.int32) for v in values])


def shard_place(count, own, came, shard, start, size):
    steps = [k for k, _ in came]
    width = own.shape[1]
    tile = size
    while tile > 128 and tile % 2 == 0 and start % (tile // 2) == 0:
        tile //= 2

    def kernel(at_ref, own_ref, *refs):
        out = refs[-1]
        here = at_ref[0]
        out[here] = own_ref[...]

        def act(index, place):
            out[place] = refs[index][...]

        each_arrival(steps, here, count, act)

    return pl.pallas_call(
        kernel,
        grid_spec=pltpu.PrefetchScalarGridSpec(
            num_scalar_prefetch=1,
            grid=(size // tile,),
            in_specs=[pl.BlockSpec((tile, width), lambda b, at_ref: (b + start // tile, 0))]
            * (len(came) + 1),
            out_specs=pl.BlockSpec((count, tile, width), lambda b, at_ref: (0, b, 0)),
        ),
        out_shape=jax.ShapeDtypeStruct((count, size, width), LOW),
        cost_estimate=cost(4 * count * size * width),
    )(scalars(shard), own, *[piece for _, piece in came])


def strip_place(local, pieces, steps, shard, devices, start, tile):
    count = max(steps) + 1
    reps = len(pieces)
    rows, width = local.shape
    strip = pieces[0].shape[0] // len(steps)

    def kernel(at_ref, own_ref, *refs):
        out = refs[-1]
        here = at_ref[0]
        out[here] = own_ref[...]
        for j in range(reps):
            base = pl.multiple_of(at_ref[1 + j] * strip, strip)

            def act(index, place):
                out[place, pl.ds(base, strip)] = refs[j][index * strip : (index + 1) * strip]

            each_arrival(steps, here, count, act)

    return pl.pallas_call(
        kernel,
        grid_spec=pltpu.PrefetchScalarGridSpec(
            num_scalar_prefetch=1,
            grid=(width // tile,),
            in_specs=[pl.BlockSpec((rows, tile), lambda b, at_ref: (0, b))]
            + [
                pl.BlockSpec((pieces[0].shape[0], tile), lambda b, at_ref: (0, b + start // tile))
                for _ in pieces
            ],
            out_specs=pl.BlockSpec((count, rows, tile), lambda b, at_ref: (0, 0, b)),
        ),
        out_shape=jax.ShapeDtypeStruct((count, rows, width), LOW),
        cost_estimate=cost(4 * count * rows * width),
    )(jnp.concatenate([scalars(shard), devices]), local, *pieces).reshape(count * rows, width)


def merge_rows(blocks, act, extra, widths):
    rows = blocks[0].shape[0]
    count = len(blocks)
    outs = len(widths)

    def kernel(*refs):
        index = pl.program_id(0)
        more = [r[...] for r in refs[count:-outs]]
        for k in range(count):

            @pl.when(index == k)
            def _():
                for ref, value in zip(refs[-outs:], act(refs[k][...], *more)):
                    ref[...] = value

    return pl.pallas_call(
        kernel,
        grid=(count,),
        in_specs=[
            pl.BlockSpec(a.shape, lambda b: (0, 0), pipeline_mode=pl.Buffered(1)) for a in blocks
        ]
        + [pl.BlockSpec((rows, a.shape[1]), lambda b: (b, 0)) for a in extra],
        out_specs=[pl.BlockSpec((rows, w), lambda b: (b, 0)) for w in widths],
        out_shape=[jax.ShapeDtypeStruct((count * rows, w), LOW) for w in widths],
        cost_estimate=cost(count * rows * sum(widths) * 4),
    )(*blocks, *extra)


def assemble(blocks, devices, grid, block_shape, block_map, outs, place, weights=()):
    reps = len(blocks)
    count = len(weights)

    def kernel(dev_ref, *refs):
        held = refs[-1]
        out_refs = refs[reps + count : -1]
        for k in range(reps):
            held[dev_ref[k]] = refs[k][...].astype(F32)
        for j in range(reps):
            place(pl.program_id(0), j, held[j], out_refs)
        total = None
        for i in range(count):
            value = refs[reps + i][...].astype(F32) * out_refs[i][...]
            value = jnp.sum(value, -1, keepdims=True)
            if value.ndim == 3:
                value = jnp.sum(value, 0)
            total = value if total is None else total + value
        if count:
            out_refs[-1][...] = total

    specs = [
        pl.BlockSpec(shape, functools.partial(lambda m, b, dev_ref: m(b), where))
        for _, shape, where in outs
    ]
    sums = []
    if count:
        rows = outs[0][1][0]
        sums = [((grid * rows, 1), (rows, 1), lambda b: (b, 0))]
    return pl.pallas_call(
        kernel,
        grid_spec=pltpu.PrefetchScalarGridSpec(
            num_scalar_prefetch=1,
            grid=(grid,),
            in_specs=[pl.BlockSpec(block_shape, lambda b, dev_ref: block_map(b)) for _ in blocks]
            + specs[:count],
            out_specs=specs
            + [pl.BlockSpec(shape, lambda b, dev_ref: (b, 0)) for _, shape, _ in sums],
            scratch_shapes=[pltpu.VMEM((reps,) + block_shape, F32)],
        ),
        out_shape=[jax.ShapeDtypeStruct(shape, F32) for shape, _, _ in outs + sums],
        cost_estimate=cost(reps * blocks[0].size * 6),
    )(devices, *blocks, *weights)


def layouts(lengths, seq_owner, devices, rows):
    count = lengths.shape[0]
    mine = seq_owner[None, :] == devices[:, None]
    own_length = jnp.where(mine, lengths[None, :], 0)
    numbers = jnp.arange(count, dtype=jnp.int32)
    ahead = numbers[:, None] < numbers[None, :]
    starts = jnp.sum(jnp.where(ahead[None], own_length[:, :, None], 0), 1)[:, None, :]
    ends = starts + own_length[:, None, :]
    row = jnp.arange(rows, dtype=jnp.int32)[None, :, None]
    inside = mine[:, None, :] & (row >= starts) & (row < ends)
    valid = jnp.any(inside, 2, keepdims=True)
    segment = jnp.sum(jnp.where(inside, numbers, 0), 2, keepdims=True)
    position = row - jnp.sum(jnp.where(inside, starts, 0), 2, keepdims=True)
    return jnp.where(valid, segment, count), position, valid


def make_local(reps, shards):
    group = Group(reps, shards)
    heads = HEADS // reps
    half = 32 * heads
    width = 2 * half

    def local(
        tokens,
        cotangent,
        lengths,
        seq_owner,
        expert_ids,
        attention_gain,
        query_weight,
        latent_down,
        latent_gain,
        latent_up,
        output_weight,
        feedforward_gain,
        router_weight,
        shared_gate,
        shared_up,
        shared_down,
        expert_gate,
        expert_up,
        expert_down,
    ):
        rows, model = tokens.shape
        rep = lax.axis_index("rep")
        shard = lax.axis_index("shard")
        devices = group.devices(rep)
        slab = model // shards
        strip = slab // reps
        lat = latent_gain.shape[0]
        cut = group.half * rows

        x_gather = Gathering(group, tokens)
        x_gather.start()
        small = jnp.concatenate(
            [
                lax.dynamic_slice_in_dim(latent_down, rep * strip, strip, 0),
                lax.dynamic_slice_in_dim(router_weight, rep * strip, strip, 0),
            ],
            1,
        )
        small = lax.all_gather(small, ("shard", "rep"), axis=0, tiled=True)
        output_shift = Shifting(
            group, lax.dynamic_slice_in_dim(output_weight, rep * strip, strip, 0)
        )
        output_shift.start()

        query_cols = heads * (NOPE + ROPE)
        up_cols = heads * (NOPE + VDIM)
        query_wide = round_up(query_cols, 128)
        query_part = lax.dynamic_slice_in_dim(query_weight, rep * query_cols, query_cols, 1)
        if query_wide > query_cols:
            query_part = jnp.pad(query_part, ((0, 0), (0, query_wide - query_cols)))
        up_part = lax.dynamic_slice_in_dim(latent_up, rep * up_cols, up_cols, 1)
        up_part = fold(up_part, slab)
        gain_rows = jnp.concatenate([attention_gain, feedforward_gain, latent_gain])
        gain_lanes = query_wide + 128
        gain_count = round_up(gain_rows.shape[0], 16 * gain_lanes)
        gain_rows = jnp.pad(gain_rows, (0, gain_count - gain_rows.shape[0])).reshape(-1, gain_lanes)
        query_part = jnp.concatenate(
            [jnp.concatenate([query_part, up_part], 1), gain_rows], 0
        )
        query_shift = Shifting(group, query_part)
        query_shift.start()

        part_s = shared_down.shape[0] // reps
        local_e = expert_down.shape[1]
        part_e = WINDOW * local_e // reps
        per = reps // WINDOW
        my_expert = rep // per
        used = part_s + part_e
        hidden = round_up(shards * used, 128)
        unit = hidden // shards
        place = jnp.arange(hidden, dtype=jnp.int32)
        within = place % unit
        is_shared = within < part_s
        is_expert = (within >= part_s) & (within < used)
        from_shared = jnp.where(
            is_shared, (place // unit) * shared_down.shape[0] + rep * part_s + within, -1
        )
        from_expert = jnp.where(
            is_expert, (place // unit) * local_e + (rep % per) * part_e + within - part_s, -1
        )
        pick_s = (
            jnp.arange(shared_gate.shape[1], dtype=jnp.int32)[:, None] == from_shared[None, :]
        ).astype(LOW)
        pick_e = (
            jnp.arange(expert_gate.shape[2], dtype=jnp.int32)[:, None] == from_expert[None, :]
        ).astype(LOW)

        def my_columns(shared, expert):
            expert = lax.dynamic_index_in_dim(expert, my_expert, 0, keepdims=False)
            return (dot(shared, pick_s) + dot(expert, pick_e)).astype(LOW)

        gate_all = jnp.concatenate(
            [my_columns(shared_gate, expert_gate), my_columns(shared_up, expert_up)], 1
        )
        lower_part = jnp.concatenate(
            [
                lax.dynamic_slice_in_dim(shared_down, rep * part_s, part_s, 0),
                lax.dynamic_slice(
                    expert_down, (my_expert, (rep % per) * part_e, 0), (1, part_e, model)
                )[0],
                jnp.zeros((unit - used, model), LOW),
            ],
            0,
        )

        segment, position, valid = layouts(lengths, seq_owner, devices * shards + shard, rows)
        total_rows = reps * rows
        seg_col = segment.reshape(total_rows, 1)
        seg_row = segment.reshape(reps, 1, rows)
        valid_all = valid.reshape(total_rows, 1).astype(F32)
        valid_own = valid_all[:rows]
        frequency = jnp.power(ROPE_BASE, -2.0 * jnp.arange(32, dtype=F32) / ROPE)
        angles = position.reshape(total_rows, 1).astype(F32) * jnp.tile(frequency, 2 * heads)[None]
        cosine = jnp.cos(angles)
        side = jnp.where(jnp.arange(width) < half, -1.0, 1.0).astype(F32)
        sine = jnp.sin(angles) * side[None, :]

        hidden_in = tokens.astype(F32)
        counts = jnp.sum(
            (expert_ids[:, :, None] == jnp.arange(NEXP, dtype=jnp.int32)).astype(F32), 1
        )
        given = jnp.concatenate(
            [cotangent, jnp.zeros((rows, 128 - NEXP), LOW), counts.astype(LOW)], 1
        )

        phase(x_gather, query_shift, output_shift)
        x_gather.start()
        query_shift.start()
        output_shift.start()
        (gate_all,) = phase(x_gather, query_shift, output_shift, gate_all)
        gate_all = lax.all_gather(gate_all, "shard", axis=0, tiled=True)
        x_gather.start()
        output_came = output_shift.whole(shard)
        shard_steps = [k for k, _ in output_came]
        output_gather = Gathering(group, jnp.concatenate([piece for _, piece in output_came], 0))
        output_gather.start()
        query_up = shard_place(shards, query_part, query_shift.result(), shard, 0, slab)
        gains = shard_place(
            shards, query_part, query_shift.result(), shard, slab, gain_rows.shape[0]
        )
        gains = gains.reshape(shards, -1).astype(F32)
        attention_gain_all = gains[:, :slab].reshape(1, model)
        mixer_gain_all = gains[:, slab : 2 * slab].reshape(1, model)
        latent_gain_all = gains[:, 2 * slab : 2 * slab + lat].reshape(1, RANK)

        lane = jnp.arange(heads * width, dtype=jnp.int32)
        head = lane // width
        spot = lane % width
        source = jnp.where(
            (spot % half) // 32 == head, (spot // half) * 32 + spot % 32, -1
        )
        spread = (jnp.arange(ROPE, dtype=jnp.int32)[:, None] == source[None, :]).astype(LOW)
        cols = heads * VDIM
        normed_all, qn, qr, keyval, kr, latent_low, up_all, latent_own, attended = attend_forward(
            devices,
            x_gather.list(),
            attention_gain_all,
            latent_gain_all,
            query_up,
            heads,
            small,
            spread,
            cosine,
            sine,
            seg_col,
            seg_row,
        )
        attended, given, lower_part = phase(attended, output_gather, given, lower_part)
        output_gather.start()
        lower_all = lax.all_gather(lower_part, "shard", axis=0, tiled=True)
        attended_own = lax.all_to_all(
            attended.reshape(reps, rows, cols), "rep", 0, 0, tiled=True
        )
        (attended_own,) = phase(attended_own, output_gather)
        output_gather.start()
        given_gather = Gathering(group, given)
        given_gather.start()
        output_all = strip_place(
            output_weight, output_gather.list(), shard_steps, shard, devices, 0, 256
        )
        attended_own = jnp.transpose(attended_own, (1, 0, 2)).reshape(rows, HEADS * VDIM)
        mid = hidden_in + dot(attended_own, output_all)
        mixed_scale = rms_scale(mid)
        mixed = (mid * mixed_scale * mixer_gain_all).astype(LOW)

        mixed_gather = Gathering(group, mixed)
        mixed_gather.start()
        (gate_all,) = phase(mixed_gather, given_gather, gate_all)
        mixed_gather.start()
        given_gather.start()
        phase(mixed_gather, given_gather)
        mixed_gather.start()
        given_gather.start()
        grad_all, counts_all = merge_rows(
            given_gather.list(),
            lambda block, ok: (
                (block[:, :model].astype(F32) * ok).astype(LOW),
                block[:, model:],
            ),
            [valid_all],
            [model, 128],
        )
        grad_all, counts_all = phase(mixed_gather, grad_all, counts_all)
        (
            mixed_all,
            hidden_low,
            d_both,
            d_mixed_first,
            d_mixed_second,
            ffn_first,
            ffn_second,
            d_weight,
            sig_own,
        ) = experts(
            jnp.reshape(my_expert, (1,)).astype(jnp.int32),
            mixed_gather.list(),
            grad_all,
            counts_all,
            valid_all,
            small,
            gate_all,
            lower_all,
            is_expert.astype(F32)[None, :],
        )
        sig_own = sig_own[:, -NEXP:]
        mixed_sum = Reducing(group, d_mixed_second, d_mixed_first)
        mixed_sum.start()
        both_grad = dot_rows(mixed_all, d_both).astype(LOW)
        ffn_second, d_weight, hidden_low, _ = phase(
            mixed_sum, ffn_second, d_weight, hidden_low, both_grad
        )
        mixed_sum.start()
        numbers = jnp.arange(reps, dtype=jnp.int32)
        by_device = jnp.sum(
            jnp.where(
                (devices[None, :] == numbers[:, None])[:, :, None],
                d_weight.reshape(1, reps, rows),
                0.0,
            ),
            1,
        )
        d_weight_own = lax.all_to_all(by_device, "rep", 0, 0, tiled=True)
        d_weight_own = jnp.sum(d_weight_own.reshape(WINDOW, per, rows), 1)
        ffn_sum = Reducing(group, ffn_second, ffn_first)
        ffn_sum.start()
        hidden_low, d_weight_own = phase(mixed_sum, ffn_sum, hidden_low, d_weight_own)
        both_grad = lax.psum_scatter(both_grad, "shard", scatter_dimension=0, tiled=True)
        mixed_sum.start()
        lower_grad = dot_rows(hidden_low, grad_all).astype(LOW)
        phase(mixed_sum, lower_grad)
        lower_grad = lax.psum_scatter(lower_grad, "shard", scatter_dimension=0, tiled=True)[:used]
        d_mixed = mixed_sum.total()

        total_own = jnp.sum(sig_own * counts, 1, keepdims=True)
        hit = counts[:, :WINDOW]
        d_route = jnp.concatenate(
            [valid_own * d_weight_own.T * hit, jnp.zeros((rows, NEXP - WINDOW), F32)], 1
        )
        inner = jnp.sum(d_route * sig_own, 1, keepdims=True)
        d_sig = ROUTE_SCALE * (d_route / total_own - counts * inner / (total_own * total_own))
        d_logits = (d_sig * sig_own * (1.0 - sig_own)).astype(LOW)
        d_mixed = d_mixed + dot_last(d_logits, small[:, RANK + ROPE :])
        grad_own = cotangent.astype(F32) * valid_own
        d_mid = grad_own + rms_back(mid, mixed_scale, mixer_gain_all, d_mixed)
        d_branch = d_mid.astype(LOW)

        out_cols = model // reps

        def output_part(index):
            picked = [
                lax.dynamic_slice_in_dim(d_branch, devices[k] * out_cols, out_cols, 1)
                for k in index
            ]
            return dot_rows(attended_own, jnp.concatenate(picked, 1)).astype(LOW)

        output_sum = Reducing(
            group,
            output_part(range(group.half, reps)),
            output_part(range(group.half)),
            axis=1,
        )
        output_sum.start()

        d_attended = dot_last(d_branch, output_all).astype(LOW)
        d_attended = jnp.transpose(d_attended.reshape(rows, reps, cols), (1, 0, 2))
        d_attended = lax.all_to_all(d_attended, "rep", 0, 0, tiled=True)
        (d_attended,) = phase(d_attended, output_sum)
        output_sum.start()
        ffn_sum.start()
        d_attended = d_attended.reshape(total_rows, cols)
        (
            d_normed_first,
            d_normed_second,
            latent_first,
            latent_second,
            attention_grad,
        ) = attend_backward(
            devices,
            (qn, qr, keyval, kr),
            d_attended,
            normed_all,
            latent_low,
            query_up,
            up_all,
            cosine,
            sine,
            seg_col,
            seg_row,
            rows,
        )
        latent_second, d_normed_second = phase(
            latent_second, d_normed_second, output_sum, ffn_sum
        )
        attention_grad = lax.psum_scatter(
            attention_grad, "shard", scatter_dimension=0, tiled=True
        ).reshape(slab, query_wide + 128)
        latent_sum = Reducing(group, latent_second, latent_first)
        latent_sum.start()
        output_sum.start()
        both_gather = Gathering(group, both_grad, early=True)
        both_gather.start()
        (d_normed_second,) = phase(latent_sum, d_normed_second)
        latent_sum.start()
        normed_sum = Reducing(group, d_normed_second, d_normed_first)
        normed_sum.start()
        phase(latent_sum, output_sum)
        latent_sum.start()
        output_grad = lax.psum_scatter(
            output_sum.total().astype(LOW), "shard", scatter_dimension=0, tiled=True
        )
        phase(latent_sum)
        d_latent_sum = latent_sum.total()
        compressed = latent_own[:, :RANK]
        d_compressed = rms_back(
            compressed, rms_scale(compressed), latent_gain_all, d_latent_sum[:, :RANK]
        )
        kg_first = d_latent_sum[:, RANK : RANK + 32]
        kg_second = d_latent_sum[:, RANK + 32 : RANK + ROPE]
        cos_own = cosine[:rows, :32]
        sin_own = sine[:rows, half : half + 32]
        d_latent = jnp.concatenate(
            [
                d_compressed,
                kg_first * cos_own + kg_second * sin_own,
                kg_second * cos_own - kg_first * sin_own,
            ],
            1,
        ).astype(LOW)
        row_gather = Gathering(group, jnp.concatenate([d_latent, d_logits], 1))
        row_gather.start()
        (lower_grad,) = phase(row_gather, both_gather, lower_grad)
        row_gather.start()
        both_gather.start()
        phase(row_gather, normed_sum)
        row_gather.start()
        normed_sum.start()
        (attention_grad,) = phase(row_gather, both_gather, attention_grad)
        both_gather.start()
        lower_gather = Gathering(group, lower_grad)
        lower_gather.start()
        rows_given = row_gather.list()
        d_down = dot_last(d_latent, small[:, : RANK + ROPE])
        (row_grads,) = merge_rows(
            rows_given,
            lambda block: (block,),
            [],
            [RANK + ROPE + NEXP],
        )

        def my_strip(values):
            return jnp.concatenate(
                [
                    lax.dynamic_slice_in_dim(values, s * slab + rep * strip, strip, 1)
                    for s in range(shards)
                ],
                1,
            )

        strip_grad = jnp.concatenate(
            [
                dot_rows(my_strip(normed_all), row_grads[:, : RANK + ROPE]),
                dot_rows(my_strip(mixed_all), row_grads[:, RANK + ROPE :]),
            ],
            1,
        ).astype(LOW)

        strip_sum = lax.psum_scatter(strip_grad, "shard", scatter_dimension=0, tiled=True)
        tile = min(slab, 64)

        def place_columns(step, j, block, refs):
            for side in (0, 1):
                for s in range(shards):
                    base = side * hidden + s * unit
                    at = s * part_s * reps + j * part_s
                    refs[2 * side][:, at : at + part_s] = block[:, base : base + part_s]
                    at = s * part_e * per + (j % per) * part_e
                    refs[2 * side + 1][j // per, :, at : at + part_e] = block[
                        :, base + part_s : base + used
                    ]

        wide_s = shared_gate.shape
        wide_e = expert_gate.shape
        sgate_grad, egate_grad, sup_grad, eup_grad, mixer_sum = assemble(
            both_gather.list(),
            devices,
            slab // tile,
            (tile, 2 * hidden),
            lambda b: (b, 0),
            [
                (wide_s, (tile, wide_s[1]), lambda b: (b, 0)),
                (wide_e, (WINDOW, tile, wide_e[2]), lambda b: (0, b, 0)),
            ]
            * 2,
            place_columns,
            (shared_gate, expert_gate, shared_up, expert_up),
        )

        _, _, output_grad = phase(lower_gather, strip_grad, sgate_grad, output_grad)
        lower_gather.start()
        query_gather = Gathering(group, attention_grad)
        query_gather.start()
        phase(lower_gather, query_gather, normed_sum)
        lower_gather.start()
        query_gather.start()
        normed_sum.start()
        ffn_sum.start()
        output_gather = Gathering(group, output_grad)
        output_gather.start()
        def place_rows(step, j, block, refs):
            refs[0][j * part_s : (j + 1) * part_s] = block[:part_s]
            at = (j % per) * part_e
            refs[1][j // per, at : at + part_e] = block[part_s:]

        lane_tile = 256
        sdown_grad, edown_grad = assemble(
            lower_gather.list(),
            devices,
            model // lane_tile,
            (used, lane_tile),
            lambda b: (0, b),
            [
                (shared_down.shape, (shared_down.shape[0], lane_tile), lambda b: (0, b)),
                (expert_down.shape, (WINDOW, local_e, lane_tile), lambda b: (0, 0, b)),
            ],
            place_rows,
        )

        strip_sum, _ = phase(query_gather, output_gather, strip_sum, sdown_grad)
        query_gather.start()
        output_gather.start()
        strip_gather = Gathering(group, strip_sum)
        strip_gather.start()
        phase(query_gather, output_gather, strip_gather, normed_sum, ffn_sum)
        output_gather.start()
        strip_gather.start()
        layer_out = (valid_own * (mid + ffn_sum.total())).astype(LOW)
        d_normed = normed_sum.total() + d_down
        token_grad = d_mid + rms_back(
            hidden_in, rms_scale(hidden_in), attention_gain_all, d_normed
        )

        def place_attention(step, j, block, refs):
            refs[0][:, j * query_cols : (j + 1) * query_cols] = block[:, :query_cols]

            @pl.when(step < up_cols // 128)
            def _():
                at = pl.multiple_of(j * up_cols + step * 128, 128)
                refs[1][:, pl.ds(at, 128)] = block[:, query_wide:]

        query_grad, up_grad, query_sum = assemble(
            query_gather.list(),
            devices,
            slab // lat,
            (lat, query_wide + 128),
            lambda b: (b, 0),
            [
                (query_weight.shape, (lat, query_weight.shape[1]), lambda b: (b, 0)),
                (latent_up.shape, latent_up.shape, lambda b: (0, 0)),
            ],
            place_attention,
            (query_weight,),
        )

        def place_output(step, j, block, refs):
            refs[0][:, j * out_cols : (j + 1) * out_cols] = block

        phase(output_gather, strip_gather, query_grad)
        strip_gather.start()
        (output_grad,) = assemble(
            output_gather.list(),
            devices,
            slab // lat,
            (lat, out_cols),
            lambda b: (b, 0),
            [(output_weight.shape, (lat, model), lambda b: (b, 0))],
            place_output,
        )

        def place_strip(step, j, block, refs):
            refs[0][:, j * strip : (j + 1) * strip] = block[:, : RANK + ROPE].T
            refs[1][:, j * strip : (j + 1) * strip] = block[:, RANK + ROPE :].T

        down_grad, router_grad = assemble(
            strip_gather.list(),
            devices,
            1,
            (strip, RANK + ROPE + NEXP),
            lambda b: (0, 0),
            [
                ((RANK + ROPE, slab), (RANK + ROPE, slab), lambda b: (0, 0)),
                ((NEXP, slab), (NEXP, slab), lambda b: (0, 0)),
            ],
            place_strip,
        )

        down_grad = down_grad.T
        router_grad = router_grad.T

        def row_sum(weight, grad):
            return jnp.sum(weight.astype(F32) * grad, -1)

        attention_gain_grad = (
            query_sum[:, 0] + row_sum(latent_down, down_grad)
        ) / attention_gain.astype(F32)
        latent_gain_grad = row_sum(latent_up, up_grad) / latent_gain.astype(F32)
        mixer_gain_grad = (
            row_sum(router_weight, router_grad) + mixer_sum[:, 0]
        ) / feedforward_gain.astype(F32)

        return (
            layer_out,
            token_grad,
            attention_gain_grad,
            query_grad,
            down_grad,
            latent_gain_grad,
            up_grad,
            output_grad,
            mixer_gain_grad,
            router_grad,
            sgate_grad,
            sup_grad,
            sdown_grad,
            egate_grad,
            eup_grad,
            edown_grad,
        )

    return local


def fold(value, rows):
    count = value.shape[1] // 128
    parts = [value[:, i * 128 : (i + 1) * 128] for i in range(count)]
    left = rows - count * value.shape[0]
    if left:
        parts.append(jnp.zeros((left, 128), value.dtype))
    return jnp.concatenate(parts, 0)


def solution(mesh):
    tokens = P(("rep", "shard"), None)
    vector = P("shard")
    matrix = P("shard", None)
    stack = P(None, "shard", None)
    in_specs = (
        (tokens, tokens, P(), P(), tokens, vector, matrix, matrix, vector, matrix, matrix, vector)
        + (matrix,) * 4
        + (stack,) * 3
    )
    out_specs = (
        (tokens, tokens, vector, matrix, matrix, vector, matrix, matrix, vector)
        + (matrix,) * 4
        + (stack,) * 3
    )
    local = make_local(mesh.shape["rep"], mesh.shape["shard"])
    return jax.shard_map(local, mesh=mesh, in_specs=in_specs, out_specs=out_specs, check_vma=False)
```
